32 devices in a mesh: seq: 8 (over z, y), samp: 4 (over x, core).
Axes of the slice: x: 2, y: 2, z: 4, core: 2. Of those that a mesh axis runs over, the one named last changes fastest.
Arguments:
- atoms: bfloat16 [48, 4096, 128], P('samp', 'seq'), may hold values from -3 to 3
- gain: float32 [128], replicated, may hold values from 0.25 to 1.75
- w_query: bfloat16 [128, 128], replicated, may hold values from -0.5 to 0.5
- w_key: bfloat16 [128, 128], replicated, may hold values from -0.5 to 0.5
- w_value: bfloat16 [128, 128], replicated, may hold values from -0.5 to 0.5
- w_gate: bfloat16 [128, 128], replicated, may hold values from -0.5 to 0.5
- w_out: bfloat16 [128, 128], replicated, may hold values from -0.5 to 0.5
- w_token: bfloat16 [128, 768], replicated, may hold values from -0.5 to 0.5
- w_pair: bfloat16 [16, 4], replicated, may hold values from -1.5 to 1.5
- pair_cond: bfloat16 [128, 32, 2048], P('seq'), may hold values from -6 to 6
- counts: int32 [8], replicated, may hold values from 472 to 512, as said below
- membership: int32 [4096], P('seq'), may hold values from 0 to 383, as said below
- pooled_cot: bfloat16 [48, 384, 768], P('samp', 'seq'), may hold values from -6 to 6
Outputs:
- pooled: bfloat16 [48, 384, 768], P('samp', 'seq')
- grad_atoms: bfloat16 [48, 4096, 128], P('samp', 'seq')
- grad_gain: float32 [128], replicated
- grad_query: float32 [128, 128], replicated
- grad_key: float32 [128, 128], replicated
- grad_value: float32 [128, 128], replicated
- grad_gate: float32 [128, 128], replicated
- grad_out: float32 [128, 128], replicated
- grad_token: float32 [128, 768], replicated
- grad_pair: float32 [16, 4], replicated
The draws below stay inside these ranges and needn't reach their ends.
Inputs may be any that keep to these rules, and one draw needn't show every extreme that they name: `counts`: live atoms fill the first slots of each shard; some shard is full. `membership`: slots of shard s name tokens s * 48 to (s + 1) * 48 - 1, never falling along the slots; every token has one or more live atoms; slots past the shard's count name its last token.
All inputs are finite; a program needn't handle non-finite values.
Results may differ from the reference program's by a relative error of at most 0.012.
Values may be sent and summed in bfloat16 or wider, within the bound.
A program may use at most 128 MiB of HBM per device.

```python
import jax
import jax.numpy as jnp
from jax import lax

D = 128
HEADS = 4
CP = 16
TOKW = 768
QBLK = 32
KWIN = 128
ATOM_DEV = 512
TOK_DEV = 48
ATOMS = 4096
TOKENS = 384
SAMPLES = 48
N_SEQ = 8


def shard_counts(key):
    base_key = jax.random.fold_in(key, 11)
    drawn_counts = jax.random.randint(jax.random.fold_in(base_key, 1), (N_SEQ,), ATOM_DEV - 40, ATOM_DEV + 1)
    fullest = jax.random.randint(jax.random.fold_in(base_key, 2), (), 0, N_SEQ)
    return jnp.where(jnp.arange(N_SEQ) == fullest, ATOM_DEV, drawn_counts).astype(jnp.int32)


def draw_counts(key, part):
    return shard_counts(key)


def draw_membership(key, part):
    counts = shard_counts(key)
    base_key = jax.random.fold_in(key, 23)
    slot_ids = jnp.arange(ATOM_DEV, dtype=jnp.int32)

    def one_shard(shard_index):
        extra_ids = jax.random.randint(jax.random.fold_in(base_key, shard_index), (ATOM_DEV,), 0, TOK_DEV).astype(jnp.int32)
        values = jnp.where(slot_ids < TOK_DEV, slot_ids, extra_ids)
        values = jnp.where(slot_ids < counts[shard_index], values, TOK_DEV)
        ordered = jnp.minimum(jnp.sort(values), TOK_DEV - 1)
        return ordered + shard_index * TOK_DEV
    return jax.vmap(one_shard)(jnp.arange(N_SEQ, dtype=jnp.int32)).reshape(-1).astype(jnp.int32)


def levels(key, dims, split, smallest, top_value):
    loudness = 1.0
    for axis_at, parts in split:
        steps = jax.random.uniform(jax.random.fold_in(jax.random.fold_in(key, 6), axis_at), (parts,), jnp.float32, smallest / len(split), top_value / len(split))
        loudness = loudness * jnp.repeat(jnp.exp(steps), dims[axis_at] // parts).reshape((-1,) + (1,) * (len(dims) - 1 - axis_at))
    return loudness


def bell_draw(stream_key, shape, scale, limit, cuts=(), held_as=jnp.bfloat16):
    values = jax.random.normal(stream_key, shape, jnp.float32) * scale
    if len(cuts) > 0:
        values = levels(stream_key, shape, cuts, -0.22, 0.18) * values
    return jnp.clip(values, min=-limit, max=limit).astype(held_as)


def setup_inputs(seed: int = 0) -> dict:
    key_list = jax.random.split(jax.random.key(seed), 14)
    atoms = bell_draw(key_list[0], (SAMPLES, ATOMS, D), 0.5, 3.0, ((0, 4), (1, 8)))
    gain = jnp.clip(1.0 + 0.15 * jax.random.normal(key_list[1], (D,), jnp.float32), 0.25, 1.75)
    w_query = bell_draw(key_list[2], (D, D), D ** -0.5, 0.5)
    w_key = bell_draw(key_list[3], (D, D), D ** -0.5, 0.5)
    w_value = bell_draw(key_list[4], (D, D), D ** -0.5, 0.5)
    w_gate = bell_draw(key_list[5], (D, D), D ** -0.5, 0.5)
    w_out = bell_draw(key_list[6], (D, D), D ** -0.5, 0.5)
    w_token = bell_draw(key_list[7], (D, TOKW), D ** -0.5, 0.5)
    w_pair = bell_draw(key_list[8], (CP, HEADS), CP ** -0.5, 1.5)
    pair_cond = bell_draw(key_list[9], (ATOMS // QBLK, QBLK, KWIN * CP), 1.0, 6.0, ((0, 8),))
    counts = draw_counts(jax.random.fold_in(key_list[13], 71), 0)
    membership = draw_membership(jax.random.fold_in(key_list[13], 71), 0)
    pooled_cot = bell_draw(key_list[12], (SAMPLES, TOKENS, TOKW), 1.0, 6.0, ((0, 4), (1, 8)))
    return {"atoms": atoms, "gain": gain, "w_query": w_query, "w_key": w_key, "w_value": w_value, "w_gate": w_gate, "w_out": w_out, "w_token": w_token, "w_pair": w_pair, "pair_cond": pair_cond, "counts": counts, "membership": membership, "pooled_cot": pooled_cot}


epsilon = 1e-05
highest = lax.Precision.HIGHEST

def windows(extended, blocks):
    span_blocks = KWIN // QBLK
    blocked = extended.reshape((blocks + span_blocks - 1, QBLK) + extended.shape[1:])
    return jnp.concatenate([blocked[offset:offset + blocks] for offset in range(span_blocks)], axis=1)

def unwindow(grad_windows, blocks):
    span_blocks = KWIN // QBLK
    summed = None
    for offset in range(span_blocks):
        grad_piece = grad_windows[:, offset * QBLK:(offset + 1) * QBLK]
        pad_widths = [(offset, span_blocks - 1 - offset)] + [(0, 0)] * (grad_piece.ndim - 1)
        padded = jnp.pad(grad_piece, pad_widths)
        summed = padded if summed is None else summed + padded
    return summed.reshape((QBLK * (blocks + span_blocks - 1),) + grad_windows.shape[2:])

def rounded(value):
    return lax.optimization_barrier(value.astype(jnp.bfloat16)).astype(jnp.float32)

def sample_pass(atoms, queries, keys_ext, values_ext, gate_pre, key_mask, pair_bias, w_out, w_token, member, inv_count, cotangent):
    atom_rows, model_width = atoms.shape
    blocks = atom_rows // QBLK
    head_dim = model_width // HEADS
    scaling = head_dim ** (-0.5)
    query_heads = queries.reshape(blocks, QBLK, HEADS, head_dim).astype(jnp.float32)
    key_heads = windows(keys_ext, blocks).reshape(blocks, KWIN, HEADS, head_dim).astype(jnp.float32)
    value_heads = windows(values_ext, blocks).reshape(blocks, KWIN, HEADS, head_dim).astype(jnp.float32)
    scores = jnp.einsum('bihd,bjhd->bhij', query_heads, key_heads) * scaling + pair_bias
    exp_scores = jnp.where(key_mask[:, None, None, :], jnp.exp(scores), 0.0)
    attn_probs = exp_scores / lax.optimization_barrier(jnp.sum(exp_scores, axis=-1, keepdims=True))
    probs_low = rounded(attn_probs)
    attended = jnp.einsum('bhij,bjhd->bihd', probs_low, value_heads).reshape(atom_rows, model_width)
    gate_sig = jax.nn.sigmoid(gate_pre)
    gated_out = (gate_sig * attended).astype(jnp.bfloat16)
    updated = (atoms.astype(jnp.float32) + jnp.dot(gated_out, w_out, preferred_element_type=jnp.float32)).astype(jnp.bfloat16)
    token_pre = jnp.dot(updated, w_token, preferred_element_type=jnp.float32)
    token_sig = jax.nn.sigmoid(token_pre)
    token_act = (token_pre * token_sig).astype(jnp.bfloat16)
    shards = member.shape[0]
    channels = token_act.shape[-1]
    grouped = token_act.reshape(shards, -1, channels).astype(jnp.float32)
    member_f = member.astype(jnp.float32)
    pooled = (jnp.einsum('sat,sac->stc', member_f, grouped) * inv_count[:, :, None]).astype(jnp.bfloat16)
    pooled = pooled.reshape(-1, channels)
    scaled_cot = cotangent.reshape(shards, -1, channels).astype(jnp.float32) * inv_count[:, :, None]
    grad_act = jnp.einsum('sat,stc->sac', member_f, scaled_cot, precision=highest).reshape(atom_rows, channels)
    grad_pre = (grad_act * token_sig * (1.0 + token_pre * (1.0 - token_sig))).astype(jnp.bfloat16)
    grad_token = jnp.dot(updated.T, grad_pre, preferred_element_type=jnp.float32)
    grad_updated = jnp.dot(grad_pre, w_token.T, preferred_element_type=jnp.float32).astype(jnp.bfloat16)
    grad_outw = jnp.dot(gated_out.T, grad_updated, preferred_element_type=jnp.float32)
    grad_gated = jnp.dot(grad_updated, w_out.T, preferred_element_type=jnp.float32)
    grad_gatepre = (grad_gated * attended * gate_sig * (1.0 - gate_sig)).astype(jnp.bfloat16)
    grad_att = rounded(grad_gated * gate_sig)
    grad_heads = grad_att.reshape(blocks, QBLK, HEADS, head_dim)
    grad_probs = jnp.einsum('bihd,bjhd->bhij', grad_heads, value_heads)
    grad_scores = attn_probs * (grad_probs - lax.optimization_barrier(jnp.sum(attn_probs * grad_probs, axis=-1, keepdims=True)))
    scores_low = rounded(grad_scores)
    grad_queries = jnp.einsum('bhij,bjhd->bihd', scores_low, key_heads).reshape(atom_rows, model_width) * scaling
    grad_key_win = jnp.einsum('bhij,bihd->bjhd', scores_low, query_heads).reshape(blocks, KWIN, model_width) * scaling
    grad_value_win = jnp.einsum('bhij,bihd->bjhd', probs_low, grad_heads).reshape(blocks, KWIN, model_width)
    return (pooled, grad_updated, grad_queries, unwindow(grad_key_win, blocks), unwindow(grad_value_win, blocks), grad_gatepre, grad_outw, grad_token, grad_scores)

def reference(atoms, gain, w_query, w_key, w_value, w_gate, w_out, w_token, w_pair, pair_cond, counts, membership, pooled_cot):
    rim_width = (KWIN - QBLK) // 2
    blocks = ATOMS // QBLK
    slot_ids = jnp.arange(ATOMS, dtype=jnp.int32)
    alive_slots = slot_ids % ATOM_DEV < counts[slot_ids // ATOM_DEV]
    key_mask = windows(jnp.pad(alive_slots, (rim_width, rim_width)), blocks)
    pair_f = pair_cond.reshape(blocks, QBLK, KWIN, CP).astype(jnp.float32)
    pair_bias = jnp.einsum('bijc,ch->bhij', pair_f, w_pair.astype(jnp.float32))
    local_ids = membership.reshape(N_SEQ, ATOM_DEV) - (jnp.arange(N_SEQ, dtype=jnp.int32) * TOK_DEV)[:, None]
    member = ((local_ids[:, :, None] == jnp.arange(TOK_DEV, dtype=jnp.int32)[None, None, :]) & alive_slots.reshape(N_SEQ, ATOM_DEV)[:, :, None]).astype(jnp.bfloat16)
    inv_count = 1.0 / lax.optimization_barrier(jnp.sum(member.astype(jnp.float32), axis=1))

    def per_sample(totals, inputs):
        sample_atoms, cotangent = inputs
        atoms_f = sample_atoms.astype(jnp.float32)
        centred = atoms_f - lax.optimization_barrier(jnp.mean(atoms_f, axis=-1, keepdims=True))
        variance = lax.optimization_barrier(jnp.mean(centred * centred, axis=-1, keepdims=True))
        inv_std = lax.rsqrt(variance + epsilon)
        normed = centred * inv_std
        hidden = (normed * gain).astype(jnp.bfloat16)
        queries = jnp.dot(hidden, w_query, preferred_element_type=jnp.float32).astype(jnp.bfloat16)
        keys = jnp.dot(hidden, w_key, preferred_element_type=jnp.float32).astype(jnp.bfloat16)
        values = jnp.dot(hidden, w_value, preferred_element_type=jnp.float32).astype(jnp.bfloat16)
        gate_pre = jnp.dot(hidden, w_gate, preferred_element_type=jnp.float32)
        keys_ext = jnp.pad(keys, ((rim_width, rim_width), (0, 0)))
        values_ext = jnp.pad(values, ((rim_width, rim_width), (0, 0)))
        pooled, grad_updated, grad_queries, grad_keys_ext, grad_values_ext, grad_gatepre, grad_outw, grad_tokw, grad_scores = sample_pass(sample_atoms, queries, keys_ext, values_ext, gate_pre, key_mask, pair_bias, w_out, w_token, member, inv_count, cotangent)
        grad_q_low = grad_queries.astype(jnp.bfloat16)
        grad_k_low = grad_keys_ext[rim_width:rim_width + ATOMS].astype(jnp.bfloat16)
        grad_v_low = grad_values_ext[rim_width:rim_width + ATOMS].astype(jnp.bfloat16)
        grad_hidden = jnp.dot(grad_q_low, w_query.T, preferred_element_type=jnp.float32) + jnp.dot(grad_k_low, w_key.T, preferred_element_type=jnp.float32) + jnp.dot(grad_v_low, w_value.T, preferred_element_type=jnp.float32) + jnp.dot(grad_gatepre, w_gate.T, preferred_element_type=jnp.float32)
        grad_normed = grad_hidden * gain
        grad_ln = inv_std * (grad_normed - lax.optimization_barrier(jnp.mean(grad_normed, axis=-1, keepdims=True)) - normed * lax.optimization_barrier(jnp.mean(grad_normed * normed, axis=-1, keepdims=True)))
        grad_sample = (grad_updated.astype(jnp.float32) + grad_ln).astype(jnp.bfloat16)
        acc_gain, acc_query, acc_key, acc_value, acc_gate, acc_out, acc_token, acc_scores = totals
        totals = (acc_gain + lax.optimization_barrier(jnp.sum(grad_hidden * normed, axis=0)), acc_query + jnp.dot(hidden.T, grad_q_low, preferred_element_type=jnp.float32), acc_key + jnp.dot(hidden.T, grad_k_low, preferred_element_type=jnp.float32), acc_value + jnp.dot(hidden.T, grad_v_low, preferred_element_type=jnp.float32), acc_gate + jnp.dot(hidden.T, grad_gatepre, preferred_element_type=jnp.float32), acc_out + grad_outw, acc_token + grad_tokw, acc_scores + grad_scores)
        return (totals, (pooled, grad_sample))
    start = (jnp.zeros((D,), jnp.float32), jnp.zeros((D, D), jnp.float32), jnp.zeros((D, D), jnp.float32), jnp.zeros((D, D), jnp.float32), jnp.zeros((D, D), jnp.float32), jnp.zeros((D, D), jnp.float32), jnp.zeros((D, TOKW), jnp.float32), jnp.zeros((blocks, HEADS, QBLK, KWIN), jnp.float32))
    totals, (pooled, grad_atoms) = lax.scan(per_sample, start, (atoms, pooled_cot))
    grad_gain, grad_query, grad_key, grad_value, grad_gate, grad_out, grad_token, score_sum = totals
    grad_pair = jnp.einsum('bijc,bhij->ch', pair_f, score_sum)
    return (pooled, grad_atoms, grad_gain, grad_query, grad_key, grad_value, grad_gate, grad_out, grad_token, grad_pair)
```

```python
import functools

import jax
import jax.numpy as jnp
from jax import lax
from jax.experimental import pallas as pl
from jax.experimental.pallas import tpu as pltpu
from jax.sharding import PartitionSpec as P

HEADS = 4
QBLK = 32
KWIN = 128
LOG2E = 1.4426950408889634

epsilon = 1e-05
F32 = jnp.float32
BF16 = jnp.bfloat16
NN = (((1,), (0,)), ((), ()))
NT = (((1,), (1,)), ((), ()))
TN = (((0,), (0,)), ((), ()))
GROUP = 4
LANES = 128
MESH = pl.DeviceIdType.MESH


def mm(a, b, dims=NN):
    return lax.dot_general(a, b, dims, preferred_element_type=F32)


def sigmoid(x):
    return 0.5 * jnp.tanh(0.5 * x) + 0.5


def layer_norm(x, gain):
    centred = x - jnp.mean(x, axis=-1, keepdims=True)
    variance = jnp.mean(centred * centred, axis=-1, keepdims=True)
    inv_std = lax.rsqrt(variance + epsilon)
    normed = centred * inv_std
    return normed, inv_std, (normed * gain).astype(BF16)


def head_lanes(width):
    lane = lax.broadcasted_iota(jnp.int32, (1, width), 1)
    return lane // (width // HEADS)


def expand(block, masks):
    return jnp.concatenate([block * m for m in masks], axis=0)


def collapse(wide, lane_head):
    rows = wide.shape[0] // HEADS
    out = wide[:rows]
    for h in range(1, HEADS):
        out = jnp.where(lane_head == h, wide[h * rows : (h + 1) * rows], out)
    return out


def lane_swap(parts, lane_block):
    count = len(parts)
    outs = []
    for b in range(count):
        out = None
        for a in range(count):
            shift = (QBLK * (a - b)) % LANES
            moved = parts[a] if shift == 0 else pltpu.roll(parts[a], shift, 1)
            out = moved if out is None else jnp.where(lane_block == a, moved, out)
        outs.append(out)
    return outs


def pair_weights(wpair_ref, per):
    channels = wpair_ref.shape[0]
    high, wide = HEADS * per, per * channels
    row = lax.broadcasted_iota(jnp.int32, (high, HEADS), 0) // per
    head = lax.broadcasted_iota(jnp.int32, (high, HEADS), 1)
    pick = jnp.where(row == head, 1.0, 0.0).astype(BF16)
    by_row = mm(pick, wpair_ref[...], NT).astype(BF16)
    lane = lax.rem(lax.broadcasted_iota(jnp.int32, (channels, wide), 1), channels)
    chan = lax.broadcasted_iota(jnp.int32, (channels, wide), 0)
    spread = mm(by_row, jnp.where(lane == chan, 1.0, 0.0).astype(BF16))
    key = lax.rem(lax.broadcasted_iota(jnp.int32, (high, wide), 0), per)
    spot = lax.broadcasted_iota(jnp.int32, (high, wide), 1) // channels
    return jnp.where(key == spot, spread, 0.0).astype(BF16)


def build_bias(counts_ref, pair_ref, wsm, bias_scr, blocks, rows):
    pos = lax.axis_index("seq")
    size = lax.axis_size("seq")
    own = counts_ref[pos]
    left = jnp.where(pos > 0, counts_ref[jnp.maximum(pos - 1, 0)], 0)
    right = jnp.where(pos < size - 1, counts_ref[jnp.minimum(pos + 1, size - 1)], 0)
    rim = (KWIN - QBLK) // 2
    lane_block = head_lanes(LANES)
    chunk = wsm.shape[1]
    per = wsm.shape[0] // HEADS
    for kk in range(pair_ref.shape[1] // chunk):
        biased = mm(wsm, pair_ref[:, kk * chunk : (kk + 1) * chunk], NT)
        for g in range(blocks // GROUP):
            parts = [
                biased[h * per : (h + 1) * per, g * LANES : (g + 1) * LANES] for h in range(HEADS)
            ]
            for w, out in enumerate(lane_swap(parts, lane_block)):
                b = g * GROUP + w
                slot = (
                    lax.broadcasted_iota(jnp.int32, (per, LANES), 0) + kk * per + b * QBLK - rim
                )
                alive = (
                    ((slot < 0) & (slot + rows < left))
                    | ((slot >= 0) & (slot < own))
                    | ((slot >= rows) & (slot - rows < right))
                )
                bias_scr[b, kk * per : (kk + 1) * per, :] = jnp.where(alive, out * LOG2E, -1e30)


def pair_gradient(pair_ref, score_scr, per, chunk, blocks):
    lane_block = head_lanes(LANES)
    total = None
    for kk in range(pair_ref.shape[1] // chunk):
        columns = []
        for g in range(blocks // GROUP):
            parts = [score_scr[g * GROUP + w, kk * per : (kk + 1) * per, :] for w in range(GROUP)]
            columns.append(jnp.concatenate(lane_swap(parts, lane_block), axis=0))
        grads = jnp.concatenate(columns, axis=1).astype(BF16)
        part = mm(grads, pair_ref[:, kk * chunk : (kk + 1) * chunk])
        total = part if total is None else total + part
    high, wide = total.shape
    row = lax.broadcasted_iota(jnp.int32, (high, wide), 0)
    lane = lax.broadcasted_iota(jnp.int32, (high, wide), 1)
    diagonal = jnp.where(lax.rem(row, per) == lane // (wide // per), total, 0.0)
    lines = []
    for h in range(HEADS):
        line = jnp.sum(diagonal[h * per : (h + 1) * per], axis=0, keepdims=True)
        folded = line[:, :LANES]
        for n in range(1, wide // LANES):
            folded = folded + line[:, n * LANES : (n + 1) * LANES]
        lines.append(folded)
    return lines


def weave(*lists):
    lists = [x for x in lists if x]
    done = [0] * len(lists)
    while True:
        best = None
        for n, x in enumerate(lists):
            if done[n] < len(x):
                share = (done[n] + 0.5) / len(x)
                if best is None or share < best[0]:
                    best = (share, n)
        if best is None:
            return
        n = best[1]
        lists[n][done[n]]()
        done[n] += 1


def axis_sizes():
    return [(axis, lax.axis_size(axis)) for axis in ("samp", "seq")]


def shifted_index(axis, size, distance):
    return lax.rem(lax.axis_index(axis) + distance, size)


class Summer:
    def __init__(self, buf, out, streams, orders, send_sem, recv_sem, slots):
        self.buf, self.out, self.streams, self.orders = buf, out, streams, orders
        self.send_sem, self.recv_sem = send_sem, recv_sem
        self.sends, self.recvs = slots[: 2 * streams], slots[2 * streams :]
        self.unit = buf.shape[0] // streams
        self.peers = sum(size - 1 for _, size in orders[0])

    def spans(self, stream):
        (a0, s0), (a1, s1) = self.orders[stream]
        off0 = stream * self.unit
        len1 = self.unit // s0
        len2 = len1 // s1
        off1 = off0 + lax.axis_index(a0) * len1
        off2 = off1 + lax.axis_index(a1) * len2
        return [(off0, self.unit), (off1, len1), (off2, len2)]

    def copy(self, stream, src, dst, slot, partner):
        at = stream * 2 * self.peers + slot
        return pltpu.make_async_remote_copy(
            src_ref=src,
            dst_ref=dst,
            send_sem=self.send_sem.at[at],
            recv_sem=self.recv_sem.at[at],
            device_id=partner,
            device_id_type=MESH,
        )

    def scatter_copies(self, stream, k):
        axis, size = self.orders[stream][k]
        base = 0 if k == 0 else self.orders[stream][0][1] - 1
        return [
            self.copy(
                stream,
                self.sends[2 * stream + k].at[d - 1],
                self.recvs[2 * stream + k].at[d - 1],
                base + d - 1,
                {axis: shifted_index(axis, size, d)},
            )
            for d in range(1, size)
        ]

    def gather_copies(self, stream, k):
        axis, size = self.orders[stream][k]
        base = self.peers + (0 if k == 1 else self.orders[stream][1][1] - 1)
        off, length = self.spans(stream)[k + 1]
        part = self.out.at[pl.ds(pl.multiple_of(off, 16), length), :]
        return [
            self.copy(stream, part, part, base + d - 1, {axis: shifted_index(axis, size, d)})
            for d in range(1, size)
        ]

    def scatter(self, k):
        for stream in range(self.streams):
            spans = self.spans(stream)
            axis, size = self.orders[stream][k]
            if k > 0:
                off, length = spans[k]
                rows = pl.ds(pl.multiple_of(off, 16), length)
                self.buf[rows, :] = self.absorbed(stream, k - 1)
            off, length = spans[k][0], spans[k + 1][1]
            for d, copy in enumerate(self.scatter_copies(stream, k), 1):
                give = pl.multiple_of(off + shifted_index(axis, size, d) * length, 16)
                self.sends[2 * stream + k][d - 1] = self.buf[pl.ds(give, length), :].astype(BF16)
                copy.start()

    def absorbed(self, stream, k):
        off, length = self.spans(stream)[k + 1]
        value = self.buf[pl.ds(pl.multiple_of(off, 16), length), :]
        for n, copy in enumerate(self.scatter_copies(stream, k)):
            copy.wait()
            value = value + self.recvs[2 * stream + k][n].astype(F32)
        return value

    def gather(self, k):
        for stream in range(self.streams):
            if k == 1:
                off, length = self.spans(stream)[2]
                rows = pl.ds(pl.multiple_of(off, 16), length)
                self.out[rows, :] = self.absorbed(stream, 1).astype(BF16)
            else:
                for copy in self.gather_copies(stream, 1):
                    copy.wait()
            for copy in self.gather_copies(stream, k):
                copy.start()

    def finish(self):
        for stream in range(self.streams):
            for copy in self.gather_copies(stream, 0):
                copy.wait()

    def actions(self):
        return [
            lambda: self.scatter(0),
            lambda: self.scatter(1),
            lambda: self.gather(1),
            lambda: self.gather(0),
            self.finish,
        ]


def step_kernel(
    samples,
    early_streams,
    late_streams,
    counts_ref,
    atoms_hbm,
    atoms_ref,
    again_ref,
    gain_ref,
    wq_ref,
    wk_ref,
    wv_ref,
    wg_ref,
    wo_ref,
    wt_ref,
    wpair_ref,
    pair_ref,
    ids_ref,
    cot_ref,
    pooled_ref,
    gatoms_ref,
    early_ref,
    late_ref,
    small_ref,
    low_in,
    high_in,
    edge_out,
    edge_in,
    bias_scr,
    score_scr,
    member_scr,
    member_t_scr,
    inv_scr,
    wqg_scr,
    wkv_scr,
    wall_scr,
    hid_scr,
    gate_scr,
    gated_scr,
    back_scr,
    q_all,
    kv_all,
    low_all,
    gx_all,
    dg_all,
    gupd_all,
    d_scr,
    gout_scr,
    gtok_scr,
    gw_scr,
    ggain_scr,
    early_buf,
    late_buf,
    early_sum,
    late_sum,
    small_a,
    small_b,
    small_src,
    halo_send,
    halo_recv,
    edge_send,
    edge_recv,
    early_send,
    early_recv,
    late_send,
    late_recv,
    small_send,
    small_recv,
    *slots,
):
    step = pl.program_id(0)
    rows, width = q_all.shape[1:]
    blocks = rows // QBLK
    rim = (KWIN - QBLK) // 2
    tokens = inv_scr.shape[0]
    per = 2 * LANES // wpair_ref.shape[0]
    pair_chunk = per * wpair_ref.shape[0]
    scaling = (width // HEADS) ** (-0.5)
    lane_head = head_lanes(width)
    masks = [(lane_head == h).astype(F32).astype(BF16) for h in range(HEADS)]
    ones = jnp.ones((KWIN, width), BF16)
    axes = axis_sizes()
    pos = lax.axis_index("seq")
    size = lax.axis_size("seq")
    last = 2 * samples

    early_orders = [axes[::-1] if s % 2 == 1 else axes for s in range(early_streams)]
    early = Summer(
        early_buf,
        early_sum,
        early_streams,
        early_orders,
        early_send,
        early_recv,
        slots[: 4 * early_streams],
    )
    late = Summer(
        late_buf,
        late_sum,
        late_streams,
        [axes] * late_streams,
        late_send,
        late_recv,
        slots[4 * early_streams :],
    )

    def to_right(src, dst, send_sem, recv_sem):
        return pltpu.make_async_remote_copy(
            src_ref=src,
            dst_ref=dst,
            send_sem=send_sem,
            recv_sem=recv_sem,
            device_id={"seq": jnp.minimum(pos + 1, size - 1)},
            device_id_type=MESH,
        )

    def to_left(src, dst, send_sem, recv_sem):
        return pltpu.make_async_remote_copy(
            src_ref=src,
            dst_ref=dst,
            send_sem=send_sem,
            recv_sem=recv_sem,
            device_id={"seq": jnp.maximum(pos - 1, 0)},
            device_id_type=MESH,
        )

    def halo(part):
        span = pl.ds(0, 1) if part == 0 else pl.ds(1, samples - 1)
        right = to_right(
            atoms_hbm.at[span, rows - rim : rows, :],
            low_in.at[span],
            halo_send.at[0, part],
            halo_recv.at[0, part],
        )
        left = to_left(
            atoms_hbm.at[span, 0:rim, :],
            high_in.at[span],
            halo_send.at[1, part],
            halo_recv.at[1, part],
        )
        return right, left

    def edges(j):
        right = to_right(
            edge_out.at[1, j], edge_in.at[0, j], edge_send.at[0, j], edge_recv.at[0, j]
        )
        left = to_left(
            edge_out.at[0, j], edge_in.at[1, j], edge_send.at[1, j], edge_recv.at[1, j]
        )
        return right, left

    def launch(pair):
        right, left = pair

        @pl.when(pos < size - 1)
        def _():
            right.start()

        @pl.when(pos > 0)
        def _():
            left.start()

    def collect(pair):
        right, left = pair

        @pl.when(pos < size - 1)
        def _():
            right.wait_send()
            left.wait_recv()

        @pl.when(pos > 0)
        def _():
            left.wait_send()
            right.wait_recv()

    def forward_stages(s):
        slot = lax.rem(s, 2)
        gain = gain_ref[...]
        stages = []
        cuts = 4
        chunk = rows // cuts

        def rims():
            hid_scr[:rim] = layer_norm(low_in[s].astype(F32), gain)[2]
            hid_scr[rim + rows :] = layer_norm(high_in[s].astype(F32), gain)[2]
            kv_all[s, :rim] = mm(hid_scr[:rim], wkv_scr[...]).astype(BF16)
            kv_all[s, rim + rows :] = mm(hid_scr[rim + rows :], wkv_scr[...]).astype(BF16)

        def norm(c):
            def run():
                x = atoms_ref[0, c * chunk : (c + 1) * chunk].astype(F32)
                hid_scr[rim + c * chunk : rim + (c + 1) * chunk] = layer_norm(x, gain)[2]

            return run

        def project(c):
            def run():
                span = slice(c * chunk, (c + 1) * chunk)
                hidden = hid_scr[rim + c * chunk : rim + (c + 1) * chunk]
                kv_all[s, rim + c * chunk : rim + (c + 1) * chunk] = mm(
                    hidden, wkv_scr[...]
                ).astype(BF16)
                qg = mm(hidden, wqg_scr[...])
                q_all[s, span] = qg[:, :width].astype(BF16)
                gate_scr[span] = sigmoid(qg[:, width:])

            return run

        def score(spans):
            def run():
                q_exp = [expand(q_all[s, b * QBLK : (b + 1) * QBLK, :], masks) for b in spans]
                scores = [
                    mm(kv_all[s, b * QBLK : b * QBLK + KWIN, :width], q, NT)
                    for b, q in zip(spans, q_exp)
                ]
                for b, sc in zip(spans, scores):
                    low_all[s, b] = jnp.exp2(sc * (scaling * LOG2E) + bias_scr[b]).astype(BF16)

            return run

        def attend(spans):
            def run():
                wide = [
                    mm(
                        low_all[s, b],
                        jnp.concatenate(
                            [kv_all[s, b * QBLK : b * QBLK + KWIN, width:], ones], axis=1
                        ),
                        TN,
                    )
                    for b in spans
                ]
                for b, o in zip(spans, wide):
                    span = slice(b * QBLK, (b + 1) * QBLK)
                    inv = 1.0 / collapse(o[:, width:], lane_head)
                    att = collapse(o[:, :width], lane_head) * inv
                    gate = gate_scr[span]
                    gated = gate * att
                    scaled = gate * inv
                    gated_scr[slot, span] = gated.astype(BF16)
                    back_scr[slot, 0, span] = scaled
                    back_scr[slot, 1, span] = -(scaled * att)
                    back_scr[slot, 2, span] = gated * (1.0 - gate)

            return run

        stages.append(rims)
        stages.append(norm(0))
        for c in range(cuts):
            if c + 1 < cuts:
                stages.append(norm(c + 1))
            stages.append(project(c))
        groups = [
            [g * GROUP + w for w in range(GROUP)] for g in range(blocks // GROUP)
        ]
        stages.append(score(groups[0]))
        for g in range(len(groups)):
            if g + 1 < len(groups):
                stages.append(score(groups[g + 1]))
            stages.append(attend(groups[g]))
        return stages

    def token_stages(s):
        slot = lax.rem(s, 2)
        chunk = 256
        half = rows // 2
        held = {}
        stages = []

        def begin():
            gated = gated_scr[slot]
            x = again_ref[0].astype(F32)
            held["updated"] = (x + mm(gated, wo_ref[...])).astype(BF16)
            held["cot"] = (cot_ref[0].astype(F32) * inv_scr[...]).astype(BF16)
            held["gupd"] = [None, None]

        def piece(c, r):
            def run():
                cols = slice(c * chunk, (c + 1) * chunk)
                wt = wt_ref[:, cols]
                span = slice(r * half, (r + 1) * half)
                upd = held["updated"][span]
                pre = mm(upd, wt)
                sig = sigmoid(pre)
                act = pre * sig
                grad_act = mm(member_scr[span, :], held["cot"][:, cols])
                grad_pre = (grad_act * (sig + act * (1.0 - sig))).astype(BF16)
                pooled = mm(member_t_scr[:, span], act.astype(BF16))
                gtok = mm(upd, grad_pre, TN)
                part = mm(grad_pre, wt, NT)
                if r == 0:
                    held["pooled"], held["gtok"] = pooled, gtok
                else:
                    pooled_ref[0, :, cols] = ((held["pooled"] + pooled) * inv_scr[...]).astype(BF16)
                    gtok_scr[:, cols] += held["gtok"] + gtok
                before = held["gupd"][r]
                held["gupd"][r] = part if before is None else before + part

            return run

        def end():
            grad_updated = jnp.concatenate(held["gupd"], axis=0).astype(BF16)
            gupd_all[s] = grad_updated
            gout_scr[...] += mm(gated_scr[slot], grad_updated, TN)
            grad_gated = mm(grad_updated, wo_ref[...], NT)
            gx_all[s, :, :width] = (grad_gated * back_scr[slot, 0]).astype(BF16)
            gx_all[s, :, width:] = (grad_gated * back_scr[slot, 1]).astype(BF16)
            dg_all[s] = (grad_gated * back_scr[slot, 2]).astype(BF16)

        stages.append(begin)
        for c in range(wt_ref.shape[1] // chunk):
            for r in range(2):
                stages.append(piece(c, r))
        stages.append(end)
        return stages

    def backward_stages(s):
        slot = lax.rem(s, 2)
        open_k = []
        open_v = []
        held = {}
        stages = []

        def tiles(x):
            return [x[n * QBLK : (n + 1) * QBLK] for n in range(KWIN // QBLK)]

        def store(at, k, v):
            if at < rim:
                edge_out[0, s, at : at + k.shape[0], :width] = k
                edge_out[0, s, at : at + k.shape[0], width:] = v
            elif at < rim + rows:
                d_scr[slot, at - rim : at - rim + k.shape[0], width : 2 * width] = k
                d_scr[slot, at - rim : at - rim + k.shape[0], 2 * width : 3 * width] = v
            else:
                at = at - rim - rows
                edge_out[1, s, at : at + k.shape[0], :width] = k
                edge_out[1, s, at : at + k.shape[0], width:] = v

        def close(first, count):
            for n in range(count):
                at = (first + n) * QBLK
                k = (open_k[n] * scaling).astype(BF16)
                v = open_v[n].astype(BF16)
                half = QBLK // 2
                store(at, k[:half], v[:half])
                store(at + half, k[half:], v[half:])
            del open_k[:count]
            del open_v[:count]

        def merge(opened, parts):
            for n, part in enumerate(parts):
                if n < len(opened):
                    opened[n] = opened[n] + part
                else:
                    opened.append(part)

        def grads(g, spans):
            def run():
                gx = [
                    jnp.concatenate(
                        [
                            expand(gx_all[s, b * QBLK : (b + 1) * QBLK, :width], masks),
                            expand(gx_all[s, b * QBLK : (b + 1) * QBLK, width:], masks),
                        ],
                        axis=1,
                    )
                    for b in spans
                ]
                gps = [
                    mm(
                        jnp.concatenate(
                            [kv_all[s, b * QBLK : b * QBLK + KWIN, width:], ones], axis=1
                        ),
                        x,
                        NT,
                    )
                    for b, x in zip(spans, gx)
                ]
                dss = [low_all[s, b].astype(F32) * gp for b, gp in zip(spans, gps)]
                for b, ds in zip(spans, dss):
                    score_scr[b] += ds
                held[g] = [ds.astype(BF16) for ds in dss]
                held[g, "dv"] = [mm(low_all[s, b], x[:, :width]) for b, x in zip(spans, gx)]

            return run

        def products(g, spans):
            def run():
                lows = held.pop(g)
                dvs = held.pop((g, "dv"))
                q_exp = [expand(q_all[s, b * QBLK : (b + 1) * QBLK, :], masks) for b in spans]
                dks = [mm(low, q) for low, q in zip(lows, q_exp)]
                dqs = [
                    mm(low, kv_all[s, b * QBLK : b * QBLK + KWIN, :width], TN)
                    for b, low in zip(spans, lows)
                ]
                for b, dk, dv in zip(spans, dks, dvs):
                    merge(open_k, tiles(dk))
                    merge(open_v, tiles(dv))
                    close(b, 1)
                for b, dq in zip(spans, dqs):
                    d_scr[slot, b * QBLK : (b + 1) * QBLK, :width] = (
                        collapse(dq, lane_head) * scaling
                    ).astype(BF16)

            return run

        group = 2
        groups = [[g * group + w for w in range(group)] for g in range(blocks // group)]
        stages.append(grads(0, groups[0]))
        for g in range(len(groups)):
            if g + 1 < len(groups):
                stages.append(grads(g + 1, groups[g + 1]))
            stages.append(products(g, groups[g]))
        stages.append(lambda: close(blocks, len(open_k)))
        return stages

    def tail_stages(s):
        slot = lax.rem(s, 2)
        gain = gain_ref[...]
        stages = []
        cuts = 2
        chunk = rows // cuts
        held = {}

        def gather():
            d_scr[slot, :, 3 * width :] = dg_all[s]
            d_scr[slot, :rim, width : 3 * width] = (
                d_scr[slot, :rim, width : 3 * width].astype(F32) + edge_in[0, s].astype(F32)
            ).astype(BF16)
            d_scr[slot, rows - rim :, width : 3 * width] = (
                d_scr[slot, rows - rim :, width : 3 * width].astype(F32)
                + edge_in[1, s].astype(F32)
            ).astype(BF16)

        def norm(c):
            def run():
                held[c] = layer_norm(again_ref[0, c * chunk : (c + 1) * chunk].astype(F32), gain)

            return run

        def multiply(c):
            def run():
                d = d_scr[slot, c * chunk : (c + 1) * chunk]
                held["gh", c] = mm(d, wall_scr[...], NT)
                gw_scr[...] += mm(held[c][2], d, TN)

            return run

        def finish(c):
            def run():
                normed, inv_std, _ = held[c]
                grad_hidden = held["gh", c]
                gn = grad_hidden * normed
                ggain_scr[...] += jnp.sum(gn, axis=0, keepdims=True)
                gx = grad_hidden * gain
                grad_ln = inv_std * (
                    gx
                    - jnp.mean(gx, axis=-1, keepdims=True)
                    - normed * jnp.mean(gn * gain, axis=-1, keepdims=True)
                )
                span = slice(c * chunk, (c + 1) * chunk)
                gatoms_ref[0, span] = (gupd_all[s, span].astype(F32) + grad_ln).astype(BF16)

            return run

        stages.append(gather)
        for c in range(cuts):
            stages += [norm(c), multiply(c), finish(c)]
        return stages

    @pl.when(step == 0)
    def _():
        barrier = pltpu.get_barrier_semaphore()
        for axis, count in axes:
            for d in range(1, count):
                pl.semaphore_signal(
                    barrier,
                    inc=1,
                    device_id={axis: shifted_index(axis, count, d)},
                    device_id_type=MESH,
                )

        @pl.when(pos == 0)
        def _():
            low_in[...] = jnp.zeros_like(low_in)
            edge_in[0] = jnp.zeros_like(edge_in[0])

        @pl.when(pos == size - 1)
        def _():
            high_in[...] = jnp.zeros_like(high_in)
            edge_in[1] = jnp.zeros_like(edge_in[1])

        pl.semaphore_wait(barrier, sum(count - 1 for _, count in axes))
        for part in range(2):
            launch(halo(part))
        build_bias(
            counts_ref, pair_ref, pair_weights(wpair_ref, per), bias_scr, blocks, rows
        )
        token = lax.broadcasted_iota(jnp.int32, (tokens, rows), 0)
        place = lax.broadcasted_iota(jnp.int32, (tokens, rows), 1)
        hit = (ids_ref[...] - pos * tokens == token) & (place < counts_ref[pos])
        member_t = jnp.where(hit, 1.0, 0.0).astype(F32)
        inv_scr[...] = 1.0 / jnp.sum(member_t, axis=1, keepdims=True)
        member_t_scr[...] = member_t.astype(BF16)
        member_scr[...] = member_t.T.astype(BF16)
        wqg_scr[:, :width] = wq_ref[...]
        wqg_scr[:, width:] = wg_ref[...]
        wkv_scr[:, :width] = wk_ref[...]
        wkv_scr[:, width:] = wv_ref[...]
        for n, ref in enumerate((wq_ref, wk_ref, wv_ref, wg_ref)):
            wall_scr[:, n * width : (n + 1) * width] = ref[...]
        for ref in (score_scr, gout_scr, gtok_scr, gw_scr, ggain_scr):
            ref[...] = jnp.zeros_like(ref)
        collect(halo(0))
        weave(forward_stages(0))
        collect(halo(1))

    @pl.when((step > 0) & (step < samples))
    def _():
        weave(token_stages(step - 1), forward_stages(step))

    @pl.when(step == samples)
    def _():
        weave(token_stages(samples - 1), backward_stages(0))

    @pl.when((step > samples) & (step < last))
    def _():
        collect(edges(step - samples - 1))
        weave(tail_stages(step - samples - 1), backward_stages(step - samples))

    @pl.when((step >= samples) & (step < last))
    def _():
        launch(edges(step - samples))

    def fill_early():
        for n in range(gtok_scr.shape[1] // width):
            early_buf[n * width : (n + 1) * width, :] = gtok_scr[:, n * width : (n + 1) * width]
        at = gtok_scr.shape[1]
        early_buf[at : at + width, :] = gout_scr[...]
        early_buf[at + width :, :] = jnp.zeros((early_buf.shape[0] - at - width, width), F32)

    for n, action in enumerate(early.actions()):

        def run(n=n, action=action):
            if n == 0:
                fill_early()
            action()

        pl.when(step == min(samples + 2 * n, last))(run)

    @pl.when(step == last)
    def _():
        lines = pair_gradient(pair_ref, score_scr, per, pair_chunk, blocks)
        collect(edges(samples - 1))
        weave(tail_stages(samples - 1))
        for n in range(4):
            late_buf[n * width : (n + 1) * width, :] = gw_scr[:, n * width : (n + 1) * width]
        if late_buf.shape[0] > 4 * width:
            late_buf[4 * width :, :] = jnp.zeros((late_buf.shape[0] - 4 * width, width), F32)
        acts = late.actions()
        acts[0]()
        small_src[0] = jnp.concatenate(
            lines + [ggain_scr[...], jnp.zeros((8 - HEADS - 1, width), F32)], axis=0
        )

        def small_copies(k):
            axis, count = axes[k]
            base = 0 if k == 0 else axes[0][1] - 1
            return [
                pltpu.make_async_remote_copy(
                    src_ref=small_src.at[k],
                    dst_ref=(small_a, small_b)[k].at[d - 1],
                    send_sem=small_send.at[base + d - 1],
                    recv_sem=small_recv.at[base + d - 1],
                    device_id={axis: shifted_index(axis, count, d)},
                    device_id_type=MESH,
                )
                for d in range(1, count)
            ]

        for copy in small_copies(0):
            copy.start()
        acts[1]()
        value = small_src[0]
        for n, copy in enumerate(small_copies(0)):
            copy.wait()
            value = value + small_a[n]
        small_src[1] = value
        for copy in small_copies(1):
            copy.start()
        acts[2]()
        for n, copy in enumerate(small_copies(1)):
            copy.wait()
            value = value + small_b[n]
        small_ref[...] = value
        acts[3]()
        early_ref[...] = early_sum[...]
        acts[4]()
        late_ref[...] = late_sum[...]


def unpack_kernel(
    channels,
    early_ref,
    late_ref,
    small_ref,
    ggain_out,
    gq_out,
    gk_out,
    gv_out,
    gg_out,
    gout_out,
    gtok_out,
    gpair_out,
):
    width = gout_out.shape[0]
    blocks = gtok_out.shape[1] // width

    def block(ref, n):
        return ref[n * width : (n + 1) * width, :].astype(F32)

    for n in range(blocks):
        gtok_out[:, n * width : (n + 1) * width] = block(early_ref, n)
    gout_out[...] = block(early_ref, blocks)
    for n, ref in enumerate((gq_out, gk_out, gv_out, gg_out)):
        ref[...] = block(late_ref, n)
    lines = small_ref[...]
    ggain_out[...] = lines[HEADS : HEADS + 1]
    shift = width // 2
    while shift >= channels:
        lines = lines + pltpu.roll(lines, shift, 1)
        shift //= 2
    gpair_out[...] = lines[:HEADS, :channels]


def whole(*shape):
    return pl.BlockSpec(shape, lambda s: (0,) * len(shape))


def sum_scratch(total, streams, orders, width):
    unit = total // streams
    slots = []
    for stream in range(streams):
        length = unit
        for _, size in orders[stream]:
            length //= size
            slots.append(pltpu.VMEM((size - 1, length, width), BF16))
    return slots * 2


def on_device(
    atoms,
    gain,
    w_query,
    w_key,
    w_value,
    w_gate,
    w_out,
    w_token,
    w_pair,
    pair_cond,
    counts,
    membership,
    pooled_cot,
):
    samples, rows, width = atoms.shape
    blocks = rows // QBLK
    rim = (KWIN - QBLK) // 2
    tokens, token_width = pooled_cot.shape[1:]
    channels = w_pair.shape[0]
    pair2 = pair_cond.reshape(blocks * QBLK, pair_cond.shape[-1])
    gain2 = gain.reshape(1, width)
    ids2 = membership.reshape(1, rows)
    square = whole(width, width)
    shape = jax.ShapeDtypeStruct
    vmem = pltpu.VMEM
    dma = pltpu.SemaphoreType.DMA

    axes = axis_sizes()
    devices = axes[0][1] * axes[1][1]
    peers = sum(size - 1 for _, size in axes)
    unit = 16 * devices
    early_total = -(-(token_width + width) // unit) * unit
    late_total = -(-(4 * width) // unit) * unit
    early_streams = early_total // unit
    late_streams = late_total // unit
    early_orders = [axes[::-1] if s % 2 == 1 else axes for s in range(early_streams)]

    def clip(x):
        return jnp.clip(x, 0, samples - 1)

    def again(i):
        return jnp.where(i <= samples, clip(i - 1), clip(i - samples - 1))

    pooled, gatoms, early, late, small = pl.pallas_call(
        functools.partial(step_kernel, samples, early_streams, late_streams),
        grid=(2 * samples + 1,),
        in_specs=[
            pl.BlockSpec(memory_space=pltpu.SMEM),
            pl.BlockSpec(memory_space=pl.ANY),
            pl.BlockSpec((1, rows, width), lambda i: (clip(i), 0, 0)),
            pl.BlockSpec((1, rows, width), lambda i: (again(i), 0, 0)),
            whole(1, width),
            square,
            square,
            square,
            square,
            square,
            whole(width, token_width),
            whole(*w_pair.shape),
            whole(*pair2.shape),
            whole(1, rows),
            pl.BlockSpec((1, tokens, token_width), lambda i: (clip(i - 1), 0, 0)),
        ],
        out_specs=[
            pl.BlockSpec((1, tokens, token_width), lambda i: (clip(i - 1), 0, 0)),
            pl.BlockSpec((1, rows, width), lambda i: (clip(i - samples - 1), 0, 0)),
            whole(early_total, width),
            whole(late_total, width),
            whole(8, width),
        ],
        out_shape=[
            shape((samples, tokens, token_width), BF16),
            shape((samples, rows, width), BF16),
            shape((early_total, width), BF16),
            shape((late_total, width), BF16),
            shape((8, width), F32),
        ],
        scratch_shapes=[
            vmem((samples, rim, width), BF16),
            vmem((samples, rim, width), BF16),
            vmem((2, samples, rim, 2 * width), BF16),
            vmem((2, samples, rim, 2 * width), BF16),
            vmem((blocks, KWIN, LANES), F32),
            vmem((blocks, KWIN, LANES), F32),
            vmem((rows, tokens), BF16),
            vmem((tokens, rows), BF16),
            vmem((tokens, 1), F32),
            vmem((width, 2 * width), BF16),
            vmem((width, 2 * width), BF16),
            vmem((width, 4 * width), BF16),
            vmem((rows + 2 * rim, width), BF16),
            vmem((rows, width), F32),
            vmem((2, rows, width), BF16),
            vmem((2, 3, rows, width), F32),
            vmem((samples, rows, width), BF16),
            vmem((samples, rows + 2 * rim, 2 * width), BF16),
            vmem((samples, blocks, KWIN, LANES), BF16),
            vmem((samples, rows, 2 * width), BF16),
            vmem((samples, rows, width), BF16),
            vmem((samples, rows, width), BF16),
            vmem((2, rows, 4 * width), BF16),
            vmem((width, width), F32),
            vmem((width, token_width), F32),
            vmem((width, 4 * width), F32),
            vmem((1, width), F32),
            vmem((early_total, width), F32),
            vmem((late_total, width), F32),
            vmem((early_total, width), BF16),
            vmem((late_total, width), BF16),
            vmem((axes[0][1] - 1, 8, width), F32),
            vmem((axes[1][1] - 1, 8, width), F32),
            vmem((2, 8, width), F32),
            dma((2, 2)),
            dma((2, 2)),
            dma((2, samples)),
            dma((2, samples)),
            dma((2 * early_streams * peers,)),
            dma((2 * early_streams * peers,)),
            dma((2 * late_streams * peers,)),
            dma((2 * late_streams * peers,)),
            dma((peers,)),
            dma((peers,)),
        ]
        + sum_scratch(early_total, early_streams, early_orders, width)
        + sum_scratch(late_total, late_streams, [axes] * late_streams, width),
        compiler_params=pltpu.CompilerParams(
            dimension_semantics=("arbitrary",),
            vmem_limit_bytes=56 * 1024 * 1024,
            collective_id=0,
            has_side_effects=True,
        ),
    )(
        counts,
        atoms,
        atoms,
        atoms,
        gain2,
        w_query,
        w_key,
        w_value,
        w_gate,
        w_out,
        w_token,
        w_pair,
        pair2,
        ids2,
        pooled_cot,
    )
    spec = pl.BlockSpec(memory_space=pltpu.VMEM)
    ggain, gq, gk, gv, gg, gout, gtok, gpair = pl.pallas_call(
        functools.partial(unpack_kernel, channels),
        in_specs=[spec] * 3,
        out_specs=[spec] * 8,
        out_shape=[shape((1, width), F32)]
        + [shape((width, width), F32)] * 5
        + [shape((width, token_width), F32), shape((HEADS, channels), F32)],
    )(early, late, small)
    return (pooled, gatoms, ggain.reshape(width), gq, gk, gv, gg, gout, gtok, gpair.T)


def solution(mesh):
    placed = (
        P("samp", "seq", None),
        P(),
        P(),
        P(),
        P(),
        P(),
        P(),
        P(),
        P(),
        P("seq", None, None),
        P(),
        P("seq"),
        P("samp", "seq", None),
    )
    return jax.shard_map(
        on_device,
        mesh=mesh,
        in_specs=placed,
        out_specs=(
            P("samp", "seq", None),
            P("samp", "seq", None),
            P(),
            P(),
            P(),
            P(),
            P(),
            P(),
            P(),
            P(),
        ),
        check_vma=False,
    )
```

```python
import functools

import jax
import jax.numpy as jnp
from jax import lax
from jax.experimental import pallas as pl
from jax.experimental.pallas import tpu as pltpu
from jax.sharding import PartitionSpec as P

HEADS = 4
QBLK = 32
KWIN = 128
LOG2E = 1.4426950408889634

epsilon = 1e-05
F32 = jnp.float32
BF16 = jnp.bfloat16
NN = (((1,), (0,)), ((), ()))
NT = (((1,), (1,)), ((), ()))
TN = (((0,), (0,)), ((), ()))
GROUP = 4
FGROUP = 4
PARTS = 2
LANES = 128
MESH = pl.DeviceIdType.MESH
LAG = 3


def mm(a, b, dims=NN):
    return lax.dot_general(a, b, dims, preferred_element_type=F32)


def sigmoid(x):
    return 0.5 * jnp.tanh(0.5 * x) + 0.5


def layer_norm(x, gain):
    centred = x - jnp.mean(x, axis=-1, keepdims=True)
    variance = jnp.mean(centred * centred, axis=-1, keepdims=True)
    inv_std = lax.rsqrt(variance + epsilon)
    normed = centred * inv_std
    return normed, inv_std, (normed * gain).astype(BF16)


def head_lanes(width):
    lane = lax.broadcasted_iota(jnp.int32, (1, width), 1)
    return lane // (width // HEADS)


def expand(block, masks):
    return jnp.concatenate([block * m for m in masks], axis=0)


def collapse(wide, lane_head):
    rows = wide.shape[0] // HEADS
    out = wide[:rows]
    for h in range(1, HEADS):
        out = jnp.where(lane_head == h, wide[h * rows : (h + 1) * rows], out)
    return out


def lane_swap(parts, lane_block):
    count = len(parts)
    outs = []
    for b in range(count):
        out = None
        for a in range(count):
            shift = (QBLK * (a - b)) % LANES
            moved = parts[a] if shift == 0 else pltpu.roll(parts[a], shift, 1)
            out = moved if out is None else jnp.where(lane_block == a, moved, out)
        outs.append(out)
    return outs


def pair_weights(wpair_ref, per):
    channels = wpair_ref.shape[1]
    high, wide = HEADS * per, per * channels
    row = lax.broadcasted_iota(jnp.int32, (high, HEADS), 0) // per
    head = lax.broadcasted_iota(jnp.int32, (high, HEADS), 1)
    pick = jnp.where(row == head, 1.0, 0.0).astype(BF16)
    by_row = mm(pick, wpair_ref[...]).astype(BF16)
    lane = lax.rem(lax.broadcasted_iota(jnp.int32, (channels, wide), 1), channels)
    chan = lax.broadcasted_iota(jnp.int32, (channels, wide), 0)
    spread = mm(by_row, jnp.where(lane == chan, 1.0, 0.0).astype(BF16))
    key = lax.rem(lax.broadcasted_iota(jnp.int32, (high, wide), 0), per)
    spot = lax.broadcasted_iota(jnp.int32, (high, wide), 1) // channels
    return jnp.where(key == spot, spread, 0.0).astype(BF16)


def build_bias(counts_ref, pair_ref, wsm, bias_scr, blocks, rows):
    pos = lax.axis_index("seq")
    size = lax.axis_size("seq")
    own = counts_ref[pos]
    left = jnp.where(pos > 0, counts_ref[jnp.maximum(pos - 1, 0)], 0)
    right = jnp.where(pos < size - 1, counts_ref[jnp.minimum(pos + 1, size - 1)], 0)
    rim = (KWIN - QBLK) // 2
    lane_block = head_lanes(LANES)
    chunk = wsm.shape[1]
    per = wsm.shape[0] // HEADS
    for kk in range(pair_ref.shape[1] // chunk):
        biased = mm(wsm, pair_ref[:, kk * chunk : (kk + 1) * chunk], NT)
        for g in range(blocks // GROUP):
            parts = [
                biased[h * per : (h + 1) * per, g * LANES : (g + 1) * LANES] for h in range(HEADS)
            ]
            for w, out in enumerate(lane_swap(parts, lane_block)):
                b = g * GROUP + w
                slot = (
                    lax.broadcasted_iota(jnp.int32, (per, LANES), 0) + kk * per + b * QBLK - rim
                )
                alive = (
                    ((slot < 0) & (slot + rows < left))
                    | ((slot >= 0) & (slot < own))
                    | ((slot >= rows) & (slot - rows < right))
                )
                bias_scr[b, kk * per : (kk + 1) * per, :] = jnp.where(alive, out * LOG2E, -1e30)


def pair_gradient(pair_ref, score_scr, per, chunk, blocks):
    lane_block = head_lanes(LANES)
    total = None
    for kk in range(pair_ref.shape[1] // chunk):
        columns = []
        for g in range(blocks // GROUP):
            parts = [score_scr[g * GROUP + w, kk * per : (kk + 1) * per, :] for w in range(GROUP)]
            columns.append(jnp.concatenate(lane_swap(parts, lane_block), axis=0))
        grads = jnp.concatenate(columns, axis=1).astype(BF16)
        part = mm(grads, pair_ref[:, kk * chunk : (kk + 1) * chunk])
        total = part if total is None else total + part
    high, wide = total.shape
    row = lax.broadcasted_iota(jnp.int32, (high, wide), 0)
    lane = lax.broadcasted_iota(jnp.int32, (high, wide), 1)
    diagonal = jnp.where(lax.rem(row, per) == lane // (wide // per), total, 0.0)
    lines = []
    for h in range(HEADS):
        line = jnp.sum(diagonal[h * per : (h + 1) * per], axis=0, keepdims=True)
        folded = line[:, :LANES]
        for n in range(1, wide // LANES):
            folded = folded + line[:, n * LANES : (n + 1) * LANES]
        lines.append(folded)
    return lines


def weave(*lists):
    lists = [x for x in lists if x]
    done = [0] * len(lists)
    while True:
        best = None
        for n, x in enumerate(lists):
            if done[n] < len(x):
                share = (done[n] + 0.5) / len(x)
                if best is None or share < best[0]:
                    best = (share, n)
        if best is None:
            return
        n = best[1]
        lists[n][done[n]]()
        done[n] += 1


def axis_sizes():
    return [(axis, lax.axis_size(axis)) for axis in ("samp", "seq")]


def shifted_index(axis, size, distance):
    return lax.rem(lax.axis_index(axis) + distance, size)


class Summer:
    def __init__(self, buf, out, streams, orders, send_sem, recv_sem, slots):
        self.buf, self.out, self.streams, self.orders = buf, out, streams, orders
        self.send_sem, self.recv_sem = send_sem, recv_sem
        self.sends, self.recvs = slots[: 2 * streams], slots[2 * streams :]
        self.unit = buf.shape[0] // streams
        self.peers = sum(size - 1 for _, size in orders[0])

    def spans(self, stream):
        (a0, s0), (a1, s1) = self.orders[stream]
        off0 = stream * self.unit
        len1 = self.unit // s0
        len2 = len1 // s1
        off1 = off0 + lax.axis_index(a0) * len1
        off2 = off1 + lax.axis_index(a1) * len2
        return [(off0, self.unit), (off1, len1), (off2, len2)]

    def copy(self, stream, src, dst, slot, partner):
        at = stream * 2 * self.peers + slot
        return pltpu.make_async_remote_copy(
            src_ref=src,
            dst_ref=dst,
            send_sem=self.send_sem.at[at],
            recv_sem=self.recv_sem.at[at],
            device_id=partner,
            device_id_type=MESH,
        )

    def scatter_copies(self, stream, k):
        axis, size = self.orders[stream][k]
        base = 0 if k == 0 else self.orders[stream][0][1] - 1
        return [
            self.copy(
                stream,
                self.sends[2 * stream + k].at[d - 1],
                self.recvs[2 * stream + k].at[d - 1],
                base + d - 1,
                {axis: shifted_index(axis, size, d)},
            )
            for d in range(1, size)
        ]

    def gather_copies(self, stream, k):
        axis, size = self.orders[stream][k]
        base = self.peers + (0 if k == 1 else self.orders[stream][1][1] - 1)
        off, length = self.spans(stream)[k + 1]
        part = self.out.at[pl.ds(pl.multiple_of(off, 16), length), :]
        return [
            self.copy(stream, part, part, base + d - 1, {axis: shifted_index(axis, size, d)})
            for d in range(1, size)
        ]

    def scatter(self, k):
        for stream in range(self.streams):
            spans = self.spans(stream)
            axis, size = self.orders[stream][k]
            if k > 0:
                off, length = spans[k]
                rows = pl.ds(pl.multiple_of(off, 16), length)
                self.buf[rows, :] = self.absorbed(stream, k - 1)
            off, length = spans[k][0], spans[k + 1][1]
            for d, copy in enumerate(self.scatter_copies(stream, k), 1):
                give = pl.multiple_of(off + shifted_index(axis, size, d) * length, 16)
                self.sends[2 * stream + k][d - 1] = self.buf[pl.ds(give, length), :].astype(BF16)
                copy.start()

    def absorbed(self, stream, k):
        off, length = self.spans(stream)[k + 1]
        value = self.buf[pl.ds(pl.multiple_of(off, 16), length), :]
        for n, copy in enumerate(self.scatter_copies(stream, k)):
            copy.wait()
            value = value + self.recvs[2 * stream + k][n].astype(F32)
        return value

    def gather(self, k):
        for stream in range(self.streams):
            if k == 1:
                off, length = self.spans(stream)[2]
                rows = pl.ds(pl.multiple_of(off, 16), length)
                self.out[rows, :] = self.absorbed(stream, 1).astype(BF16)
            else:
                for copy in self.gather_copies(stream, 1):
                    copy.wait()
            for copy in self.gather_copies(stream, k):
                copy.start()

    def finish(self):
        for stream in range(self.streams):
            for copy in self.gather_copies(stream, 0):
                copy.wait()

    def actions(self):
        return [
            lambda: self.scatter(0),
            lambda: self.scatter(1),
            lambda: self.gather(1),
            lambda: self.gather(0),
            self.finish,
        ]


def step_kernel(
    samples,
    early_streams,
    late_streams,
    counts_ref,
    atoms_hbm,
    atoms_ref,
    again_ref,
    gain_ref,
    wq_ref,
    wk_ref,
    wv_ref,
    wg_ref,
    wo_ref,
    wt_ref,
    wpair_ref,
    pair_ref,
    ids_ref,
    cot_ref,
    pooled_ref,
    gatoms_ref,
    early_ref,
    late_ref,
    small_ref,
    low_in,
    high_in,
    edge_out,
    edge_in,
    bias_scr,
    score_scr,
    member_scr,
    member_t_scr,
    inv_scr,
    wqg_scr,
    wkv_scr,
    wall_scr,
    hid_all,
    gate_scr,
    gated_scr,
    back_scr,
    q_all,
    kv_all,
    low_all,
    gatt_all,
    gupd_all,
    d_all,
    gout_scr,
    gtok_scr,
    gw_scr,
    early_buf,
    late_buf,
    early_sum,
    late_sum,
    small_a,
    small_b,
    small_src,
    halo_send,
    halo_recv,
    edge_send,
    edge_recv,
    early_send,
    early_recv,
    late_send,
    late_recv,
    small_send,
    small_recv,
    *slots,
):
    step = pl.program_id(0)
    rows, width = q_all.shape[1:]
    blocks = rows // QBLK
    rim = (KWIN - QBLK) // 2
    tokens = inv_scr.shape[0]
    per = 2 * LANES // wpair_ref.shape[1]
    pair_chunk = per * wpair_ref.shape[1]
    scaling = (width // HEADS) ** (-0.5)
    lane_head = head_lanes(width)
    masks = [(lane_head == h).astype(F32).astype(BF16) for h in range(HEADS)]
    axes = axis_sizes()
    pos = lax.axis_index("seq")
    size = lax.axis_size("seq")
    last = 3 * samples - 1

    early_orders = [axes[::-1] if s % 2 == 1 else axes for s in range(early_streams)]
    early = Summer(
        early_buf,
        early_sum,
        early_streams,
        early_orders,
        early_send,
        early_recv,
        slots[: 4 * early_streams],
    )
    late = Summer(
        late_buf,
        late_sum,
        late_streams,
        [axes] * late_streams,
        late_send,
        late_recv,
        slots[4 * early_streams :],
    )

    def to_right(src, dst, send_sem, recv_sem):
        return pltpu.make_async_remote_copy(
            src_ref=src,
            dst_ref=dst,
            send_sem=send_sem,
            recv_sem=recv_sem,
            device_id={"seq": jnp.minimum(pos + 1, size - 1)},
            device_id_type=MESH,
        )

    def to_left(src, dst, send_sem, recv_sem):
        return pltpu.make_async_remote_copy(
            src_ref=src,
            dst_ref=dst,
            send_sem=send_sem,
            recv_sem=recv_sem,
            device_id={"seq": jnp.maximum(pos - 1, 0)},
            device_id_type=MESH,
        )

    def halo(part):
        span = pl.ds(0, 1) if part == 0 else pl.ds(1, samples - 1)
        right = to_right(
            atoms_hbm.at[span, rows - rim : rows, :],
            low_in.at[span],
            halo_send.at[0, part],
            halo_recv.at[0, part],
        )
        left = to_left(
            atoms_hbm.at[span, 0:rim, :],
            high_in.at[span],
            halo_send.at[1, part],
            halo_recv.at[1, part],
        )
        return right, left

    def edges(j):
        right = to_right(
            edge_out.at[1, j], edge_in.at[0, j], edge_send.at[0, j], edge_recv.at[0, j]
        )
        left = to_left(
            edge_out.at[0, j], edge_in.at[1, j], edge_send.at[1, j], edge_recv.at[1, j]
        )
        return right, left

    def launch(pair):
        right, left = pair

        @pl.when(pos < size - 1)
        def _():
            right.start()

        @pl.when(pos > 0)
        def _():
            left.start()

    def collect(pair):
        right, left = pair

        @pl.when(pos < size - 1)
        def _():
            right.wait_send()
            left.wait_recv()

        @pl.when(pos > 0)
        def _():
            left.wait_send()
            right.wait_recv()

    def forward_stages(s):
        slot = lax.rem(s, 2)
        gain = gain_ref[...]
        stages = []
        held = {}
        cuts = 4
        chunk = rows // cuts

        def rims():
            hid_all[s, :rim] = layer_norm(low_in[s].astype(F32), gain)[2]
            hid_all[s, rim + rows :] = layer_norm(high_in[s].astype(F32), gain)[2]
            kv_all[s, :rim] = mm(hid_all[s, :rim], wkv_scr[...]).astype(BF16)
            kv_all[s, rim + rows :] = mm(hid_all[s, rim + rows :], wkv_scr[...]).astype(BF16)

        def norm(c):
            def run():
                x = atoms_ref[0, c * chunk : (c + 1) * chunk].astype(F32)
                hid_all[s, rim + c * chunk : rim + (c + 1) * chunk] = layer_norm(x, gain)[2]

            return run

        def project(c):
            def run():
                span = slice(c * chunk, (c + 1) * chunk)
                hidden = hid_all[s, rim + c * chunk : rim + (c + 1) * chunk]
                kv_all[s, rim + c * chunk : rim + (c + 1) * chunk] = mm(
                    hidden, wkv_scr[...]
                ).astype(BF16)
                qg = mm(hidden, wqg_scr[...])
                q_all[s, span] = qg[:, :width].astype(BF16)
                gate_scr[span] = sigmoid(qg[:, width:])

            return run

        def score(g, spans):
            def run():
                q_exp = [expand(q_all[s, b * QBLK : (b + 1) * QBLK, :], masks) for b in spans]
                held[g] = [
                    mm(kv_all[s, b * QBLK : b * QBLK + KWIN, :width], q, NT)
                    for b, q in zip(spans, q_exp)
                ]

            return run

        def soften(g, spans):
            def run():
                es = [
                    jnp.exp2(sc * (scaling * LOG2E) + bias_scr[b])
                    for b, sc in zip(spans, held.pop(g))
                ]
                invs = [1.0 / jnp.sum(e, axis=0, keepdims=True) for e in es]
                for b, e, inv in zip(spans, es, invs):
                    low_all[s, b] = (e * inv).astype(BF16)

            return run

        def attend(spans):
            def run():
                wide = [
                    mm(low_all[s, b], kv_all[s, b * QBLK : b * QBLK + KWIN, width:], TN)
                    for b in spans
                ]
                for b, o in zip(spans, wide):
                    span = slice(b * QBLK, (b + 1) * QBLK)
                    att = collapse(o, lane_head)
                    gate = gate_scr[span]
                    gated = gate * att
                    gated_scr[slot, span] = gated.astype(BF16)
                    back_scr[slot, 0, span] = gate
                    back_scr[slot, 1, span] = gated * (1.0 - gate)

            return run

        stages.append(rims)
        stages.append(norm(0))
        for c in range(cuts):
            if c + 1 < cuts:
                stages.append(norm(c + 1))
            stages.append(project(c))
        groups = [[g * FGROUP + w for w in range(FGROUP)] for g in range(blocks // FGROUP)]
        count = len(groups)
        for g in range(count + 2):
            if g < count:
                stages.append(score(g, groups[g]))
            if 0 <= g - 1 < count:
                stages.append(soften(g - 1, groups[g - 1]))
            if 0 <= g - 2 < count:
                stages.append(attend(groups[g - 2]))
        return stages

    def token_stages(s):
        slot = lax.rem(s, 2)
        chunk = 256
        half = rows // 2
        held = {}
        stages = []

        def begin():
            gated = gated_scr[slot]
            x = again_ref[0].astype(F32)
            held["updated"] = (x + mm(gated, wo_ref[...])).astype(BF16)
            held["cot"] = (cot_ref[0].astype(F32) * inv_scr[...]).astype(BF16)
            held["gupd"] = [None, None]

        def enter(c, r):
            def run():
                cols = slice(c * chunk, (c + 1) * chunk)
                span = slice(r * half, (r + 1) * half)
                held[c, r] = (
                    mm(held["updated"][span], wt_ref[:, cols]),
                    mm(member_scr[span, :], held["cot"][:, cols]),
                    [],
                    [],
                )

            return run

        def act(c, r, n):
            def run():
                pre, grad_act, acts, grads = held[c, r]
                part = slice(n * half // PARTS, (n + 1) * half // PARTS)
                pre, grad_act = pre[part], grad_act[part]
                sig = sigmoid(pre)
                value = pre * sig
                acts.append(value.astype(BF16))
                grads.append((grad_act * (sig + value * (1.0 - sig))).astype(BF16))

            return run

        def leave(c, r):
            def run():
                _, _, acts, grads = held.pop((c, r))
                cols = slice(c * chunk, (c + 1) * chunk)
                span = slice(r * half, (r + 1) * half)
                grad_pre = jnp.concatenate(grads, axis=0)
                pooled = mm(member_t_scr[:, span], jnp.concatenate(acts, axis=0))
                gtok = mm(held["updated"][span], grad_pre, TN)
                part = mm(grad_pre, wt_ref[:, cols], NT)
                if r == 0:
                    held["pooled"], held["gtok"] = pooled, gtok
                else:
                    pooled_ref[0, :, cols] = ((held["pooled"] + pooled) * inv_scr[...]).astype(BF16)
                    gtok_scr[:, cols] += held["gtok"] + gtok
                before = held["gupd"][r]
                held["gupd"][r] = part if before is None else before + part

            return run

        def end():
            grad_updated = jnp.concatenate(held["gupd"], axis=0).astype(BF16)
            gupd_all[s] = grad_updated
            gout_scr[...] += mm(gated_scr[slot], grad_updated, TN)
            grad_gated = mm(grad_updated, wo_ref[...], NT)
            gatt_all[s] = (grad_gated * back_scr[slot, 0]).astype(BF16)
            d_all[s, :, 3 * width :] = (grad_gated * back_scr[slot, 1]).astype(BF16)

        stages.append(begin)
        pieces = [(c, r) for c in range(wt_ref.shape[1] // chunk) for r in range(2)]
        for n in range(len(pieces) + 1):
            if n < len(pieces):
                stages.append(enter(*pieces[n]))
            if n > 0:
                for part in range(PARTS):
                    stages.append(act(*pieces[n - 1], part))
                stages.append(leave(*pieces[n - 1]))
        stages.append(end)
        return stages

    def backward_stages(s):
        open_k = []
        open_v = []
        held = {}
        stages = []

        def tiles(x):
            return [x[n * QBLK : (n + 1) * QBLK] for n in range(KWIN // QBLK)]

        def store(at, k, v):
            if at < rim:
                edge_out[0, s, at : at + k.shape[0], :width] = k
                edge_out[0, s, at : at + k.shape[0], width:] = v
            elif at < rim + rows:
                d_all[s, at - rim : at - rim + k.shape[0], width : 2 * width] = k
                d_all[s, at - rim : at - rim + k.shape[0], 2 * width : 3 * width] = v
            else:
                at = at - rim - rows
                edge_out[1, s, at : at + k.shape[0], :width] = k
                edge_out[1, s, at : at + k.shape[0], width:] = v

        def close(first, count):
            for n in range(count):
                at = (first + n) * QBLK
                k = (open_k[n] * scaling).astype(BF16)
                v = open_v[n].astype(BF16)
                half = QBLK // 2
                store(at, k[:half], v[:half])
                store(at + half, k[half:], v[half:])
            del open_k[:count]
            del open_v[:count]

        def merge(opened, parts):
            for n, part in enumerate(parts):
                if n < len(opened):
                    opened[n] = opened[n] + part
                else:
                    opened.append(part)

        def grads(g, spans):
            def run():
                ges = [expand(gatt_all[s, b * QBLK : (b + 1) * QBLK, :], masks) for b in spans]
                gps = [
                    mm(kv_all[s, b * QBLK : b * QBLK + KWIN, width:], ge, NT)
                    for b, ge in zip(spans, ges)
                ]
                ps = [low_all[s, b].astype(F32) for b in spans]
                ts = [p * gp for p, gp in zip(ps, gps)]
                sums = [jnp.sum(t, axis=0, keepdims=True) for t in ts]
                dss = [t - p * total for p, t, total in zip(ps, ts, sums)]
                for b, ds in zip(spans, dss):
                    score_scr[b] += ds
                held[g] = [ds.astype(BF16) for ds in dss]
                held[g, "dv"] = [mm(low_all[s, b], ge) for b, ge in zip(spans, ges)]

            return run

        def products(g, spans):
            def run():
                lows = held.pop(g)
                dvs = held.pop((g, "dv"))
                q_exp = [expand(q_all[s, b * QBLK : (b + 1) * QBLK, :], masks) for b in spans]
                dks = [mm(low, q) for low, q in zip(lows, q_exp)]
                dqs = [
                    mm(low, kv_all[s, b * QBLK : b * QBLK + KWIN, :width], TN)
                    for b, low in zip(spans, lows)
                ]
                for b, dk, dv in zip(spans, dks, dvs):
                    merge(open_k, tiles(dk))
                    merge(open_v, tiles(dv))
                    close(b, 1)
                for b, dq in zip(spans, dqs):
                    d_all[s, b * QBLK : (b + 1) * QBLK, :width] = (
                        collapse(dq, lane_head) * scaling
                    ).astype(BF16)

            return run

        group = 2
        groups = [[g * group + w for w in range(group)] for g in range(blocks // group)]
        stages.append(grads(0, groups[0]))
        for g in range(len(groups)):
            if g + 1 < len(groups):
                stages.append(grads(g + 1, groups[g + 1]))
            stages.append(products(g, groups[g]))
        stages.append(lambda: close(blocks, len(open_k)))
        return stages

    def weight_stages(s):
        cuts = 2
        chunk = rows // cuts

        def join():
            for side, at in ((0, 0), (1, rows - rim)):
                d_all[s, at : at + rim, width : 3 * width] = (
                    d_all[s, at : at + rim, width : 3 * width].astype(F32)
                    + edge_in[side, s].astype(F32)
                ).astype(BF16)

        def multiply(c):
            def run():
                hidden = hid_all[s, rim + c * chunk : rim + (c + 1) * chunk]
                gw_scr[...] += mm(hidden, d_all[s, c * chunk : (c + 1) * chunk], TN)

            return run

        return [join] + [multiply(c) for c in range(cuts)]

    def finish_stages(s):
        gain = gain_ref[...]
        stages = []
        cuts = 2
        chunk = rows // cuts
        held = {}

        def norm(c):
            def run():
                held[c] = layer_norm(again_ref[0, c * chunk : (c + 1) * chunk].astype(F32), gain)

            return run

        def multiply(c):
            def run():
                held["gh", c] = mm(d_all[s, c * chunk : (c + 1) * chunk], wall_scr[...], NT)

            return run

        def finish(c):
            def run():
                normed, inv_std, _ = held[c]
                gx = held["gh", c] * gain
                grad_ln = inv_std * (
                    gx
                    - jnp.mean(gx, axis=-1, keepdims=True)
                    - normed * jnp.mean(gx * normed, axis=-1, keepdims=True)
                )
                span = slice(c * chunk, (c + 1) * chunk)
                gatoms_ref[0, span] = (gupd_all[s, span].astype(F32) + grad_ln).astype(BF16)

            return run

        for c in range(cuts):
            stages += [norm(c), multiply(c)]
        for c in range(cuts):
            stages.append(finish(c))
        return stages

    @pl.when(step == 0)
    def _():
        barrier = pltpu.get_barrier_semaphore()
        for axis, count in axes:
            for d in range(1, count):
                pl.semaphore_signal(
                    barrier,
                    inc=1,
                    device_id={axis: shifted_index(axis, count, d)},
                    device_id_type=MESH,
                )

        @pl.when(pos == 0)
        def _():
            low_in[...] = jnp.zeros_like(low_in)
            edge_in[0] = jnp.zeros_like(edge_in[0])

        @pl.when(pos == size - 1)
        def _():
            high_in[...] = jnp.zeros_like(high_in)
            edge_in[1] = jnp.zeros_like(edge_in[1])

        pl.semaphore_wait(barrier, sum(count - 1 for _, count in axes))
        for part in range(2):
            launch(halo(part))
        build_bias(
            counts_ref, pair_ref, pair_weights(wpair_ref, per), bias_scr, blocks, rows
        )
        token = lax.broadcasted_iota(jnp.int32, (tokens, rows), 0)
        place = lax.broadcasted_iota(jnp.int32, (tokens, rows), 1)
        hit = (ids_ref[...] - pos * tokens == token) & (place < counts_ref[pos])
        member_t = jnp.where(hit, 1.0, 0.0).astype(F32)
        inv_scr[...] = 1.0 / jnp.sum(member_t, axis=1, keepdims=True)
        member_t_scr[...] = member_t.astype(BF16)
        member_scr[...] = member_t.T.astype(BF16)
        wqg_scr[:, :width] = wq_ref[...]
        wqg_scr[:, width:] = wg_ref[...]
        wkv_scr[:, :width] = wk_ref[...]
        wkv_scr[:, width:] = wv_ref[...]
        for n, ref in enumerate((wq_ref, wk_ref, wv_ref, wg_ref)):
            wall_scr[:, n * width : (n + 1) * width] = ref[...]
        for ref in (score_scr, gout_scr, gtok_scr, gw_scr):
            ref[...] = jnp.zeros_like(ref)
        collect(halo(0))
        weave(forward_stages(0))
        collect(halo(1))

    @pl.when((step > 0) & (step < samples))
    def _():
        weave(token_stages(step - 1), forward_stages(step))

    @pl.when(step == samples)
    def _():
        weave(token_stages(samples - 1), backward_stages(0))

    @pl.when((step > samples) & (step < samples + LAG))
    def _():
        weave(backward_stages(step - samples))

    @pl.when((step >= samples + LAG) & (step < 2 * samples))
    def _():
        collect(edges(step - samples - LAG))
        weave(weight_stages(step - samples - LAG), backward_stages(step - samples))

    @pl.when((step >= samples) & (step < 2 * samples))
    def _():
        launch(edges(step - samples))

    @pl.when(step >= 2 * samples)
    def _():
        weave(finish_stages(step - 2 * samples))

    @pl.when(step == 2 * samples)
    def _():
        lines = pair_gradient(pair_ref, score_scr, per, pair_chunk, blocks)
        for n, line in enumerate(lines):
            small_src[0, n : n + 1, :] = line
        small_src[0, HEADS:, :] = jnp.zeros((8 - HEADS, width), F32)

    def fill_early():
        for n in range(gtok_scr.shape[1] // width):
            early_buf[n * width : (n + 1) * width, :] = gtok_scr[:, n * width : (n + 1) * width]
        at = gtok_scr.shape[1]
        early_buf[at : at + width, :] = gout_scr[...]
        early_buf[at + width :, :] = jnp.zeros((early_buf.shape[0] - at - width, width), F32)

    for n, action in enumerate(early.actions()):

        def run(n=n, action=action):
            if n == 0:
                fill_early()
            action()

        pl.when(step == min(samples + 1 + 2 * n, last))(run)

    def small_copies(k):
        axis, count = axes[k]
        base = 0 if k == 0 else axes[0][1] - 1
        return [
            pltpu.make_async_remote_copy(
                src_ref=small_src.at[k],
                dst_ref=(small_a, small_b)[k].at[d - 1],
                send_sem=small_send.at[base + d - 1],
                recv_sem=small_recv.at[base + d - 1],
                device_id={axis: shifted_index(axis, count, d)},
                device_id_type=MESH,
            )
            for d in range(1, count)
        ]

    def small_total(k):
        value = small_src[k]
        for n, copy in enumerate(small_copies(k)):
            copy.wait()
            value = value + (small_a, small_b)[k][n]
        return value

    def late_start():
        for s in range(samples - LAG, samples):
            collect(edges(s))
            weave(weight_stages(s))
        for n in range(4):
            late_buf[n * width : (n + 1) * width, :] = gw_scr[:, n * width : (n + 1) * width]
        if late_buf.shape[0] > 4 * width:
            late_buf[4 * width :, :] = jnp.zeros((late_buf.shape[0] - 4 * width, width), F32)
        late.scatter(0)
        for copy in small_copies(0):
            copy.start()

    def late_second():
        late.scatter(1)
        small_src[1] = small_total(0)
        for copy in small_copies(1):
            copy.start()

    def late_third():
        late.gather(1)
        small_ref[...] = small_total(1)

    def late_end():
        late.finish()
        early_ref[...] = early_sum[...]
        late_ref[...] = late_sum[...]

    late_actions = [late_start, late_second, late_third, lambda: late.gather(0), late_end]
    for n, action in enumerate(late_actions):
        at = last if n == len(late_actions) - 1 else min(2 * samples + 2 + 2 * n, last)
        pl.when(step == at)(action)


def unpack_kernel(
    channels,
    early_ref,
    late_ref,
    small_ref,
    gain_ref,
    wq_ref,
    wk_ref,
    wv_ref,
    wg_ref,
    ggain_out,
    gq_out,
    gk_out,
    gv_out,
    gg_out,
    gout_out,
    gtok_out,
    gpair_out,
):
    width = gout_out.shape[0]
    blocks = gtok_out.shape[1] // width

    def block(ref, n):
        return ref[n * width : (n + 1) * width, :].astype(F32)

    for n in range(blocks):
        gtok_out[:, n * width : (n + 1) * width] = block(early_ref, n)
    gout_out[...] = block(early_ref, blocks)
    by_gain = None
    weights = (wq_ref, wk_ref, wv_ref, wg_ref)
    for n, (ref, weight) in enumerate(zip((gq_out, gk_out, gv_out, gg_out), weights)):
        grad = block(late_ref, n)
        ref[...] = grad
        part = grad * weight[...].astype(F32)
        by_gain = part if by_gain is None else by_gain + part
    ggain_out[...] = jnp.sum(by_gain.T, axis=0, keepdims=True) / gain_ref[...]
    lines = small_ref[...]
    shift = width // 2
    while shift >= channels:
        lines = lines + pltpu.roll(lines, shift, 1)
        shift //= 2
    gpair_out[...] = lines[:HEADS, :channels]


def whole(*shape):
    return pl.BlockSpec(shape, lambda s: (0,) * len(shape))


def sum_scratch(total, streams, orders, width):
    unit = total // streams
    slots = []
    for stream in range(streams):
        length = unit
        for _, size in orders[stream]:
            length //= size
            slots.append(pltpu.VMEM((size - 1, length, width), BF16))
    return slots * 2


def on_device(
    atoms,
    gain,
    w_query,
    w_key,
    w_value,
    w_gate,
    w_out,
    w_token,
    w_pair,
    pair_cond,
    counts,
    membership,
    pooled_cot,
):
    samples, rows, width = atoms.shape
    blocks = rows // QBLK
    rim = (KWIN - QBLK) // 2
    tokens, token_width = pooled_cot.shape[1:]
    channels = w_pair.shape[0]
    pair2 = pair_cond.reshape(blocks * QBLK, pair_cond.shape[-1])
    gain2 = gain.reshape(1, width)
    ids2 = membership.reshape(1, rows)
    square = whole(width, width)
    shape = jax.ShapeDtypeStruct
    vmem = pltpu.VMEM
    dma = pltpu.SemaphoreType.DMA

    axes = axis_sizes()
    devices = axes[0][1] * axes[1][1]
    peers = sum(size - 1 for _, size in axes)
    unit = 16 * devices
    early_total = -(-(token_width + width) // unit) * unit
    late_total = -(-(4 * width) // unit) * unit
    early_streams = early_total // unit
    late_streams = late_total // unit
    early_orders = [axes[::-1] if s % 2 == 1 else axes for s in range(early_streams)]

    def clip(x):
        return jnp.clip(x, 0, samples - 1)

    def again(i):
        return jnp.where(i <= samples, clip(i - 1), clip(i - 2 * samples))

    pooled, gatoms, early, late, small = pl.pallas_call(
        functools.partial(step_kernel, samples, early_streams, late_streams),
        grid=(3 * samples,),
        in_specs=[
            pl.BlockSpec(memory_space=pltpu.SMEM),
            pl.BlockSpec(memory_space=pl.ANY),
            pl.BlockSpec((1, rows, width), lambda i: (clip(i), 0, 0)),
            pl.BlockSpec((1, rows, width), lambda i: (again(i), 0, 0)),
            whole(1, width),
            square,
            square,
            square,
            square,
            square,
            whole(width, token_width),
            whole(*w_pair.T.shape),
            whole(*pair2.shape),
            whole(1, rows),
            pl.BlockSpec((1, tokens, token_width), lambda i: (clip(i - 1), 0, 0)),
        ],
        out_specs=[
            pl.BlockSpec((1, tokens, token_width), lambda i: (clip(i - 1), 0, 0)),
            pl.BlockSpec((1, rows, width), lambda i: (clip(i - 2 * samples), 0, 0)),
            whole(early_total, width),
            whole(late_total, width),
            whole(8, width),
        ],
        out_shape=[
            shape((samples, tokens, token_width), BF16),
            shape((samples, rows, width), BF16),
            shape((early_total, width), BF16),
            shape((late_total, width), BF16),
            shape((8, width), F32),
        ],
        scratch_shapes=[
            vmem((samples, rim, width), BF16),
            vmem((samples, rim, width), BF16),
            vmem((2, samples, rim, 2 * width), BF16),
            vmem((2, samples, rim, 2 * width), BF16),
            vmem((blocks, KWIN, LANES), F32),
            vmem((blocks, KWIN, LANES), F32),
            vmem((rows, tokens), BF16),
            vmem((tokens, rows), BF16),
            vmem((tokens, 1), F32),
            vmem((width, 2 * width), BF16),
            vmem((width, 2 * width), BF16),
            vmem((width, 4 * width), BF16),
            vmem((samples, rows + 2 * rim, width), BF16),
            vmem((rows, width), F32),
            vmem((2, rows, width), BF16),
            vmem((2, 2, rows, width), F32),
            vmem((samples, rows, width), BF16),
            vmem((samples, rows + 2 * rim, 2 * width), BF16),
            vmem((samples, blocks, KWIN, LANES), BF16),
            vmem((samples, rows, width), BF16),
            vmem((samples, rows, width), BF16),
            vmem((samples, rows, 4 * width), BF16),
            vmem((width, width), F32),
            vmem((width, token_width), F32),
            vmem((width, 4 * width), F32),
            vmem((early_total, width), F32),
            vmem((late_total, width), F32),
            vmem((early_total, width), BF16),
            vmem((late_total, width), BF16),
            vmem((axes[0][1] - 1, 8, width), F32),
            vmem((axes[1][1] - 1, 8, width), F32),
            vmem((2, 8, width), F32),
            dma((2, 2)),
            dma((2, 2)),
            dma((2, samples)),
            dma((2, samples)),
            dma((2 * early_streams * peers,)),
            dma((2 * early_streams * peers,)),
            dma((2 * late_streams * peers,)),
            dma((2 * late_streams * peers,)),
            dma((peers,)),
            dma((peers,)),
        ]
        + sum_scratch(early_total, early_streams, early_orders, width)
        + sum_scratch(late_total, late_streams, [axes] * late_streams, width),
        compiler_params=pltpu.CompilerParams(
            dimension_semantics=("arbitrary",),
            vmem_limit_bytes=56 * 1024 * 1024,
            collective_id=0,
            has_side_effects=True,
        ),
    )(
        counts,
        atoms,
        atoms,
        atoms,
        gain2,
        w_query,
        w_key,
        w_value,
        w_gate,
        w_out,
        w_token,
        w_pair.T,
        pair2,
        ids2,
        pooled_cot,
    )
    spec = pl.BlockSpec(memory_space=pltpu.VMEM)
    ggain, gq, gk, gv, gg, gout, gtok, gpair = pl.pallas_call(
        functools.partial(unpack_kernel, channels),
        in_specs=[spec] * 8,
        out_specs=[spec] * 8,
        out_shape=[shape((1, width), F32)]
        + [shape((width, width), F32)] * 5
        + [shape((width, token_width), F32), shape((HEADS, channels), F32)],
    )(early, late, small, gain2, w_query, w_key, w_value, w_gate)
    return (pooled, gatoms, ggain.reshape(width), gq, gk, gv, gg, gout, gtok, gpair.T)


def solution(mesh):
    placed = (
        P("samp", "seq", None),
        P(),
        P(),
        P(),
        P(),
        P(),
        P(),
        P(),
        P(),
        P("seq", None, None),
        P(),
        P("seq"),
        P("samp", "seq", None),
    )
    return jax.shard_map(
        on_device,
        mesh=mesh,
        in_specs=placed,
        out_specs=(
            P("samp", "seq", None),
            P("samp", "seq", None),
            P(),
            P(),
            P(),
            P(),
            P(),
            P(),
            P(),
            P(),
        ),
        check_vma=False,
    )
```

```python
import functools

import jax
import jax.numpy as jnp
from jax import lax
from jax.experimental import pallas as pl
from jax.experimental.pallas import tpu as pltpu
from jax.sharding import PartitionSpec as P

HEADS = 4
QBLK = 32
KWIN = 128
LOG2E = 1.4426950408889634

epsilon = 1e-05
F32 = jnp.float32
BF16 = jnp.bfloat16
NN = (((1,), (0,)), ((), ()))
NT = (((1,), (1,)), ((), ()))
TN = (((0,), (0,)), ((), ()))
GROUP = 4
FGROUP = 8
PARTS = 2
BGROUP = 8
LANES = 128
MESH = pl.DeviceIdType.MESH
LAG = 3
EARLY_AT = (1, 4, 8, 12, 1 << 20)
LATE_AT = (2, 5, 7, 9, 1 << 20)


def mm(a, b, dims=NN):
    return lax.dot_general(a, b, dims, preferred_element_type=F32)


def sigmoid(x):
    return 0.5 * jnp.tanh(0.5 * x) + 0.5


def layer_norm(x, gain):
    centred = x - jnp.mean(x, axis=-1, keepdims=True)
    variance = jnp.mean(centred * centred, axis=-1, keepdims=True)
    inv_std = lax.rsqrt(variance + epsilon)
    normed = centred * inv_std
    return normed, inv_std, (normed * gain).astype(BF16)


def head_lanes(width):
    lane = lax.broadcasted_iota(jnp.int32, (1, width), 1)
    return lane // (width // HEADS)


def expand(block, masks):
    return jnp.concatenate([block * m for m in masks], axis=0)


def collapse(wide, lane_head):
    rows = wide.shape[0] // HEADS
    out = wide[:rows]
    for h in range(1, HEADS):
        out = jnp.where(lane_head == h, wide[h * rows : (h + 1) * rows], out)
    return out


def lane_swap(parts, lane_block):
    count = len(parts)
    outs = []
    for b in range(count):
        out = None
        for a in range(count):
            shift = (QBLK * (a - b)) % LANES
            moved = parts[a] if shift == 0 else pltpu.roll(parts[a], shift, 1)
            out = moved if out is None else jnp.where(lane_block == a, moved, out)
        outs.append(out)
    return outs


def pair_weights(wpair_ref, per):
    channels = wpair_ref.shape[1]
    high, wide = HEADS * per, per * channels
    row = lax.broadcasted_iota(jnp.int32, (high, HEADS), 0) // per
    head = lax.broadcasted_iota(jnp.int32, (high, HEADS), 1)
    pick = jnp.where(row == head, 1.0, 0.0).astype(BF16)
    by_row = mm(pick, wpair_ref[...]).astype(BF16)
    lane = lax.rem(lax.broadcasted_iota(jnp.int32, (channels, wide), 1), channels)
    chan = lax.broadcasted_iota(jnp.int32, (channels, wide), 0)
    spread = mm(by_row, jnp.where(lane == chan, 1.0, 0.0).astype(BF16))
    key = lax.rem(lax.broadcasted_iota(jnp.int32, (high, wide), 0), per)
    spot = lax.broadcasted_iota(jnp.int32, (high, wide), 1) // channels
    return jnp.where(key == spot, spread, 0.0).astype(BF16)


def build_bias(counts_ref, pair_ref, wsm, bias_scr, blocks, rows):
    pos = lax.axis_index("seq")
    size = lax.axis_size("seq")
    own = counts_ref[pos]
    left = jnp.where(pos > 0, counts_ref[jnp.maximum(pos - 1, 0)], 0)
    right = jnp.where(pos < size - 1, counts_ref[jnp.minimum(pos + 1, size - 1)], 0)
    rim = (KWIN - QBLK) // 2
    lane_block = head_lanes(LANES)
    chunk = wsm.shape[1]
    per = wsm.shape[0] // HEADS
    for kk in range(pair_ref.shape[1] // chunk):
        biased = mm(wsm, pair_ref[:, kk * chunk : (kk + 1) * chunk], NT)
        for g in range(blocks // GROUP):
            parts = [
                biased[h * per : (h + 1) * per, g * LANES : (g + 1) * LANES] for h in range(HEADS)
            ]
            for w, out in enumerate(lane_swap(parts, lane_block)):
                b = g * GROUP + w
                slot = (
                    lax.broadcasted_iota(jnp.int32, (per, LANES), 0) + kk * per + b * QBLK - rim
                )
                alive = (
                    ((slot < 0) & (slot + rows < left))
                    | ((slot >= 0) & (slot < own))
                    | ((slot >= rows) & (slot - rows < right))
                )
                bias_scr[b, kk * per : (kk + 1) * per, :] = jnp.where(alive, out * LOG2E, -1e30)


def pair_gradient(pair_ref, score_scr, per, chunk, blocks):
    lane_block = head_lanes(LANES)
    total = None
    for kk in range(pair_ref.shape[1] // chunk):
        columns = []
        for g in range(blocks // GROUP):
            parts = [score_scr[g * GROUP + w, kk * per : (kk + 1) * per, :] for w in range(GROUP)]
            columns.append(jnp.concatenate(lane_swap(parts, lane_block), axis=0))
        grads = jnp.concatenate(columns, axis=1).astype(BF16)
        part = mm(grads, pair_ref[:, kk * chunk : (kk + 1) * chunk])
        total = part if total is None else total + part
    high, wide = total.shape
    row = lax.broadcasted_iota(jnp.int32, (high, wide), 0)
    lane = lax.broadcasted_iota(jnp.int32, (high, wide), 1)
    diagonal = jnp.where(lax.rem(row, per) == lane // (wide // per), total, 0.0)
    lines = []
    for h in range(HEADS):
        line = jnp.sum(diagonal[h * per : (h + 1) * per], axis=0, keepdims=True)
        folded = line[:, :LANES]
        for n in range(1, wide // LANES):
            folded = folded + line[:, n * LANES : (n + 1) * LANES]
        lines.append(folded)
    return lines


def weave(*lists):
    lists = [x for x in lists if x]
    done = [0] * len(lists)
    while True:
        best = None
        for n, x in enumerate(lists):
            if done[n] < len(x):
                share = (done[n] + 0.5) / len(x)
                if best is None or share < best[0]:
                    best = (share, n)
        if best is None:
            return
        n = best[1]
        lists[n][done[n]]()
        done[n] += 1


def axis_sizes():
    return [(axis, lax.axis_size(axis)) for axis in ("samp", "seq")]


def shifted_index(axis, size, distance):
    return lax.rem(lax.axis_index(axis) + distance, size)


class Summer:
    def __init__(self, buf, out, streams, orders, send_sem, recv_sem, slots):
        self.buf, self.out, self.streams, self.orders = buf, out, streams, orders
        self.send_sem, self.recv_sem = send_sem, recv_sem
        self.sends, self.recvs = slots[: 2 * streams], slots[2 * streams :]
        self.unit = buf.shape[0] // streams
        self.peers = sum(size - 1 for _, size in orders[0])

    def spans(self, stream):
        (a0, s0), (a1, s1) = self.orders[stream]
        off0 = stream * self.unit
        len1 = self.unit // s0
        len2 = len1 // s1
        off1 = off0 + lax.axis_index(a0) * len1
        off2 = off1 + lax.axis_index(a1) * len2
        return [(off0, self.unit), (off1, len1), (off2, len2)]

    def copy(self, stream, src, dst, slot, partner):
        at = stream * 2 * self.peers + slot
        return pltpu.make_async_remote_copy(
            src_ref=src,
            dst_ref=dst,
            send_sem=self.send_sem.at[at],
            recv_sem=self.recv_sem.at[at],
            device_id=partner,
            device_id_type=MESH,
        )

    def scatter_copies(self, stream, k):
        axis, size = self.orders[stream][k]
        base = 0 if k == 0 else self.orders[stream][0][1] - 1
        return [
            self.copy(
                stream,
                self.sends[2 * stream + k].at[d - 1],
                self.recvs[2 * stream + k].at[d - 1],
                base + d - 1,
                {axis: shifted_index(axis, size, d)},
            )
            for d in range(1, size)
        ]

    def gather_copies(self, stream, k):
        axis, size = self.orders[stream][k]
        base = self.peers + (0 if k == 1 else self.orders[stream][1][1] - 1)
        off, length = self.spans(stream)[k + 1]
        part = self.out.at[pl.ds(pl.multiple_of(off, 16), length), :]
        return [
            self.copy(stream, part, part, base + d - 1, {axis: shifted_index(axis, size, d)})
            for d in range(1, size)
        ]

    def scatter(self, k):
        for stream in range(self.streams):
            spans = self.spans(stream)
            axis, size = self.orders[stream][k]
            if k > 0:
                off, length = spans[k]
                rows = pl.ds(pl.multiple_of(off, 16), length)
                self.buf[rows, :] = self.absorbed(stream, k - 1)
            off, length = spans[k][0], spans[k + 1][1]
            for d, copy in enumerate(self.scatter_copies(stream, k), 1):
                give = pl.multiple_of(off + shifted_index(axis, size, d) * length, 16)
                self.sends[2 * stream + k][d - 1] = self.buf[pl.ds(give, length), :].astype(BF16)
                copy.start()

    def absorbed(self, stream, k):
        off, length = self.spans(stream)[k + 1]
        value = self.buf[pl.ds(pl.multiple_of(off, 16), length), :]
        for n, copy in enumerate(self.scatter_copies(stream, k)):
            copy.wait()
            value = value + self.recvs[2 * stream + k][n].astype(F32)
        return value

    def gather(self, k):
        for stream in range(self.streams):
            if k == 1:
                off, length = self.spans(stream)[2]
                rows = pl.ds(pl.multiple_of(off, 16), length)
                self.out[rows, :] = self.absorbed(stream, 1).astype(BF16)
            else:
                for copy in self.gather_copies(stream, 1):
                    copy.wait()
            for copy in self.gather_copies(stream, k):
                copy.start()

    def finish(self):
        for stream in range(self.streams):
            for copy in self.gather_copies(stream, 0):
                copy.wait()

    def actions(self):
        return [
            lambda: self.scatter(0),
            lambda: self.scatter(1),
            lambda: self.gather(1),
            lambda: self.gather(0),
            self.finish,
        ]


def step_kernel(
    samples,
    early_streams,
    late_streams,
    counts_ref,
    atoms_hbm,
    atoms_ref,
    again_ref,
    gain_ref,
    wq_ref,
    wk_ref,
    wv_ref,
    wg_ref,
    wo_ref,
    wt_ref,
    wpair_ref,
    pair_ref,
    ids_ref,
    cot_ref,
    pooled_ref,
    gatoms_ref,
    early_ref,
    late_ref,
    small_ref,
    low_in,
    high_in,
    edge_out,
    edge_in,
    bias_scr,
    score_scr,
    member_scr,
    member_t_scr,
    inv_scr,
    wqg_scr,
    wkv_scr,
    wall_scr,
    hid_all,
    gate_scr,
    gated_scr,
    back_scr,
    q_all,
    kv_all,
    low_all,
    gatt_all,
    gupd_all,
    d_all,
    gout_scr,
    gtok_scr,
    gw_scr,
    early_buf,
    late_buf,
    early_sum,
    late_sum,
    small_a,
    small_b,
    small_src,
    halo_send,
    halo_recv,
    edge_send,
    edge_recv,
    early_send,
    early_recv,
    late_send,
    late_recv,
    small_send,
    small_recv,
    *slots,
):
    step = pl.program_id(0)
    rows, width = q_all.shape[1:]
    blocks = rows // QBLK
    rim = (KWIN - QBLK) // 2
    tokens = inv_scr.shape[0]
    per = 2 * LANES // wpair_ref.shape[1]
    pair_chunk = per * wpair_ref.shape[1]
    scaling = (width // HEADS) ** (-0.5)
    lane_head = head_lanes(width)
    masks = [(lane_head == h).astype(F32).astype(BF16) for h in range(HEADS)]
    axes = axis_sizes()
    pos = lax.axis_index("seq")
    size = lax.axis_size("seq")
    last = 3 * samples - 1

    early_orders = [axes] * early_streams
    early = Summer(
        early_buf,
        early_sum,
        early_streams,
        early_orders,
        early_send,
        early_recv,
        slots[: 4 * early_streams],
    )
    late = Summer(
        late_buf,
        late_sum,
        late_streams,
        [axes] * late_streams,
        late_send,
        late_recv,
        slots[4 * early_streams :],
    )

    def to_right(src, dst, send_sem, recv_sem):
        return pltpu.make_async_remote_copy(
            src_ref=src,
            dst_ref=dst,
            send_sem=send_sem,
            recv_sem=recv_sem,
            device_id={"seq": jnp.minimum(pos + 1, size - 1)},
            device_id_type=MESH,
        )

    def to_left(src, dst, send_sem, recv_sem):
        return pltpu.make_async_remote_copy(
            src_ref=src,
            dst_ref=dst,
            send_sem=send_sem,
            recv_sem=recv_sem,
            device_id={"seq": jnp.maximum(pos - 1, 0)},
            device_id_type=MESH,
        )

    halo_cuts = ((0, 1), (1, 2), (3, samples - 3))

    def halo(part):
        first, count = halo_cuts[part]
        span = pl.ds(first, count)
        right = to_right(
            atoms_hbm.at[span, rows - rim : rows, :],
            low_in.at[span],
            halo_send.at[0, part],
            halo_recv.at[0, part],
        )
        left = to_left(
            atoms_hbm.at[span, 0:rim, :],
            high_in.at[span],
            halo_send.at[1, part],
            halo_recv.at[1, part],
        )
        return right, left

    def edges(j):
        right = to_right(
            edge_out.at[1, j], edge_in.at[0, j], edge_send.at[0, j], edge_recv.at[0, j]
        )
        left = to_left(
            edge_out.at[0, j], edge_in.at[1, j], edge_send.at[1, j], edge_recv.at[1, j]
        )
        return right, left

    def launch(pair):
        right, left = pair

        @pl.when(pos < size - 1)
        def _():
            right.start()

        @pl.when(pos > 0)
        def _():
            left.start()

    def collect(pair):
        right, left = pair

        @pl.when(pos < size - 1)
        def _():
            right.wait_send()
            left.wait_recv()

        @pl.when(pos > 0)
        def _():
            left.wait_send()
            right.wait_recv()

    def forward_stages(s):
        slot = lax.rem(s, 2)
        gain = gain_ref[...]
        stages = []
        held = {}
        cuts = 4
        chunk = rows // cuts

        def rims():
            hid_all[s, :rim] = layer_norm(low_in[s].astype(F32), gain)[2]
            hid_all[s, rim + rows :] = layer_norm(high_in[s].astype(F32), gain)[2]
            kv_all[s, :rim] = mm(hid_all[s, :rim], wkv_scr[...]).astype(BF16)
            kv_all[s, rim + rows :] = mm(hid_all[s, rim + rows :], wkv_scr[...]).astype(BF16)

        def norm(c):
            def run():
                x = atoms_ref[0, c * chunk : (c + 1) * chunk].astype(F32)
                hid_all[s, rim + c * chunk : rim + (c + 1) * chunk] = layer_norm(x, gain)[2]

            return run

        def project(c):
            def run():
                span = slice(c * chunk, (c + 1) * chunk)
                hidden = hid_all[s, rim + c * chunk : rim + (c + 1) * chunk]
                kv_all[s, rim + c * chunk : rim + (c + 1) * chunk] = mm(
                    hidden, wkv_scr[...]
                ).astype(BF16)
                qg = mm(hidden, wqg_scr[...])
                q_all[s, span] = qg[:, :width].astype(BF16)
                gate_scr[span] = sigmoid(qg[:, width:])

            return run

        def score(g, spans):
            def run():
                q_exp = [expand(q_all[s, b * QBLK : (b + 1) * QBLK, :], masks) for b in spans]
                held[g] = [
                    mm(kv_all[s, b * QBLK : b * QBLK + KWIN, :width], q, NT)
                    for b, q in zip(spans, q_exp)
                ]

            return run

        def soften(g, spans):
            def run():
                es = [
                    jnp.exp2(sc * (scaling * LOG2E) + bias_scr[b])
                    for b, sc in zip(spans, held.pop(g))
                ]
                invs = [1.0 / jnp.sum(e, axis=0, keepdims=True) for e in es]
                for b, e, inv in zip(spans, es, invs):
                    low_all[s, b] = (e * inv).astype(BF16)

            return run

        def attend(spans):
            def run():
                wide = [
                    mm(low_all[s, b], kv_all[s, b * QBLK : b * QBLK + KWIN, width:], TN)
                    for b in spans
                ]
                for b, o in zip(spans, wide):
                    span = slice(b * QBLK, (b + 1) * QBLK)
                    att = collapse(o, lane_head)
                    gate = gate_scr[span]
                    gated = gate * att
                    gated_scr[slot, span] = gated.astype(BF16)
                    back_scr[slot, 0, span] = gate
                    back_scr[slot, 1, span] = gated * (1.0 - gate)

            return run

        stages.append(norm(0))
        for c in range(cuts):
            if c + 1 < cuts:
                stages.append(norm(c + 1))
            stages.append(project(c))
        own = len(stages)
        groups = [[g * FGROUP + w for w in range(FGROUP)] for g in range(blocks // FGROUP)]
        count = len(groups)
        for g in range(count + 2):
            if g < count:
                stages.append(score(g, groups[g]))
            if 0 <= g - 1 < count:
                stages.append(soften(g - 1, groups[g - 1]))
            if 0 <= g - 2 < count:
                stages.append(attend(groups[g - 2]))
        return [rims], stages[:own], stages[own:]

    def token_stages(s):
        slot = lax.rem(s, 2)
        chunk = 256
        half = rows // 2
        held = {}
        stages = []

        def begin():
            gated = gated_scr[slot]
            x = again_ref[0].astype(F32)
            held["updated"] = (x + mm(gated, wo_ref[...])).astype(BF16)
            held["cot"] = (cot_ref[0].astype(F32) * inv_scr[...]).astype(BF16)
            held["gupd"] = [None, None]

        def enter(c, r):
            def run():
                cols = slice(c * chunk, (c + 1) * chunk)
                span = slice(r * half, (r + 1) * half)
                held[c, r] = (
                    mm(held["updated"][span], wt_ref[:, cols]),
                    mm(member_scr[span, :], held["cot"][:, cols]),
                    [],
                    [],
                )

            return run

        def act(c, r, n):
            def run():
                pre, grad_act, acts, grads = held[c, r]
                part = slice(n * half // PARTS, (n + 1) * half // PARTS)
                pre, grad_act = pre[part], grad_act[part]
                sig = sigmoid(pre)
                value = pre * sig
                acts.append(value.astype(BF16))
                grads.append((grad_act * (sig + value * (1.0 - sig))).astype(BF16))

            return run

        def leave(c, r):
            def run():
                _, _, acts, grads = held.pop((c, r))
                cols = slice(c * chunk, (c + 1) * chunk)
                span = slice(r * half, (r + 1) * half)
                grad_pre = jnp.concatenate(grads, axis=0)
                pooled = mm(member_t_scr[:, span], jnp.concatenate(acts, axis=0))
                gtok = mm(held["updated"][span], grad_pre, TN)
                part = mm(grad_pre, wt_ref[:, cols], NT)
                if r == 0:
                    held["pooled"], held["gtok"] = pooled, gtok
                else:
                    pooled_ref[0, :, cols] = ((held["pooled"] + pooled) * inv_scr[...]).astype(BF16)
                    gtok_scr[:, cols] += held["gtok"] + gtok
                before = held["gupd"][r]
                held["gupd"][r] = part if before is None else before + part

            return run

        def end():
            grad_updated = jnp.concatenate(held["gupd"], axis=0).astype(BF16)
            gupd_all[s] = grad_updated
            gout_scr[...] += mm(gated_scr[slot], grad_updated, TN)
            grad_gated = mm(grad_updated, wo_ref[...], NT)
            gatt_all[s] = (grad_gated * back_scr[slot, 0]).astype(BF16)
            d_all[s, :, 3 * width :] = (grad_gated * back_scr[slot, 1]).astype(BF16)

        stages.append(begin)
        pieces = [(c, r) for c in range(wt_ref.shape[1] // chunk) for r in range(2)]
        for n in range(len(pieces) + 1):
            if n < len(pieces):
                stages.append(enter(*pieces[n]))
            if n > 0:
                for part in range(PARTS):
                    stages.append(act(*pieces[n - 1], part))
                stages.append(leave(*pieces[n - 1]))
        stages.append(end)
        return stages

    def backward_stages(s):
        open_k = []
        open_v = []
        held = {}
        stages = []

        def tiles(x):
            return [x[n * QBLK : (n + 1) * QBLK] for n in range(KWIN // QBLK)]

        def store(at, k, v):
            if at < rim:
                edge_out[0, s, at : at + k.shape[0], :width] = k
                edge_out[0, s, at : at + k.shape[0], width:] = v
            elif at < rim + rows:
                d_all[s, at - rim : at - rim + k.shape[0], width : 2 * width] = k
                d_all[s, at - rim : at - rim + k.shape[0], 2 * width : 3 * width] = v
            else:
                at = at - rim - rows
                edge_out[1, s, at : at + k.shape[0], :width] = k
                edge_out[1, s, at : at + k.shape[0], width:] = v

        def close(first, count):
            for n in range(count):
                at = (first + n) * QBLK
                k = (open_k[n] * scaling).astype(BF16)
                v = open_v[n].astype(BF16)
                half = QBLK // 2
                store(at, k[:half], v[:half])
                store(at + half, k[half:], v[half:])
            del open_k[:count]
            del open_v[:count]

        def merge(opened, parts):
            for n, part in enumerate(parts):
                if n < len(opened):
                    opened[n] = opened[n] + part
                else:
                    opened.append(part)

        def enter(g, spans):
            def run():
                ges = [expand(gatt_all[s, b * QBLK : (b + 1) * QBLK, :], masks) for b in spans]
                held["gp", g] = [
                    mm(kv_all[s, b * QBLK : b * QBLK + KWIN, width:], ge, NT)
                    for b, ge in zip(spans, ges)
                ]
                held["dv", g] = [mm(low_all[s, b], ge) for b, ge in zip(spans, ges)]

            return run

        def middle(g, spans):
            def run():
                ps = [low_all[s, b].astype(F32) for b in spans]
                ts = [p * gp for p, gp in zip(ps, held.pop(("gp", g)))]
                sums = [jnp.sum(t, axis=0, keepdims=True) for t in ts]
                dss = [t - p * total for p, t, total in zip(ps, ts, sums)]
                for b, ds in zip(spans, dss):
                    score_scr[b] += ds
                held["ds", g] = [ds.astype(BF16) for ds in dss]

            return run

        def products(g, spans):
            def run():
                lows = held.pop(("ds", g))
                q_exp = [expand(q_all[s, b * QBLK : (b + 1) * QBLK, :], masks) for b in spans]
                held["dk", g] = [mm(low, q) for low, q in zip(lows, q_exp)]
                held["dq", g] = [
                    mm(low, kv_all[s, b * QBLK : b * QBLK + KWIN, :width], TN)
                    for b, low in zip(spans, lows)
                ]

            return run

        def settle(g, spans):
            def run():
                for b, dk, dv in zip(spans, held.pop(("dk", g)), held.pop(("dv", g))):
                    merge(open_k, tiles(dk))
                    merge(open_v, tiles(dv))
                    close(b, 1)
                for b, dq in zip(spans, held.pop(("dq", g))):
                    d_all[s, b * QBLK : (b + 1) * QBLK, :width] = (
                        collapse(dq, lane_head) * scaling
                    ).astype(BF16)

            return run

        groups = [[g * BGROUP + w for w in range(BGROUP)] for g in range(blocks // BGROUP)]
        count = len(groups)
        for g in range(count + 2):
            for lag, make in enumerate((enter, middle)):
                if 0 <= g - lag < count:
                    stages.append(make(g - lag, groups[g - lag]))
            if 0 <= g - 1 < count:
                stages.append(products(g - 1, groups[g - 1]))
            if 0 <= g - 2 < count:
                stages.append(settle(g - 2, groups[g - 2]))
        stages.append(lambda: close(blocks, len(open_k)))
        return stages

    def weight_stages(s):
        cuts = 2
        chunk = rows // cuts

        def join():
            for side, at in ((0, 0), (1, rows - rim)):
                d_all[s, at : at + rim, width : 3 * width] = (
                    d_all[s, at : at + rim, width : 3 * width].astype(F32)
                    + edge_in[side, s].astype(F32)
                ).astype(BF16)

        def multiply(c):
            def run():
                hidden = hid_all[s, rim + c * chunk : rim + (c + 1) * chunk]
                gw_scr[...] += mm(hidden, d_all[s, c * chunk : (c + 1) * chunk], TN)

            return run

        return [join] + [multiply(c) for c in range(cuts)]

    def finish_stages(s):
        gain = gain_ref[...]
        stages = []
        cuts = 2
        chunk = rows // cuts
        held = {}

        def norm(c):
            def run():
                held[c] = layer_norm(again_ref[0, c * chunk : (c + 1) * chunk].astype(F32), gain)

            return run

        def multiply(c):
            def run():
                held["gh", c] = mm(d_all[s, c * chunk : (c + 1) * chunk], wall_scr[...], NT)

            return run

        def finish(c):
            def run():
                normed, inv_std, _ = held[c]
                gx = held["gh", c] * gain
                grad_ln = inv_std * (
                    gx
                    - jnp.mean(gx, axis=-1, keepdims=True)
                    - normed * jnp.mean(gx * normed, axis=-1, keepdims=True)
                )
                span = slice(c * chunk, (c + 1) * chunk)
                gatoms_ref[0, span] = (gupd_all[s, span].astype(F32) + grad_ln).astype(BF16)

            return run

        for c in range(cuts):
            stages += [norm(c), multiply(c)]
        for c in range(cuts):
            stages.append(finish(c))
        return stages

    @pl.when(step == 0)
    def _():
        barrier = pltpu.get_barrier_semaphore()
        for axis, count in axes:
            for d in range(1, count):
                pl.semaphore_signal(
                    barrier,
                    inc=1,
                    device_id={axis: shifted_index(axis, count, d)},
                    device_id_type=MESH,
                )

        @pl.when(pos == 0)
        def _():
            low_in[...] = jnp.zeros_like(low_in)
            edge_in[0] = jnp.zeros_like(edge_in[0])

        @pl.when(pos == size - 1)
        def _():
            high_in[...] = jnp.zeros_like(high_in)
            edge_in[1] = jnp.zeros_like(edge_in[1])

        build_bias(
            counts_ref, pair_ref, pair_weights(wpair_ref, per), bias_scr, blocks, rows
        )
        token = lax.broadcasted_iota(jnp.int32, (tokens, rows), 0)
        place = lax.broadcasted_iota(jnp.int32, (tokens, rows), 1)
        hit = (ids_ref[...] - pos * tokens == token) & (place < counts_ref[pos])
        member_t = jnp.where(hit, 1.0, 0.0).astype(F32)
        inv_scr[...] = 1.0 / jnp.sum(member_t, axis=1, keepdims=True)
        member_t_scr[...] = member_t.astype(BF16)
        member_scr[...] = member_t.T.astype(BF16)
        wqg_scr[:, :width] = wq_ref[...]
        wqg_scr[:, width:] = wg_ref[...]
        wkv_scr[:, :width] = wk_ref[...]
        wkv_scr[:, width:] = wv_ref[...]
        for n, ref in enumerate((wq_ref, wk_ref, wv_ref, wg_ref)):
            wall_scr[:, n * width : (n + 1) * width] = ref[...]
        for ref in (score_scr, gout_scr, gtok_scr, gw_scr):
            ref[...] = jnp.zeros_like(ref)
        pl.semaphore_wait(barrier, sum(count - 1 for _, count in axes))
        for part in range(len(halo_cuts)):
            launch(halo(part))
        outer, own, rest = forward_stages(0)
        weave(own)
        collect(halo(0))
        weave(outer + rest)

    for part in range(1, len(halo_cuts)):
        pl.when(step == halo_cuts[part][0])(lambda part=part: collect(halo(part)))

    @pl.when((step > 0) & (step < samples))
    def _():
        outer, own, rest = forward_stages(step)
        weave(token_stages(step - 1), outer + own + rest)

    @pl.when(step == samples)
    def _():
        weave(token_stages(samples - 1), backward_stages(0))

    @pl.when((step > samples) & (step < samples + LAG))
    def _():
        weave(backward_stages(step - samples))

    @pl.when((step >= samples + LAG) & (step < 2 * samples))
    def _():
        collect(edges(step - samples - LAG))
        weave(weight_stages(step - samples - LAG), backward_stages(step - samples))

    @pl.when((step >= samples) & (step < 2 * samples))
    def _():
        launch(edges(step - samples))

    @pl.when(step >= 2 * samples)
    def _():
        weave(finish_stages(step - 2 * samples))

    @pl.when(step == min(2 * samples + 3, last))
    def _():
        lines = pair_gradient(pair_ref, score_scr, per, pair_chunk, blocks)
        for n, line in enumerate(lines):
            small_src[0, n : n + 1, :] = line
        small_src[0, HEADS:, :] = jnp.zeros((8 - HEADS, width), F32)

    def fill_early():
        for n in range(gtok_scr.shape[1] // width):
            early_buf[n * width : (n + 1) * width, :] = gtok_scr[:, n * width : (n + 1) * width]
        at = gtok_scr.shape[1]
        early_buf[at : at + width, :] = gout_scr[...]
        early_buf[at + width :, :] = jnp.zeros((early_buf.shape[0] - at - width, width), F32)

    for n, action in enumerate(early.actions()):

        def run(n=n, action=action):
            if n == 0:
                fill_early()
            action()

        pl.when(step == min(samples + EARLY_AT[n], last))(run)

    def small_copies(k):
        axis, count = axes[k]
        base = 0 if k == 0 else axes[0][1] - 1
        return [
            pltpu.make_async_remote_copy(
                src_ref=small_src.at[k],
                dst_ref=(small_a, small_b)[k].at[d - 1],
                send_sem=small_send.at[base + d - 1],
                recv_sem=small_recv.at[base + d - 1],
                device_id={axis: shifted_index(axis, count, d)},
                device_id_type=MESH,
            )
            for d in range(1, count)
        ]

    def small_total(k):
        value = small_src[k]
        for n, copy in enumerate(small_copies(k)):
            copy.wait()
            value = value + (small_a, small_b)[k][n]
        return value

    def late_start():
        for s in range(samples - LAG, samples):
            collect(edges(s))
            weave(weight_stages(s))
        for n in range(4):
            late_buf[n * width : (n + 1) * width, :] = gw_scr[:, n * width : (n + 1) * width]
        if late_buf.shape[0] > 4 * width:
            late_buf[4 * width :, :] = jnp.zeros((late_buf.shape[0] - 4 * width, width), F32)
        late.scatter(0)

    def late_second():
        for copy in small_copies(0):
            copy.start()
        late.scatter(1)

    def late_third():
        late.gather(1)
        small_src[1] = small_total(0)
        for copy in small_copies(1):
            copy.start()

    def late_fourth():
        late.gather(0)
        small_ref[...] = small_total(1)

    def late_end():
        late.finish()
        early_ref[...] = early_sum[...]
        late_ref[...] = late_sum[...]

    late_actions = [late_start, late_second, late_third, late_fourth, late_end]
    for n, action in enumerate(late_actions):
        pl.when(step == min(2 * samples + LATE_AT[n], last))(action)


def unpack_kernel(
    channels,
    early_ref,
    late_ref,
    small_ref,
    gain_ref,
    wq_ref,
    wk_ref,
    wv_ref,
    wg_ref,
    pooled_ref,
    gatoms_ref,
    ggain_out,
    gq_out,
    gk_out,
    gv_out,
    gg_out,
    gout_out,
    gtok_out,
    gpair_out,
    pooled_out,
    gatoms_out,
    pooled_scr,
    gatoms_scr,
    sems,
):
    moves = []
    count = sems.shape[0] // 4
    for n, (src, mid, dst) in enumerate(
        ((pooled_ref, pooled_scr, pooled_out), (gatoms_ref, gatoms_scr, gatoms_out))
    ):
        size = src.shape[0] // count
        for c in range(count):
            span = pl.ds(c * size, size)
            at = 2 * (n * count + c)
            moves.append(
                (
                    pltpu.make_async_copy(src.at[span], mid.at[span], sems.at[at]),
                    pltpu.make_async_copy(mid.at[span], dst.at[span], sems.at[at + 1]),
                )
            )
    for fetch, _ in moves:
        fetch.start()
    width = gout_out.shape[0]
    blocks = gtok_out.shape[1] // width

    def block(ref, n):
        return ref[n * width : (n + 1) * width, :].astype(F32)

    for fetch, put in moves:
        fetch.wait()
        put.start()
    for n in range(blocks):
        gtok_out[:, n * width : (n + 1) * width] = block(early_ref, n)
    gout_out[...] = block(early_ref, blocks)
    by_gain = None
    weights = (wq_ref, wk_ref, wv_ref, wg_ref)
    for n, (ref, weight) in enumerate(zip((gq_out, gk_out, gv_out, gg_out), weights)):
        grad = block(late_ref, n)
        ref[...] = grad
        part = grad * weight[...].astype(F32)
        by_gain = part if by_gain is None else by_gain + part
    ggain_out[...] = jnp.sum(by_gain.T, axis=0, keepdims=True) / gain_ref[...]
    lines = small_ref[...]
    shift = width // 2
    while shift >= channels:
        lines = lines + pltpu.roll(lines, shift, 1)
        shift //= 2
    gpair_out[...] = lines[:HEADS, :channels]
    for _, put in moves:
        put.wait()


def whole(*shape):
    return pl.BlockSpec(shape, lambda s: (0,) * len(shape))


def sum_scratch(total, streams, orders, width):
    unit = total // streams
    slots = []
    for stream in range(streams):
        length = unit
        for _, size in orders[stream]:
            length //= size
            slots.append(pltpu.VMEM((size - 1, length, width), BF16))
    return slots * 2


def on_device(
    atoms,
    gain,
    w_query,
    w_key,
    w_value,
    w_gate,
    w_out,
    w_token,
    w_pair,
    pair_cond,
    counts,
    membership,
    pooled_cot,
):
    samples, rows, width = atoms.shape
    blocks = rows // QBLK
    rim = (KWIN - QBLK) // 2
    tokens, token_width = pooled_cot.shape[1:]
    channels = w_pair.shape[0]
    pair2 = pair_cond.reshape(blocks * QBLK, pair_cond.shape[-1])
    gain2 = gain.reshape(1, width)
    ids2 = membership.reshape(1, rows)
    square = whole(width, width)
    shape = jax.ShapeDtypeStruct
    vmem = pltpu.VMEM
    dma = pltpu.SemaphoreType.DMA

    axes = axis_sizes()
    devices = axes[0][1] * axes[1][1]
    peers = sum(size - 1 for _, size in axes)
    unit = 16 * devices
    early_total = -(-(token_width + width) // unit) * unit
    late_total = -(-(4 * width) // unit) * unit
    early_streams = early_total // unit
    late_streams = late_total // unit
    early_orders = [axes] * early_streams

    def clip(x):
        return jnp.clip(x, 0, samples - 1)

    def again(i):
        return jnp.where(i <= samples, clip(i - 1), clip(i - 2 * samples))

    pooled, gatoms, early, late, small = pl.pallas_call(
        functools.partial(step_kernel, samples, early_streams, late_streams),
        grid=(3 * samples,),
        in_specs=[
            pl.BlockSpec(memory_space=pltpu.SMEM),
            pl.BlockSpec(memory_space=pl.ANY),
            pl.BlockSpec((1, rows, width), lambda i: (clip(i), 0, 0)),
            pl.BlockSpec((1, rows, width), lambda i: (again(i), 0, 0)),
            whole(1, width),
            square,
            square,
            square,
            square,
            square,
            whole(width, token_width),
            whole(*w_pair.T.shape),
            whole(*pair2.shape),
            whole(1, rows),
            pl.BlockSpec((1, tokens, token_width), lambda i: (clip(i - 1), 0, 0)),
        ],
        out_specs=[
            pl.BlockSpec((1, tokens, token_width), lambda i: (clip(i - 1), 0, 0)),
            pl.BlockSpec((1, rows, width), lambda i: (clip(i - 2 * samples), 0, 0)),
            whole(early_total, width),
            whole(late_total, width),
            whole(8, width),
        ],
        out_shape=[
            shape((samples, tokens, token_width), BF16),
            shape((samples, rows, width), BF16),
            shape((early_total, width), BF16),
            shape((late_total, width), BF16),
            shape((8, width), F32),
        ],
        scratch_shapes=[
            vmem((samples, rim, width), BF16),
            vmem((samples, rim, width), BF16),
            vmem((2, samples, rim, 2 * width), BF16),
            vmem((2, samples, rim, 2 * width), BF16),
            vmem((blocks, KWIN, LANES), F32),
            vmem((blocks, KWIN, LANES), F32),
            vmem((rows, tokens), BF16),
            vmem((tokens, rows), BF16),
            vmem((tokens, 1), F32),
            vmem((width, 2 * width), BF16),
            vmem((width, 2 * width), BF16),
            vmem((width, 4 * width), BF16),
            vmem((samples, rows + 2 * rim, width), BF16),
            vmem((rows, width), F32),
            vmem((2, rows, width), BF16),
            vmem((2, 2, rows, width), F32),
            vmem((samples, rows, width), BF16),
            vmem((samples, rows + 2 * rim, 2 * width), BF16),
            vmem((samples, blocks, KWIN, LANES), BF16),
            vmem((samples, rows, width), BF16),
            vmem((samples, rows, width), BF16),
            vmem((samples, rows, 4 * width), BF16),
            vmem((width, width), F32),
            vmem((width, token_width), F32),
            vmem((width, 4 * width), F32),
            vmem((early_total, width), F32),
            vmem((late_total, width), F32),
            vmem((early_total, width), BF16),
            vmem((late_total, width), BF16),
            vmem((axes[0][1] - 1, 8, width), F32),
            vmem((axes[1][1] - 1, 8, width), F32),
            vmem((2, 8, width), F32),
            dma((2, 3)),
            dma((2, 3)),
            dma((2, samples)),
            dma((2, samples)),
            dma((2 * early_streams * peers,)),
            dma((2 * early_streams * peers,)),
            dma((2 * late_streams * peers,)),
            dma((2 * late_streams * peers,)),
            dma((peers,)),
            dma((peers,)),
        ]
        + sum_scratch(early_total, early_streams, early_orders, width)
        + sum_scratch(late_total, late_streams, [axes] * late_streams, width),
        compiler_params=pltpu.CompilerParams(
            dimension_semantics=("arbitrary",),
            vmem_limit_bytes=56 * 1024 * 1024,
            collective_id=0,
            has_side_effects=True,
        ),
    )(
        counts,
        atoms,
        atoms,
        atoms,
        gain2,
        w_query,
        w_key,
        w_value,
        w_gate,
        w_out,
        w_token,
        w_pair.T,
        pair2,
        ids2,
        pooled_cot,
    )
    spec = pl.BlockSpec(memory_space=pltpu.VMEM)
    anywhere = pl.BlockSpec(memory_space=pl.ANY)
    pieces = next(n for n in (4, 3, 2, 1) if samples % n == 0)
    ggain, gq, gk, gv, gg, gout, gtok, gpair, pooled, gatoms = pl.pallas_call(
        functools.partial(unpack_kernel, channels),
        in_specs=[spec] * 8 + [anywhere] * 2,
        out_specs=[spec] * 8 + [anywhere] * 2,
        out_shape=[shape((1, width), F32)]
        + [shape((width, width), F32)] * 5
        + [shape((width, token_width), F32), shape((HEADS, channels), F32)]
        + [shape(pooled.shape, BF16), shape(gatoms.shape, BF16)],
        scratch_shapes=[vmem(pooled.shape, BF16), vmem(gatoms.shape, BF16), dma((4 * pieces,))],
    )(early, late, small, gain2, w_query, w_key, w_value, w_gate, pooled, gatoms)
    return (pooled, gatoms, ggain.reshape(width), gq, gk, gv, gg, gout, gtok, gpair.T)


def solution(mesh):
    placed = (
        P("samp", "seq", None),
        P(),
        P(),
        P(),
        P(),
        P(),
        P(),
        P(),
        P(),
        P("seq", None, None),
        P(),
        P("seq"),
        P("samp", "seq", None),
    )
    return jax.shard_map(
        on_device,
        mesh=mesh,
        in_specs=placed,
        out_specs=(
            P("samp", "seq", None),
            P("samp", "seq", None),
            P(),
            P(),
            P(),
            P(),
            P(),
            P(),
            P(),
            P(),
        ),
        check_vma=False,
    )
```

```python
import functools

import jax
import jax.numpy as jnp
from jax import lax
from jax.experimental import pallas as pl
from jax.experimental.pallas import tpu as pltpu
from jax.sharding import PartitionSpec as P

HEADS = 4
QBLK = 32
KWIN = 128
LOG2E = 1.4426950408889634

epsilon = 1e-05
F32 = jnp.float32
BF16 = jnp.bfloat16
NN = (((1,), (0,)), ((), ()))
NT = (((1,), (1,)), ((), ()))
TN = (((0,), (0,)), ((), ()))
GROUP = 4
FGROUP = 8
PARTS = 1
BGROUP = 8
LANES = 128
MESH = pl.DeviceIdType.MESH
LAG = 3
EARLY_AT = (1, 4, 8, 12, 1 << 20)
LATE_AT = (2, 5, 7, 9, 1 << 20)


def mm(a, b, dims=NN):
    return lax.dot_general(a, b, dims, preferred_element_type=F32)


def sigmoid(x):
    return 0.5 * jnp.tanh(0.5 * x) + 0.5


def layer_norm(x, gain):
    centred = x - jnp.mean(x, axis=-1, keepdims=True)
    variance = jnp.mean(centred * centred, axis=-1, keepdims=True)
    inv_std = lax.rsqrt(variance + epsilon)
    normed = centred * inv_std
    return normed, inv_std, (normed * gain).astype(BF16)


def head_lanes(width):
    lane = lax.broadcasted_iota(jnp.int32, (1, width), 1)
    return lane // (width // HEADS)


def expand(block, masks):
    return jnp.concatenate([block * m for m in masks], axis=0)


def collapse(wide, lane_head):
    rows = wide.shape[0] // HEADS
    out = wide[:rows]
    for h in range(1, HEADS):
        out = jnp.where(lane_head == h, wide[h * rows : (h + 1) * rows], out)
    return out


def lane_swap(parts, lane_block):
    count = len(parts)
    outs = []
    for b in range(count):
        out = None
        for a in range(count):
            shift = (QBLK * (a - b)) % LANES
            moved = parts[a] if shift == 0 else pltpu.roll(parts[a], shift, 1)
            out = moved if out is None else jnp.where(lane_block == a, moved, out)
        outs.append(out)
    return outs


def pair_weights(wpair_ref, per):
    channels = wpair_ref.shape[1]
    high, wide = HEADS * per, per * channels
    row = lax.broadcasted_iota(jnp.int32, (high, HEADS), 0) // per
    head = lax.broadcasted_iota(jnp.int32, (high, HEADS), 1)
    pick = jnp.where(row == head, 1.0, 0.0).astype(BF16)
    by_row = mm(pick, wpair_ref[...]).astype(BF16)
    lane = lax.rem(lax.broadcasted_iota(jnp.int32, (channels, wide), 1), channels)
    chan = lax.broadcasted_iota(jnp.int32, (channels, wide), 0)
    spread = mm(by_row, jnp.where(lane == chan, 1.0, 0.0).astype(BF16))
    key = lax.rem(lax.broadcasted_iota(jnp.int32, (high, wide), 0), per)
    spot = lax.broadcasted_iota(jnp.int32, (high, wide), 1) // channels
    return jnp.where(key == spot, spread, 0.0).astype(BF16)


def build_bias(counts_ref, pair_ref, wsm, bias_scr, blocks, rows):
    pos = lax.axis_index("seq")
    size = lax.axis_size("seq")
    own = counts_ref[pos]
    left = jnp.where(pos > 0, counts_ref[jnp.maximum(pos - 1, 0)], 0)
    right = jnp.where(pos < size - 1, counts_ref[jnp.minimum(pos + 1, size - 1)], 0)
    rim = (KWIN - QBLK) // 2
    lane_block = head_lanes(LANES)
    chunk = wsm.shape[1]
    per = wsm.shape[0] // HEADS
    for kk in range(pair_ref.shape[1] // chunk):
        biased = mm(wsm, pair_ref[:, kk * chunk : (kk + 1) * chunk], NT)
        for g in range(blocks // GROUP):
            parts = [
                biased[h * per : (h + 1) * per, g * LANES : (g + 1) * LANES] for h in range(HEADS)
            ]
            for w, out in enumerate(lane_swap(parts, lane_block)):
                b = g * GROUP + w
                slot = (
                    lax.broadcasted_iota(jnp.int32, (per, LANES), 0) + kk * per + b * QBLK - rim
                )
                alive = (
                    ((slot < 0) & (slot + rows < left))
                    | ((slot >= 0) & (slot < own))
                    | ((slot >= rows) & (slot - rows < right))
                )
                bias_scr[b, kk * per : (kk + 1) * per, :] = jnp.where(alive, out * LOG2E, -1e30)


def pair_gradient(pair_ref, score_scr, per, chunk, blocks):
    lane_block = head_lanes(LANES)
    total = None
    for kk in range(pair_ref.shape[1] // chunk):
        columns = []
        for g in range(blocks // GROUP):
            parts = [score_scr[g * GROUP + w, kk * per : (kk + 1) * per, :] for w in range(GROUP)]
            columns.append(jnp.concatenate(lane_swap(parts, lane_block), axis=0))
        grads = jnp.concatenate(columns, axis=1).astype(BF16)
        part = mm(grads, pair_ref[:, kk * chunk : (kk + 1) * chunk])
        total = part if total is None else total + part
    high, wide = total.shape
    row = lax.broadcasted_iota(jnp.int32, (high, wide), 0)
    lane = lax.broadcasted_iota(jnp.int32, (high, wide), 1)
    diagonal = jnp.where(lax.rem(row, per) == lane // (wide // per), total, 0.0)
    lines = []
    for h in range(HEADS):
        line = jnp.sum(diagonal[h * per : (h + 1) * per], axis=0, keepdims=True)
        folded = line[:, :LANES]
        for n in range(1, wide // LANES):
            folded = folded + line[:, n * LANES : (n + 1) * LANES]
        lines.append(folded)
    return lines


def weave(*lists):
    lists = [x for x in lists if x]
    done = [0] * len(lists)
    while True:
        best = None
        for n, x in enumerate(lists):
            if done[n] < len(x):
                share = (done[n] + 0.5) / len(x)
                if best is None or share < best[0]:
                    best = (share, n)
        if best is None:
            return
        n = best[1]
        lists[n][done[n]]()
        done[n] += 1


def axis_sizes():
    return [(axis, lax.axis_size(axis)) for axis in ("samp", "seq")]


def shifted_index(axis, size, distance):
    return lax.rem(lax.axis_index(axis) + distance, size)


class Summer:
    def __init__(self, buf, out, streams, orders, send_sem, recv_sem, slots):
        self.buf, self.out, self.streams, self.orders = buf, out, streams, orders
        self.send_sem, self.recv_sem = send_sem, recv_sem
        self.sends, self.recvs = slots[: 2 * streams], slots[2 * streams :]
        self.unit = buf.shape[0] // streams
        self.peers = sum(size - 1 for _, size in orders[0])

    def spans(self, stream):
        (a0, s0), (a1, s1) = self.orders[stream]
        off0 = stream * self.unit
        len1 = self.unit // s0
        len2 = len1 // s1
        off1 = off0 + lax.axis_index(a0) * len1
        off2 = off1 + lax.axis_index(a1) * len2
        return [(off0, self.unit), (off1, len1), (off2, len2)]

    def copy(self, stream, src, dst, slot, partner):
        at = stream * 2 * self.peers + slot
        return pltpu.make_async_remote_copy(
            src_ref=src,
            dst_ref=dst,
            send_sem=self.send_sem.at[at],
            recv_sem=self.recv_sem.at[at],
            device_id=partner,
            device_id_type=MESH,
        )

    def scatter_copies(self, stream, k):
        axis, size = self.orders[stream][k]
        base = 0 if k == 0 else self.orders[stream][0][1] - 1
        return [
            self.copy(
                stream,
                self.sends[2 * stream + k].at[d - 1],
                self.recvs[2 * stream + k].at[d - 1],
                base + d - 1,
                {axis: shifted_index(axis, size, d)},
            )
            for d in range(1, size)
        ]

    def gather_copies(self, stream, k):
        axis, size = self.orders[stream][k]
        base = self.peers + (0 if k == 1 else self.orders[stream][1][1] - 1)
        off, length = self.spans(stream)[k + 1]
        part = self.out.at[pl.ds(pl.multiple_of(off, 16), length), :]
        return [
            self.copy(stream, part, part, base + d - 1, {axis: shifted_index(axis, size, d)})
            for d in range(1, size)
        ]

    def scatter(self, k):
        for stream in range(self.streams):
            spans = self.spans(stream)
            axis, size = self.orders[stream][k]
            if k > 0:
                off, length = spans[k]
                rows = pl.ds(pl.multiple_of(off, 16), length)
                self.buf[rows, :] = self.absorbed(stream, k - 1)
            off, length = spans[k][0], spans[k + 1][1]
            for d, copy in enumerate(self.scatter_copies(stream, k), 1):
                give = pl.multiple_of(off + shifted_index(axis, size, d) * length, 16)
                self.sends[2 * stream + k][d - 1] = self.buf[pl.ds(give, length), :].astype(BF16)
                copy.start()

    def absorbed(self, stream, k):
        off, length = self.spans(stream)[k + 1]
        value = self.buf[pl.ds(pl.multiple_of(off, 16), length), :]
        for n, copy in enumerate(self.scatter_copies(stream, k)):
            copy.wait()
            value = value + self.recvs[2 * stream + k][n].astype(F32)
        return value

    def gather(self, k):
        for stream in range(self.streams):
            if k == 1:
                off, length = self.spans(stream)[2]
                rows = pl.ds(pl.multiple_of(off, 16), length)
                self.out[rows, :] = self.absorbed(stream, 1).astype(BF16)
            else:
                for copy in self.gather_copies(stream, 1):
                    copy.wait()
            for copy in self.gather_copies(stream, k):
                copy.start()

    def finish(self):
        for stream in range(self.streams):
            for copy in self.gather_copies(stream, 0):
                copy.wait()

    def actions(self):
        return [
            lambda: self.scatter(0),
            lambda: self.scatter(1),
            lambda: self.gather(1),
            lambda: self.gather(0),
            self.finish,
        ]


def step_kernel(
    samples,
    early_streams,
    late_streams,
    counts_ref,
    atoms_hbm,
    atoms_ref,
    again_ref,
    gain_ref,
    wq_ref,
    wk_ref,
    wv_ref,
    wg_ref,
    wo_ref,
    wt_ref,
    wpair_ref,
    pair_hbm,
    ids_ref,
    cot_ref,
    pooled_ref,
    gatoms_ref,
    early_ref,
    late_ref,
    small_ref,
    low_in,
    high_in,
    edge_out,
    edge_in,
    pair_ref,
    bias_scr,
    score_scr,
    member_scr,
    member_t_scr,
    inv_scr,
    wqg_scr,
    wkv_scr,
    wall_scr,
    half_scr,
    hid_all,
    gate_scr,
    gated_scr,
    back_scr,
    q_all,
    kv_all,
    low_all,
    gatt_all,
    gupd_all,
    d_all,
    gout_scr,
    gtok_scr,
    gw_scr,
    early_buf,
    late_buf,
    early_sum,
    late_sum,
    small_a,
    small_b,
    small_src,
    halo_send,
    halo_recv,
    edge_send,
    edge_recv,
    early_send,
    early_recv,
    late_send,
    late_recv,
    small_send,
    small_recv,
    pair_sem,
    *slots,
):
    step = pl.program_id(0)
    rows, width = q_all.shape[1:]
    blocks = rows // QBLK
    rim = (KWIN - QBLK) // 2
    tokens = inv_scr.shape[0]
    per = 2 * LANES // wpair_ref.shape[1]
    pair_chunk = per * wpair_ref.shape[1]
    scaling = (width // HEADS) ** (-0.5)
    lane_head = head_lanes(width)
    masks = [(lane_head == h).astype(F32).astype(BF16) for h in range(HEADS)]
    axes = axis_sizes()
    pos = lax.axis_index("seq")
    size = lax.axis_size("seq")
    last = 3 * samples - 1

    early_orders = [axes] * early_streams
    early = Summer(
        early_buf,
        early_sum,
        early_streams,
        early_orders,
        early_send,
        early_recv,
        slots[: 4 * early_streams],
    )
    late = Summer(
        late_buf,
        late_sum,
        late_streams,
        [axes] * late_streams,
        late_send,
        late_recv,
        slots[4 * early_streams :],
    )

    def to_right(src, dst, send_sem, recv_sem):
        return pltpu.make_async_remote_copy(
            src_ref=src,
            dst_ref=dst,
            send_sem=send_sem,
            recv_sem=recv_sem,
            device_id={"seq": jnp.minimum(pos + 1, size - 1)},
            device_id_type=MESH,
        )

    def to_left(src, dst, send_sem, recv_sem):
        return pltpu.make_async_remote_copy(
            src_ref=src,
            dst_ref=dst,
            send_sem=send_sem,
            recv_sem=recv_sem,
            device_id={"seq": jnp.maximum(pos - 1, 0)},
            device_id_type=MESH,
        )

    halo_cuts = ((0, 1), (1, 2), (3, samples - 3))

    def halo(part):
        first, count = halo_cuts[part]
        span = pl.ds(first, count)
        right = to_right(
            atoms_hbm.at[span, rows - rim : rows, :],
            low_in.at[span],
            halo_send.at[0, part],
            halo_recv.at[0, part],
        )
        left = to_left(
            atoms_hbm.at[span, 0:rim, :],
            high_in.at[span],
            halo_send.at[1, part],
            halo_recv.at[1, part],
        )
        return right, left

    def edges(j):
        right = to_right(
            edge_out.at[1, j], edge_in.at[0, j], edge_send.at[0, j], edge_recv.at[0, j]
        )
        left = to_left(
            edge_out.at[0, j], edge_in.at[1, j], edge_send.at[1, j], edge_recv.at[1, j]
        )
        return right, left

    def launch(pair):
        right, left = pair

        @pl.when(pos < size - 1)
        def _():
            right.start()

        @pl.when(pos > 0)
        def _():
            left.start()

    def collect(pair):
        right, left = pair

        @pl.when(pos < size - 1)
        def _():
            right.wait_send()
            left.wait_recv()

        @pl.when(pos > 0)
        def _():
            left.wait_send()
            right.wait_recv()

    def forward_stages(s):
        slot = lax.rem(s, 2)
        gain = gain_ref[...]
        stages = []
        held = {}
        cuts = 4
        chunk = rows // cuts

        def rims():
            hid_all[s, :rim] = layer_norm(low_in[s].astype(F32), gain)[2]
            hid_all[s, rim + rows :] = layer_norm(high_in[s].astype(F32), gain)[2]
            kv_all[s, :rim] = mm(hid_all[s, :rim], wkv_scr[...]).astype(BF16)
            kv_all[s, rim + rows :] = mm(hid_all[s, rim + rows :], wkv_scr[...]).astype(BF16)

        def norm(c):
            def run():
                x = atoms_ref[0, c * chunk : (c + 1) * chunk].astype(F32)
                hid_all[s, rim + c * chunk : rim + (c + 1) * chunk] = layer_norm(x, gain)[2]

            return run

        def project(c):
            def run():
                span = slice(c * chunk, (c + 1) * chunk)
                hidden = hid_all[s, rim + c * chunk : rim + (c + 1) * chunk]
                kv_all[s, rim + c * chunk : rim + (c + 1) * chunk] = mm(
                    hidden, wkv_scr[...]
                ).astype(BF16)
                qg = mm(hidden, wqg_scr[...])
                q_all[s, span] = qg[:, :width].astype(BF16)
                gate_scr[span] = sigmoid(qg[:, width:])

            return run

        def score(g, spans):
            def run():
                q_exp = [expand(q_all[s, b * QBLK : (b + 1) * QBLK, :], masks) for b in spans]
                held[g] = [
                    mm(kv_all[s, b * QBLK : b * QBLK + KWIN, :width], q, NT)
                    for b, q in zip(spans, q_exp)
                ]

            return run

        def soften(g, spans):
            def run():
                es = [
                    jnp.exp2(sc * (scaling * LOG2E) + bias_scr[b])
                    for b, sc in zip(spans, held.pop(g))
                ]
                invs = [1.0 / jnp.sum(e, axis=0, keepdims=True) for e in es]
                for b, e, inv in zip(spans, es, invs):
                    low_all[s, b] = (e * inv).astype(BF16)

            return run

        def attend(spans):
            def run():
                wide = [
                    mm(low_all[s, b], kv_all[s, b * QBLK : b * QBLK + KWIN, width:], TN)
                    for b in spans
                ]
                for b, o in zip(spans, wide):
                    span = slice(b * QBLK, (b + 1) * QBLK)
                    att = collapse(o, lane_head)
                    gate = gate_scr[span]
                    gated = gate * att
                    gated_scr[slot, span] = gated.astype(BF16)
                    back_scr[slot, 0, span] = gate
                    back_scr[slot, 1, span] = gated * (1.0 - gate)

            return run

        stages.append(norm(0))
        for c in range(cuts):
            if c + 1 < cuts:
                stages.append(norm(c + 1))
            stages.append(project(c))
        own = len(stages)
        groups = [[g * FGROUP + w for w in range(FGROUP)] for g in range(blocks // FGROUP)]
        count = len(groups)
        for g in range(count + 2):
            if g < count:
                stages.append(score(g, groups[g]))
            if 0 <= g - 1 < count:
                stages.append(soften(g - 1, groups[g - 1]))
            if 0 <= g - 2 < count:
                stages.append(attend(groups[g - 2]))
        return [rims], stages[:own], stages[own:]

    def token_stages(s):
        slot = lax.rem(s, 2)
        chunk = 256
        half = rows // 2
        held = {}
        stages = []

        def begin():
            gated = gated_scr[slot]
            x = again_ref[0].astype(F32)
            held["updated"] = (x + mm(gated, wo_ref[...])).astype(BF16)
            held["cot"] = (cot_ref[0].astype(F32) * (0.5 * inv_scr[...])).astype(BF16)
            held["gupd"] = [None, None]

        def enter(c, r):
            def run():
                cols = slice(c * chunk, (c + 1) * chunk)
                span = slice(r * half, (r + 1) * half)
                held[c, r] = (
                    mm(held["updated"][span], half_scr[:, cols]),
                    mm(member_scr[span, :], held["cot"][:, cols]),
                    [],
                    [],
                )

            return run

        def act(c, r, n):
            def run():
                pre, grad_act, acts, grads = held[c, r]
                part = slice(n * half // PARTS, (n + 1) * half // PARTS)
                pre, grad_act = pre[part], grad_act[part]
                bent = jnp.tanh(pre)
                rise = 1.0 + bent
                value = pre * rise
                acts.append(value.astype(BF16))
                grads.append((grad_act * (rise + value * (1.0 - bent))).astype(BF16))

            return run

        def leave(c, r):
            def run():
                _, _, acts, grads = held.pop((c, r))
                cols = slice(c * chunk, (c + 1) * chunk)
                span = slice(r * half, (r + 1) * half)
                grad_pre = jnp.concatenate(grads, axis=0)
                pooled = mm(member_t_scr[:, span], jnp.concatenate(acts, axis=0))
                gtok = mm(held["updated"][span], grad_pre, TN)
                part = mm(grad_pre, wt_ref[:, cols], NT)
                if r == 0:
                    held["pooled"], held["gtok"] = pooled, gtok
                else:
                    pooled_ref[0, :, cols] = ((held["pooled"] + pooled) * inv_scr[...]).astype(BF16)
                    gtok_scr[:, cols] += held["gtok"] + gtok
                before = held["gupd"][r]
                held["gupd"][r] = part if before is None else before + part

            return run

        def end():
            grad_updated = jnp.concatenate(held["gupd"], axis=0).astype(BF16)
            gupd_all[s] = grad_updated
            gout_scr[...] += mm(gated_scr[slot], grad_updated, TN)
            grad_gated = mm(grad_updated, wo_ref[...], NT)
            gatt_all[s] = (grad_gated * back_scr[slot, 0]).astype(BF16)
            d_all[s, :, 3 * width :] = (grad_gated * back_scr[slot, 1]).astype(BF16)

        stages.append(begin)
        pieces = [(c, r) for c in range(wt_ref.shape[1] // chunk) for r in range(2)]
        for n in range(len(pieces) + 1):
            if n < len(pieces):
                stages.append(enter(*pieces[n]))
            if n > 0:
                for part in range(PARTS):
                    stages.append(act(*pieces[n - 1], part))
                stages.append(leave(*pieces[n - 1]))
        stages.append(end)
        return stages

    def backward_stages(s):
        open_k = []
        open_v = []
        held = {}
        stages = []

        def tiles(x):
            return [x[n * QBLK : (n + 1) * QBLK] for n in range(KWIN // QBLK)]

        def store(at, k, v):
            if at < rim:
                edge_out[0, s, at : at + k.shape[0], :width] = k
                edge_out[0, s, at : at + k.shape[0], width:] = v
            elif at < rim + rows:
                d_all[s, at - rim : at - rim + k.shape[0], width : 2 * width] = k
                d_all[s, at - rim : at - rim + k.shape[0], 2 * width : 3 * width] = v
            else:
                at = at - rim - rows
                edge_out[1, s, at : at + k.shape[0], :width] = k
                edge_out[1, s, at : at + k.shape[0], width:] = v

        def close(first, count):
            for n in range(count):
                at = (first + n) * QBLK
                k = (open_k[n] * scaling).astype(BF16)
                v = open_v[n].astype(BF16)
                half = QBLK // 2
                store(at, k[:half], v[:half])
                store(at + half, k[half:], v[half:])
            del open_k[:count]
            del open_v[:count]

        def merge(opened, parts):
            for n, part in enumerate(parts):
                if n < len(opened):
                    opened[n] = opened[n] + part
                else:
                    opened.append(part)

        def enter(g, spans):
            def run():
                ges = [expand(gatt_all[s, b * QBLK : (b + 1) * QBLK, :], masks) for b in spans]
                held["gp", g] = [
                    mm(kv_all[s, b * QBLK : b * QBLK + KWIN, width:], ge, NT)
                    for b, ge in zip(spans, ges)
                ]
                held["dv", g] = [mm(low_all[s, b], ge) for b, ge in zip(spans, ges)]

            return run

        def middle(g, spans):
            def run():
                ps = [low_all[s, b].astype(F32) for b in spans]
                ts = [p * gp for p, gp in zip(ps, held.pop(("gp", g)))]
                sums = [jnp.sum(t, axis=0, keepdims=True) for t in ts]
                dss = [t - p * total for p, t, total in zip(ps, ts, sums)]
                for b, ds in zip(spans, dss):
                    score_scr[b] += ds
                held["ds", g] = [ds.astype(BF16) for ds in dss]

            return run

        def products(g, spans):
            def run():
                lows = held.pop(("ds", g))
                q_exp = [expand(q_all[s, b * QBLK : (b + 1) * QBLK, :], masks) for b in spans]
                held["dk", g] = [mm(low, q) for low, q in zip(lows, q_exp)]
                held["dq", g] = [
                    mm(low, kv_all[s, b * QBLK : b * QBLK + KWIN, :width], TN)
                    for b, low in zip(spans, lows)
                ]

            return run

        def settle(g, spans):
            def run():
                for b, dk, dv in zip(spans, held.pop(("dk", g)), held.pop(("dv", g))):
                    merge(open_k, tiles(dk))
                    merge(open_v, tiles(dv))
                    close(b, 1)
                for b, dq in zip(spans, held.pop(("dq", g))):
                    d_all[s, b * QBLK : (b + 1) * QBLK, :width] = (
                        collapse(dq, lane_head) * scaling
                    ).astype(BF16)

            return run

        groups = [[g * BGROUP + w for w in range(BGROUP)] for g in range(blocks // BGROUP)]
        count = len(groups)
        for g in range(count + 2):
            for lag, make in enumerate((enter, middle)):
                if 0 <= g - lag < count:
                    stages.append(make(g - lag, groups[g - lag]))
            if 0 <= g - 1 < count:
                stages.append(products(g - 1, groups[g - 1]))
            if 0 <= g - 2 < count:
                stages.append(settle(g - 2, groups[g - 2]))
        stages.append(lambda: close(blocks, len(open_k)))
        return stages

    def weight_stages(s):
        cuts = 1
        chunk = rows // cuts

        def join():
            for side, at in ((0, 0), (1, rows - rim)):
                d_all[s, at : at + rim, width : 3 * width] = (
                    d_all[s, at : at + rim, width : 3 * width].astype(F32)
                    + edge_in[side, s].astype(F32)
                ).astype(BF16)

        def multiply(c):
            def run():
                hidden = hid_all[s, rim + c * chunk : rim + (c + 1) * chunk]
                gw_scr[...] += mm(hidden, d_all[s, c * chunk : (c + 1) * chunk], TN)

            return run

        return [join] + [multiply(c) for c in range(cuts)]

    def finish_stages(s):
        gain = gain_ref[...]
        stages = []
        cuts = 2
        chunk = rows // cuts
        held = {}

        def norm(c):
            def run():
                held[c] = layer_norm(again_ref[0, c * chunk : (c + 1) * chunk].astype(F32), gain)

            return run

        def multiply(c):
            def run():
                held["gh", c] = mm(d_all[s, c * chunk : (c + 1) * chunk], wall_scr[...], NT)

            return run

        def finish(c):
            def run():
                normed, inv_std, _ = held[c]
                gx = held["gh", c] * gain
                grad_ln = inv_std * (
                    gx
                    - jnp.mean(gx, axis=-1, keepdims=True)
                    - normed * jnp.mean(gx * normed, axis=-1, keepdims=True)
                )
                span = slice(c * chunk, (c + 1) * chunk)
                gatoms_ref[0, span] = (gupd_all[s, span].astype(F32) + grad_ln).astype(BF16)

            return run

        for c in range(cuts):
            stages += [norm(c), multiply(c)]
        for c in range(cuts):
            stages.append(finish(c))
        return stages

    @pl.when(step == 0)
    def _():
        barrier = pltpu.get_barrier_semaphore()
        for axis, count in axes:
            for d in range(1, count):
                pl.semaphore_signal(
                    barrier,
                    inc=1,
                    device_id={axis: shifted_index(axis, count, d)},
                    device_id_type=MESH,
                )

        pair_copy = pltpu.make_async_copy(pair_hbm, pair_ref, pair_sem.at[0])
        pair_copy.start()

        @pl.when(pos == 0)
        def _():
            low_in[...] = jnp.zeros_like(low_in)
            edge_in[0] = jnp.zeros_like(edge_in[0])

        @pl.when(pos == size - 1)
        def _():
            high_in[...] = jnp.zeros_like(high_in)
            edge_in[1] = jnp.zeros_like(edge_in[1])

        token = lax.broadcasted_iota(jnp.int32, (tokens, rows), 0)
        place = lax.broadcasted_iota(jnp.int32, (tokens, rows), 1)
        hit = (ids_ref[...] - pos * tokens == token) & (place < counts_ref[pos])
        member_t = jnp.where(hit, 1.0, 0.0).astype(F32)
        inv_scr[...] = 1.0 / jnp.sum(member_t, axis=1, keepdims=True)
        member_t_scr[...] = member_t.astype(BF16)
        member_scr[...] = member_t.T.astype(BF16)
        half_scr[...] = (0.5 * wt_ref[...].astype(F32)).astype(BF16)
        wqg_scr[:, :width] = wq_ref[...]
        wqg_scr[:, width:] = wg_ref[...]
        wkv_scr[:, :width] = wk_ref[...]
        wkv_scr[:, width:] = wv_ref[...]
        for n, ref in enumerate((wq_ref, wk_ref, wv_ref, wg_ref)):
            wall_scr[:, n * width : (n + 1) * width] = ref[...]
        for ref in (score_scr, gout_scr, gtok_scr, gw_scr):
            ref[...] = jnp.zeros_like(ref)
        pair_copy.wait()
        build_bias(
            counts_ref, pair_ref, pair_weights(wpair_ref, per), bias_scr, blocks, rows
        )
        pl.semaphore_wait(barrier, sum(count - 1 for _, count in axes))
        for part in range(len(halo_cuts)):
            launch(halo(part))
        outer, own, rest = forward_stages(0)
        weave(own)
        collect(halo(0))
        weave(outer + rest)

    for part in range(1, len(halo_cuts)):
        pl.when(step == halo_cuts[part][0])(lambda part=part: collect(halo(part)))

    @pl.when((step > 0) & (step < samples))
    def _():
        outer, own, rest = forward_stages(step)
        weave(token_stages(step - 1), outer + own + rest)

    @pl.when(step == samples)
    def _():
        weave(token_stages(samples - 1), backward_stages(0))

    @pl.when((step > samples) & (step < samples + LAG))
    def _():
        weave(backward_stages(step - samples))

    @pl.when((step >= samples + LAG) & (step < 2 * samples))
    def _():
        collect(edges(step - samples - LAG))
        weave(weight_stages(step - samples - LAG), backward_stages(step - samples))

    @pl.when((step >= samples) & (step < 2 * samples))
    def _():
        launch(edges(step - samples))

    @pl.when(step >= 2 * samples)
    def _():
        weave(finish_stages(step - 2 * samples))

    @pl.when(step == min(2 * samples + 3, last))
    def _():
        lines = pair_gradient(pair_ref, score_scr, per, pair_chunk, blocks)
        for n, line in enumerate(lines):
            small_src[0, n : n + 1, :] = line
        small_src[0, HEADS:, :] = jnp.zeros((8 - HEADS, width), F32)

    def fill_early():
        for n in range(gtok_scr.shape[1] // width):
            early_buf[n * width : (n + 1) * width, :] = gtok_scr[:, n * width : (n + 1) * width]
        at = gtok_scr.shape[1]
        early_buf[at : at + width, :] = gout_scr[...]
        early_buf[at + width :, :] = jnp.zeros((early_buf.shape[0] - at - width, width), F32)

    for n, action in enumerate(early.actions()):

        def run(n=n, action=action):
            if n == 0:
                fill_early()
            action()

        pl.when(step == min(samples + EARLY_AT[n], last))(run)

    def small_copies(k):
        axis, count = axes[k]
        base = 0 if k == 0 else axes[0][1] - 1
        return [
            pltpu.make_async_remote_copy(
                src_ref=small_src.at[k],
                dst_ref=(small_a, small_b)[k].at[d - 1],
                send_sem=small_send.at[base + d - 1],
                recv_sem=small_recv.at[base + d - 1],
                device_id={axis: shifted_index(axis, count, d)},
                device_id_type=MESH,
            )
            for d in range(1, count)
        ]

    def small_total(k):
        value = small_src[k]
        for n, copy in enumerate(small_copies(k)):
            copy.wait()
            value = value + (small_a, small_b)[k][n]
        return value

    def late_start():
        for s in range(samples - LAG, samples):
            collect(edges(s))
            weave(weight_stages(s))
        for n in range(4):
            late_buf[n * width : (n + 1) * width, :] = gw_scr[:, n * width : (n + 1) * width]
        if late_buf.shape[0] > 4 * width:
            late_buf[4 * width :, :] = jnp.zeros((late_buf.shape[0] - 4 * width, width), F32)
        late.scatter(0)

    def late_second():
        for copy in small_copies(0):
            copy.start()
        late.scatter(1)

    def late_third():
        late.gather(1)
        small_src[1] = small_total(0)
        for copy in small_copies(1):
            copy.start()

    def late_fourth():
        late.gather(0)
        small_ref[...] = small_total(1)

    def late_end():
        late.finish()
        early_ref[...] = early_sum[...]
        late_ref[...] = late_sum[...]

    late_actions = [late_start, late_second, late_third, late_fourth, late_end]
    for n, action in enumerate(late_actions):
        pl.when(step == min(2 * samples + LATE_AT[n], last))(action)


def unpack_kernel(
    channels,
    early_ref,
    late_ref,
    small_ref,
    gain_ref,
    wq_ref,
    wk_ref,
    wv_ref,
    wg_ref,
    pooled_ref,
    gatoms_ref,
    ggain_out,
    gq_out,
    gk_out,
    gv_out,
    gg_out,
    gout_out,
    gtok_out,
    gpair_out,
    pooled_out,
    gatoms_out,
    pooled_scr,
    gatoms_scr,
    sems,
):
    moves = []
    count = sems.shape[0] // 4
    for n, (src, mid, dst) in enumerate(
        ((pooled_ref, pooled_scr, pooled_out), (gatoms_ref, gatoms_scr, gatoms_out))
    ):
        size = src.shape[0] // count
        for c in range(count):
            span = pl.ds(c * size, size)
            at = 2 * (n * count + c)
            moves.append(
                (
                    pltpu.make_async_copy(src.at[span], mid.at[span], sems.at[at]),
                    pltpu.make_async_copy(mid.at[span], dst.at[span], sems.at[at + 1]),
                )
            )
    for fetch, _ in moves:
        fetch.start()
    width = gout_out.shape[0]
    blocks = gtok_out.shape[1] // width

    def block(ref, n):
        return ref[n * width : (n + 1) * width, :].astype(F32)

    for fetch, put in moves:
        fetch.wait()
        put.start()
    for n in range(blocks):
        gtok_out[:, n * width : (n + 1) * width] = block(early_ref, n)
    gout_out[...] = block(early_ref, blocks)
    by_gain = None
    weights = (wq_ref, wk_ref, wv_ref, wg_ref)
    for n, (ref, weight) in enumerate(zip((gq_out, gk_out, gv_out, gg_out), weights)):
        grad = block(late_ref, n)
        ref[...] = grad
        part = grad * weight[...].astype(F32)
        by_gain = part if by_gain is None else by_gain + part
    ggain_out[...] = jnp.sum(by_gain.T, axis=0, keepdims=True) / gain_ref[...]
    lines = small_ref[...]
    shift = width // 2
    while shift >= channels:
        lines = lines + pltpu.roll(lines, shift, 1)
        shift //= 2
    gpair_out[...] = lines[:HEADS, :channels]
    for _, put in moves:
        put.wait()


def whole(*shape):
    return pl.BlockSpec(shape, lambda s: (0,) * len(shape))


def sum_scratch(total, streams, orders, width):
    unit = total // streams
    slots = []
    for stream in range(streams):
        length = unit
        for _, size in orders[stream]:
            length //= size
            slots.append(pltpu.VMEM((size - 1, length, width), BF16))
    return slots * 2


def on_device(
    atoms,
    gain,
    w_query,
    w_key,
    w_value,
    w_gate,
    w_out,
    w_token,
    w_pair,
    pair_cond,
    counts,
    membership,
    pooled_cot,
):
    samples, rows, width = atoms.shape
    blocks = rows // QBLK
    rim = (KWIN - QBLK) // 2
    tokens, token_width = pooled_cot.shape[1:]
    channels = w_pair.shape[0]
    pair2 = pair_cond.reshape(blocks * QBLK, pair_cond.shape[-1])
    gain2 = gain.reshape(1, width)
    ids2 = membership.reshape(1, rows)
    square = whole(width, width)
    shape = jax.ShapeDtypeStruct
    vmem = pltpu.VMEM
    dma = pltpu.SemaphoreType.DMA

    axes = axis_sizes()
    devices = axes[0][1] * axes[1][1]
    peers = sum(size - 1 for _, size in axes)
    unit = 16 * devices
    early_total = -(-(token_width + width) // unit) * unit
    late_total = -(-(4 * width) // unit) * unit
    early_streams = early_total // unit
    late_streams = late_total // unit
    early_orders = [axes] * early_streams

    def clip(x):
        return jnp.clip(x, 0, samples - 1)

    def again(i):
        return jnp.where(i <= samples, clip(i - 1), clip(i - 2 * samples))

    pooled, gatoms, early, late, small = pl.pallas_call(
        functools.partial(step_kernel, samples, early_streams, late_streams),
        grid=(3 * samples,),
        in_specs=[
            pl.BlockSpec(memory_space=pltpu.SMEM),
            pl.BlockSpec(memory_space=pl.ANY),
            pl.BlockSpec((1, rows, width), lambda i: (clip(i), 0, 0)),
            pl.BlockSpec((1, rows, width), lambda i: (again(i), 0, 0)),
            whole(1, width),
            square,
            square,
            square,
            square,
            square,
            whole(width, token_width),
            whole(*w_pair.T.shape),
            pl.BlockSpec(memory_space=pl.ANY),
            whole(1, rows),
            pl.BlockSpec((1, tokens, token_width), lambda i: (clip(i - 1), 0, 0)),
        ],
        out_specs=[
            pl.BlockSpec((1, tokens, token_width), lambda i: (clip(i - 1), 0, 0)),
            pl.BlockSpec((1, rows, width), lambda i: (clip(i - 2 * samples), 0, 0)),
            whole(early_total, width),
            whole(late_total, width),
            whole(8, width),
        ],
        out_shape=[
            shape((samples, tokens, token_width), BF16),
            shape((samples, rows, width), BF16),
            shape((early_total, width), BF16),
            shape((late_total, width), BF16),
            shape((8, width), F32),
        ],
        scratch_shapes=[
            vmem((samples, rim, width), BF16),
            vmem((samples, rim, width), BF16),
            vmem((2, samples, rim, 2 * width), BF16),
            vmem((2, samples, rim, 2 * width), BF16),
            vmem(pair2.shape, BF16),
            vmem((blocks, KWIN, LANES), F32),
            vmem((blocks, KWIN, LANES), F32),
            vmem((rows, tokens), BF16),
            vmem((tokens, rows), BF16),
            vmem((tokens, 1), F32),
            vmem((width, 2 * width), BF16),
            vmem((width, 2 * width), BF16),
            vmem((width, 4 * width), BF16),
            vmem((width, token_width), BF16),
            vmem((samples, rows + 2 * rim, width), BF16),
            vmem((rows, width), F32),
            vmem((2, rows, width), BF16),
            vmem((2, 2, rows, width), F32),
            vmem((samples, rows, width), BF16),
            vmem((samples, rows + 2 * rim, 2 * width), BF16),
            vmem((samples, blocks, KWIN, LANES), BF16),
            vmem((samples, rows, width), BF16),
            vmem((samples, rows, width), BF16),
            vmem((samples, rows, 4 * width), BF16),
            vmem((width, width), F32),
            vmem((width, token_width), F32),
            vmem((width, 4 * width), F32),
            vmem((early_total, width), F32),
            vmem((late_total, width), F32),
            vmem((early_total, width), BF16),
            vmem((late_total, width), BF16),
            vmem((axes[0][1] - 1, 8, width), F32),
            vmem((axes[1][1] - 1, 8, width), F32),
            vmem((2, 8, width), F32),
            dma((2, 3)),
            dma((2, 3)),
            dma((2, samples)),
            dma((2, samples)),
            dma((2 * early_streams * peers,)),
            dma((2 * early_streams * peers,)),
            dma((2 * late_streams * peers,)),
            dma((2 * late_streams * peers,)),
            dma((peers,)),
            dma((peers,)),
            dma((1,)),
        ]
        + sum_scratch(early_total, early_streams, early_orders, width)
        + sum_scratch(late_total, late_streams, [axes] * late_streams, width),
        compiler_params=pltpu.CompilerParams(
            dimension_semantics=("arbitrary",),
            vmem_limit_bytes=56 * 1024 * 1024,
            collective_id=0,
            has_side_effects=True,
        ),
    )(
        counts,
        atoms,
        atoms,
        atoms,
        gain2,
        w_query,
        w_key,
        w_value,
        w_gate,
        w_out,
        w_token,
        w_pair.T,
        pair2,
        ids2,
        pooled_cot,
    )
    spec = pl.BlockSpec(memory_space=pltpu.VMEM)
    anywhere = pl.BlockSpec(memory_space=pl.ANY)
    pieces = next(n for n in (4, 3, 2, 1) if samples % n == 0)
    ggain, gq, gk, gv, gg, gout, gtok, gpair, pooled, gatoms = pl.pallas_call(
        functools.partial(unpack_kernel, channels),
        in_specs=[spec] * 8 + [anywhere] * 2,
        out_specs=[spec] * 8 + [anywhere] * 2,
        out_shape=[shape((1, width), F32)]
        + [shape((width, width), F32)] * 5
        + [shape((width, token_width), F32), shape((HEADS, channels), F32)]
        + [shape(pooled.shape, BF16), shape(gatoms.shape, BF16)],
        scratch_shapes=[vmem(pooled.shape, BF16), vmem(gatoms.shape, BF16), dma((4 * pieces,))],
    )(early, late, small, gain2, w_query, w_key, w_value, w_gate, pooled, gatoms)
    return (pooled, gatoms, ggain.reshape(width), gq, gk, gv, gg, gout, gtok, gpair.T)


def solution(mesh):
    placed = (
        P("samp", "seq", None),
        P(),
        P(),
        P(),
        P(),
        P(),
        P(),
        P(),
        P(),
        P("seq", None, None),
        P(),
        P("seq"),
        P("samp", "seq", None),
    )
    return jax.shard_map(
        on_device,
        mesh=mesh,
        in_specs=placed,
        out_specs=(
            P("samp", "seq", None),
            P("samp", "seq", None),
            P(),
            P(),
            P(),
            P(),
            P(),
            P(),
            P(),
            P(),
        ),
        check_vma=False,
    )
```

```python
import functools

import jax
import jax.numpy as jnp
from jax import lax
from jax.experimental import pallas as pl
from jax.experimental.pallas import tpu as pltpu
from jax.sharding import PartitionSpec as P

HEADS = 4
QBLK = 32
KWIN = 128
LOG2E = 1.4426950408889634

epsilon = 1e-05
F32 = jnp.float32
BF16 = jnp.bfloat16
NN = (((1,), (0,)), ((), ()))
NT = (((1,), (1,)), ((), ()))
TN = (((0,), (0,)), ((), ()))
GROUP = 4
FGROUP = 8
PARTS = 1
BGROUP = 8
LANES = 128
MESH = pl.DeviceIdType.MESH
LAG = 3
EARLY_AT = (1, 4, 8, 12, 1 << 20)
LATE_AT = (2, 5, 7, 9, 1 << 20)


def mm(a, b, dims=NN):
    return lax.dot_general(a, b, dims, preferred_element_type=F32)


def sigmoid(x):
    return 0.5 * jnp.tanh(0.5 * x) + 0.5


def layer_norm(x, gain):
    centred = x - jnp.mean(x, axis=-1, keepdims=True)
    variance = jnp.mean(centred * centred, axis=-1, keepdims=True)
    inv_std = lax.rsqrt(variance + epsilon)
    normed = centred * inv_std
    return normed, inv_std, (normed * gain).astype(BF16)


def head_lanes(width):
    lane = lax.broadcasted_iota(jnp.int32, (1, width), 1)
    return lane // (width // HEADS)


def expand(block, masks):
    return jnp.concatenate([block * m for m in masks], axis=0)


def collapse(wide, lane_head):
    rows = wide.shape[0] // HEADS
    out = wide[:rows]
    for h in range(1, HEADS):
        out = jnp.where(lane_head == h, wide[h * rows : (h + 1) * rows], out)
    return out


def lane_swap(parts, lane_block):
    count = len(parts)
    outs = []
    for b in range(count):
        out = None
        for a in range(count):
            shift = (QBLK * (a - b)) % LANES
            moved = parts[a] if shift == 0 else pltpu.roll(parts[a], shift, 1)
            out = moved if out is None else jnp.where(lane_block == a, moved, out)
        outs.append(out)
    return outs


def pair_weights(wpair_ref, per):
    channels = wpair_ref.shape[1]
    high, wide = HEADS * per, per * channels
    row = lax.broadcasted_iota(jnp.int32, (high, HEADS), 0) // per
    head = lax.broadcasted_iota(jnp.int32, (high, HEADS), 1)
    pick = jnp.where(row == head, 1.0, 0.0).astype(BF16)
    by_row = mm(pick, wpair_ref[...]).astype(BF16)
    lane = lax.rem(lax.broadcasted_iota(jnp.int32, (channels, wide), 1), channels)
    chan = lax.broadcasted_iota(jnp.int32, (channels, wide), 0)
    spread = mm(by_row, jnp.where(lane == chan, 1.0, 0.0).astype(BF16))
    key = lax.rem(lax.broadcasted_iota(jnp.int32, (high, wide), 0), per)
    spot = lax.broadcasted_iota(jnp.int32, (high, wide), 1) // channels
    return jnp.where(key == spot, spread, 0.0).astype(BF16)


def build_bias(counts_ref, pair_ref, wsm, bias_scr, blocks, rows):
    pos = lax.axis_index("seq")
    size = lax.axis_size("seq")
    own = counts_ref[pos]
    left = jnp.where(pos > 0, counts_ref[jnp.maximum(pos - 1, 0)], 0)
    right = jnp.where(pos < size - 1, counts_ref[jnp.minimum(pos + 1, size - 1)], 0)
    rim = (KWIN - QBLK) // 2
    lane_block = head_lanes(LANES)
    chunk = wsm.shape[1]
    per = wsm.shape[0] // HEADS
    for kk in range(pair_ref.shape[1] // chunk):
        biased = mm(wsm, pair_ref[:, kk * chunk : (kk + 1) * chunk], NT)
        for g in range(blocks // GROUP):
            parts = [
                biased[h * per : (h + 1) * per, g * LANES : (g + 1) * LANES] for h in range(HEADS)
            ]
            for w, out in enumerate(lane_swap(parts, lane_block)):
                b = g * GROUP + w
                slot = (
                    lax.broadcasted_iota(jnp.int32, (per, LANES), 0) + kk * per + b * QBLK - rim
                )
                alive = (
                    ((slot < 0) & (slot + rows < left))
                    | ((slot >= 0) & (slot < own))
                    | ((slot >= rows) & (slot - rows < right))
                )
                bias_scr[b, kk * per : (kk + 1) * per, :] = jnp.where(alive, out * LOG2E, -1e30)


def pair_gradient(pair_ref, score_scr, per, chunk, blocks):
    lane_block = head_lanes(LANES)
    total = None
    for kk in range(pair_ref.shape[1] // chunk):
        columns = []
        for g in range(blocks // GROUP):
            parts = [score_scr[g * GROUP + w, kk * per : (kk + 1) * per, :] for w in range(GROUP)]
            columns.append(jnp.concatenate(lane_swap(parts, lane_block), axis=0))
        grads = jnp.concatenate(columns, axis=1).astype(BF16)
        part = mm(grads, pair_ref[:, kk * chunk : (kk + 1) * chunk])
        total = part if total is None else total + part
    high, wide = total.shape
    row = lax.broadcasted_iota(jnp.int32, (high, wide), 0)
    lane = lax.broadcasted_iota(jnp.int32, (high, wide), 1)
    diagonal = jnp.where(lax.rem(row, per) == lane // (wide // per), total, 0.0)
    lines = []
    for h in range(HEADS):
        line = jnp.sum(diagonal[h * per : (h + 1) * per], axis=0, keepdims=True)
        folded = line[:, :LANES]
        for n in range(1, wide // LANES):
            folded = folded + line[:, n * LANES : (n + 1) * LANES]
        lines.append(folded)
    return lines


def weave(*lists):
    lists = [x for x in lists if x]
    done = [0] * len(lists)
    while True:
        best = None
        for n, x in enumerate(lists):
            if done[n] < len(x):
                share = (done[n] + 0.5) / len(x)
                if best is None or share < best[0]:
                    best = (share, n)
        if best is None:
            return
        n = best[1]
        lists[n][done[n]]()
        done[n] += 1


def axis_sizes():
    return [(axis, lax.axis_size(axis)) for axis in ("samp", "seq")]


def shifted_index(axis, size, distance):
    return lax.rem(lax.axis_index(axis) + distance, size)


class Summer:
    def __init__(self, buf, out, streams, orders, send_sem, recv_sem, slots):
        self.buf, self.out, self.streams, self.orders = buf, out, streams, orders
        self.send_sem, self.recv_sem = send_sem, recv_sem
        self.sends, self.recvs = slots[: 2 * streams], slots[2 * streams :]
        self.unit = buf.shape[0] // streams
        self.peers = sum(size - 1 for _, size in orders[0])

    def spans(self, stream):
        (a0, s0), (a1, s1) = self.orders[stream]
        off0 = stream * self.unit
        len1 = self.unit // s0
        len2 = len1 // s1
        off1 = off0 + lax.axis_index(a0) * len1
        off2 = off1 + lax.axis_index(a1) * len2
        return [(off0, self.unit), (off1, len1), (off2, len2)]

    def copy(self, stream, src, dst, slot, partner):
        at = stream * 2 * self.peers + slot
        return pltpu.make_async_remote_copy(
            src_ref=src,
            dst_ref=dst,
            send_sem=self.send_sem.at[at],
            recv_sem=self.recv_sem.at[at],
            device_id=partner,
            device_id_type=MESH,
        )

    def scatter_copies(self, stream, k):
        axis, size = self.orders[stream][k]
        base = 0 if k == 0 else self.orders[stream][0][1] - 1
        return [
            self.copy(
                stream,
                self.sends[2 * stream + k].at[d - 1],
                self.recvs[2 * stream + k].at[d - 1],
                base + d - 1,
                {axis: shifted_index(axis, size, d)},
            )
            for d in range(1, size)
        ]

    def gather_copies(self, stream, k):
        axis, size = self.orders[stream][k]
        base = self.peers + (0 if k == 1 else self.orders[stream][1][1] - 1)
        off, length = self.spans(stream)[k + 1]
        part = self.out.at[pl.ds(pl.multiple_of(off, 16), length), :]
        return [
            self.copy(stream, part, part, base + d - 1, {axis: shifted_index(axis, size, d)})
            for d in range(1, size)
        ]

    def scatter(self, k):
        for stream in range(self.streams):
            spans = self.spans(stream)
            axis, size = self.orders[stream][k]
            if k > 0:
                off, length = spans[k]
                rows = pl.ds(pl.multiple_of(off, 16), length)
                self.buf[rows, :] = self.absorbed(stream, k - 1)
            off, length = spans[k][0], spans[k + 1][1]
            for d, copy in enumerate(self.scatter_copies(stream, k), 1):
                give = pl.multiple_of(off + shifted_index(axis, size, d) * length, 16)
                self.sends[2 * stream + k][d - 1] = self.buf[pl.ds(give, length), :].astype(BF16)
                copy.start()

    def absorbed(self, stream, k):
        off, length = self.spans(stream)[k + 1]
        value = self.buf[pl.ds(pl.multiple_of(off, 16), length), :]
        for n, copy in enumerate(self.scatter_copies(stream, k)):
            copy.wait()
            value = value + self.recvs[2 * stream + k][n].astype(F32)
        return value

    def gather(self, k):
        for stream in range(self.streams):
            if k == 1:
                off, length = self.spans(stream)[2]
                rows = pl.ds(pl.multiple_of(off, 16), length)
                self.out[rows, :] = self.absorbed(stream, 1).astype(BF16)
            else:
                for copy in self.gather_copies(stream, 1):
                    copy.wait()
            for copy in self.gather_copies(stream, k):
                copy.start()

    def finish(self):
        for stream in range(self.streams):
            for copy in self.gather_copies(stream, 0):
                copy.wait()

    def actions(self):
        return [
            lambda: self.scatter(0),
            lambda: self.scatter(1),
            lambda: self.gather(1),
            lambda: self.gather(0),
            self.finish,
        ]


def step_kernel(
    samples,
    early_streams,
    late_streams,
    counts_ref,
    atoms_hbm,
    atoms_ref,
    again_ref,
    gain_ref,
    wq_ref,
    wk_ref,
    wv_ref,
    wg_ref,
    wo_ref,
    wt_ref,
    wpair_ref,
    pair_hbm,
    ids_ref,
    cot_ref,
    pooled_ref,
    gatoms_ref,
    early_ref,
    late_ref,
    small_ref,
    low_in,
    high_in,
    edge_out,
    edge_in,
    pair_ref,
    bias_scr,
    score_scr,
    member_scr,
    member_t_scr,
    inv_scr,
    wqg_scr,
    wkv_scr,
    wall_scr,
    half_scr,
    hid_all,
    gate_scr,
    gated_scr,
    back_scr,
    q_all,
    kv_all,
    low_all,
    gatt_all,
    gupd_all,
    d_all,
    gout_scr,
    gtok_scr,
    gw_scr,
    early_buf,
    late_buf,
    early_sum,
    late_sum,
    small_a,
    small_b,
    small_src,
    halo_send,
    halo_recv,
    edge_send,
    edge_recv,
    early_send,
    early_recv,
    late_send,
    late_recv,
    small_send,
    small_recv,
    pair_sem,
    *slots,
):
    step = pl.program_id(0)
    rows, width = q_all.shape[1:]
    blocks = rows // QBLK
    rim = (KWIN - QBLK) // 2
    tokens = inv_scr.shape[0]
    per = 2 * LANES // wpair_ref.shape[1]
    pair_chunk = per * wpair_ref.shape[1]
    scaling = (width // HEADS) ** (-0.5)
    lane_head = head_lanes(width)
    masks = [(lane_head == h).astype(F32).astype(BF16) for h in range(HEADS)]
    axes = axis_sizes()
    pos = lax.axis_index("seq")
    size = lax.axis_size("seq")
    last = 3 * samples - 1

    early_orders = [axes] * early_streams
    early = Summer(
        early_buf,
        early_sum,
        early_streams,
        early_orders,
        early_send,
        early_recv,
        slots[: 4 * early_streams],
    )
    late = Summer(
        late_buf,
        late_sum,
        late_streams,
        [axes] * late_streams,
        late_send,
        late_recv,
        slots[4 * early_streams :],
    )

    def to_right(src, dst, send_sem, recv_sem):
        return pltpu.make_async_remote_copy(
            src_ref=src,
            dst_ref=dst,
            send_sem=send_sem,
            recv_sem=recv_sem,
            device_id={"seq": jnp.minimum(pos + 1, size - 1)},
            device_id_type=MESH,
        )

    def to_left(src, dst, send_sem, recv_sem):
        return pltpu.make_async_remote_copy(
            src_ref=src,
            dst_ref=dst,
            send_sem=send_sem,
            recv_sem=recv_sem,
            device_id={"seq": jnp.maximum(pos - 1, 0)},
            device_id_type=MESH,
        )

    halo_cuts = ((0, 1), (1, 2), (3, samples - 3))

    def halo(part):
        first, count = halo_cuts[part]
        span = pl.ds(first, count)
        right = to_right(
            atoms_hbm.at[span, rows - rim : rows, :],
            low_in.at[span],
            halo_send.at[0, part],
            halo_recv.at[0, part],
        )
        left = to_left(
            atoms_hbm.at[span, 0:rim, :],
            high_in.at[span],
            halo_send.at[1, part],
            halo_recv.at[1, part],
        )
        return right, left

    def edges(j):
        right = to_right(
            edge_out.at[1, j], edge_in.at[0, j], edge_send.at[0, j], edge_recv.at[0, j]
        )
        left = to_left(
            edge_out.at[0, j], edge_in.at[1, j], edge_send.at[1, j], edge_recv.at[1, j]
        )
        return right, left

    def launch(pair):
        right, left = pair

        @pl.when(pos < size - 1)
        def _():
            right.start()

        @pl.when(pos > 0)
        def _():
            left.start()

    def collect(pair):
        right, left = pair

        @pl.when(pos < size - 1)
        def _():
            right.wait_send()
            left.wait_recv()

        @pl.when(pos > 0)
        def _():
            left.wait_send()
            right.wait_recv()

    def forward_stages(s):
        slot = lax.rem(s, 2)
        gain = gain_ref[...]
        stages = []
        held = {}
        cuts = 4
        chunk = rows // cuts

        def rims():
            hid_all[s, :rim] = layer_norm(low_in[s].astype(F32), gain)[2]
            hid_all[s, rim + rows :] = layer_norm(high_in[s].astype(F32), gain)[2]
            kv_all[s, :rim] = mm(hid_all[s, :rim], wkv_scr[...]).astype(BF16)
            kv_all[s, rim + rows :] = mm(hid_all[s, rim + rows :], wkv_scr[...]).astype(BF16)

        def norm(c):
            def run():
                x = atoms_ref[0, c * chunk : (c + 1) * chunk].astype(F32)
                hid_all[s, rim + c * chunk : rim + (c + 1) * chunk] = layer_norm(x, gain)[2]

            return run

        def project(c):
            def run():
                span = slice(c * chunk, (c + 1) * chunk)
                hidden = hid_all[s, rim + c * chunk : rim + (c + 1) * chunk]
                kv_all[s, rim + c * chunk : rim + (c + 1) * chunk] = mm(
                    hidden, wkv_scr[...]
                ).astype(BF16)
                qg = mm(hidden, wqg_scr[...])
                q_all[s, span] = qg[:, :width].astype(BF16)
                gate_scr[span] = sigmoid(qg[:, width:])

            return run

        def score(g, spans):
            def run():
                q_exp = [expand(q_all[s, b * QBLK : (b + 1) * QBLK, :], masks) for b in spans]
                held[g] = [
                    mm(kv_all[s, b * QBLK : b * QBLK + KWIN, :width], q, NT)
                    for b, q in zip(spans, q_exp)
                ]

            return run

        def soften(g, spans):
            def run():
                es = [
                    jnp.exp2(sc * (scaling * LOG2E) + bias_scr[b])
                    for b, sc in zip(spans, held.pop(g))
                ]
                invs = [1.0 / jnp.sum(e, axis=0, keepdims=True) for e in es]
                for b, e, inv in zip(spans, es, invs):
                    low_all[s, b] = (e * inv).astype(BF16)

            return run

        def attend(spans):
            def run():
                wide = [
                    mm(low_all[s, b], kv_all[s, b * QBLK : b * QBLK + KWIN, width:], TN)
                    for b in spans
                ]
                for b, o in zip(spans, wide):
                    span = slice(b * QBLK, (b + 1) * QBLK)
                    att = collapse(o, lane_head)
                    gate = gate_scr[span]
                    gated = gate * att
                    gated_scr[slot, span] = gated.astype(BF16)
                    back_scr[slot, 0, span] = gate
                    back_scr[slot, 1, span] = gated * (1.0 - gate)

            return run

        stages.append(norm(0))
        for c in range(cuts):
            if c + 1 < cuts:
                stages.append(norm(c + 1))
            stages.append(project(c))
        own = len(stages)
        groups = [[g * FGROUP + w for w in range(FGROUP)] for g in range(blocks // FGROUP)]
        count = len(groups)
        for g in range(count + 2):
            if g < count:
                stages.append(score(g, groups[g]))
            if 0 <= g - 1 < count:
                stages.append(soften(g - 1, groups[g - 1]))
            if 0 <= g - 2 < count:
                stages.append(attend(groups[g - 2]))
        return [rims], stages[:own], stages[own:]

    def token_stages(s):
        slot = lax.rem(s, 2)
        chunk = 256
        half = rows // 2
        held = {}
        stages = []

        def begin():
            gated = gated_scr[slot]
            x = again_ref[0].astype(F32)
            held["updated"] = (x + mm(gated, wo_ref[...])).astype(BF16)
            held["cot"] = (cot_ref[0].astype(F32) * (0.5 * inv_scr[...])).astype(BF16)
            held["gupd"] = [None, None]

        def enter(c, r):
            def run():
                cols = slice(c * chunk, (c + 1) * chunk)
                span = slice(r * half, (r + 1) * half)
                held[c, r] = (
                    mm(held["updated"][span], half_scr[:, cols]),
                    mm(member_scr[span, :], held["cot"][:, cols]),
                    [],
                    [],
                )

            return run

        def act(c, r, n):
            def run():
                pre, grad_act, acts, grads = held[c, r]
                part = slice(n * half // PARTS, (n + 1) * half // PARTS)
                pre, grad_act = pre[part], grad_act[part]
                bent = jnp.tanh(pre)
                rise = 1.0 + bent
                value = pre * rise
                acts.append(value.astype(BF16))
                grads.append((grad_act * (rise + value * (1.0 - bent))).astype(BF16))

            return run

        def leave(c, r):
            def run():
                _, _, acts, grads = held.pop((c, r))
                cols = slice(c * chunk, (c + 1) * chunk)
                span = slice(r * half, (r + 1) * half)
                grad_pre = jnp.concatenate(grads, axis=0)
                pooled = mm(member_t_scr[:, span], jnp.concatenate(acts, axis=0))
                gtok = mm(held["updated"][span], grad_pre, TN)
                part = mm(grad_pre, wt_ref[:, cols], NT)
                if r == 0:
                    held["pooled"], held["gtok"] = pooled, gtok
                else:
                    pooled_ref[0, :, cols] = ((held["pooled"] + pooled) * inv_scr[...]).astype(BF16)
                    gtok_scr[:, cols] += held["gtok"] + gtok
                before = held["gupd"][r]
                held["gupd"][r] = part if before is None else before + part

            return run

        def end():
            grad_updated = jnp.concatenate(held["gupd"], axis=0).astype(BF16)
            gupd_all[s] = grad_updated
            gout_scr[...] += mm(gated_scr[slot], grad_updated, TN)
            grad_gated = mm(grad_updated, wo_ref[...], NT)
            gatt_all[s] = (grad_gated * back_scr[slot, 0]).astype(BF16)
            d_all[s, :, 3 * width :] = (grad_gated * back_scr[slot, 1]).astype(BF16)

        stages.append(begin)
        pieces = [(c, r) for c in range(wt_ref.shape[1] // chunk) for r in range(2)]
        for n in range(len(pieces) + 1):
            if n < len(pieces):
                stages.append(enter(*pieces[n]))
            if n > 0:
                for part in range(PARTS):
                    stages.append(act(*pieces[n - 1], part))
                stages.append(leave(*pieces[n - 1]))
        stages.append(end)
        return stages

    def backward_stages(s):
        open_k = []
        open_v = []
        held = {}
        stages = []

        def tiles(x):
            return [x[n * QBLK : (n + 1) * QBLK] for n in range(KWIN // QBLK)]

        def store(at, k, v):
            if at < rim:
                edge_out[0, s, at : at + k.shape[0], :width] = k
                edge_out[0, s, at : at + k.shape[0], width:] = v
            elif at < rim + rows:
                d_all[s, at - rim : at - rim + k.shape[0], width : 2 * width] = k
                d_all[s, at - rim : at - rim + k.shape[0], 2 * width : 3 * width] = v
            else:
                at = at - rim - rows
                edge_out[1, s, at : at + k.shape[0], :width] = k
                edge_out[1, s, at : at + k.shape[0], width:] = v

        def close(first, count):
            for n in range(count):
                at = (first + n) * QBLK
                k = (open_k[n] * scaling).astype(BF16)
                v = open_v[n].astype(BF16)
                half = QBLK // 2
                store(at, k[:half], v[:half])
                store(at + half, k[half:], v[half:])
            del open_k[:count]
            del open_v[:count]

        def merge(opened, parts):
            for n, part in enumerate(parts):
                if n < len(opened):
                    opened[n] = opened[n] + part
                else:
                    opened.append(part)

        def enter(g, spans):
            def run():
                ges = [expand(gatt_all[s, b * QBLK : (b + 1) * QBLK, :], masks) for b in spans]
                held["gp", g] = [
                    mm(kv_all[s, b * QBLK : b * QBLK + KWIN, width:], ge, NT)
                    for b, ge in zip(spans, ges)
                ]
                held["dv", g] = [mm(low_all[s, b], ge) for b, ge in zip(spans, ges)]

            return run

        def middle(g, spans):
            def run():
                ps = [low_all[s, b].astype(F32) for b in spans]
                ts = [p * gp for p, gp in zip(ps, held.pop(("gp", g)))]
                sums = [jnp.sum(t, axis=0, keepdims=True) for t in ts]
                dss = [t - p * total for p, t, total in zip(ps, ts, sums)]
                for b, ds in zip(spans, dss):
                    score_scr[b] += ds
                held["ds", g] = [ds.astype(BF16) for ds in dss]

            return run

        def products(g, spans):
            def run():
                lows = held.pop(("ds", g))
                q_exp = [expand(q_all[s, b * QBLK : (b + 1) * QBLK, :], masks) for b in spans]
                held["dk", g] = [mm(low, q) for low, q in zip(lows, q_exp)]
                held["dq", g] = [
                    mm(low, kv_all[s, b * QBLK : b * QBLK + KWIN, :width], TN)
                    for b, low in zip(spans, lows)
                ]

            return run

        def settle(g, spans):
            def run():
                for b, dk, dv in zip(spans, held.pop(("dk", g)), held.pop(("dv", g))):
                    merge(open_k, tiles(dk))
                    merge(open_v, tiles(dv))
                    close(b, 1)
                for b, dq in zip(spans, held.pop(("dq", g))):
                    d_all[s, b * QBLK : (b + 1) * QBLK, :width] = (
                        collapse(dq, lane_head) * scaling
                    ).astype(BF16)

            return run

        groups = [[g * BGROUP + w for w in range(BGROUP)] for g in range(blocks // BGROUP)]
        count = len(groups)
        for g in range(count + 2):
            for lag, make in enumerate((enter, middle)):
                if 0 <= g - lag < count:
                    stages.append(make(g - lag, groups[g - lag]))
            if 0 <= g - 1 < count:
                stages.append(products(g - 1, groups[g - 1]))
            if 0 <= g - 2 < count:
                stages.append(settle(g - 2, groups[g - 2]))
        stages.append(lambda: close(blocks, len(open_k)))
        return stages

    def weight_stages(s):
        cuts = 1
        chunk = rows // cuts

        def join():
            for side, at in ((0, 0), (1, rows - rim)):
                d_all[s, at : at + rim, width : 3 * width] = (
                    d_all[s, at : at + rim, width : 3 * width].astype(F32)
                    + edge_in[side, s].astype(F32)
                ).astype(BF16)

        def multiply(c):
            def run():
                hidden = hid_all[s, rim + c * chunk : rim + (c + 1) * chunk]
                gw_scr[...] += mm(hidden, d_all[s, c * chunk : (c + 1) * chunk], TN)

            return run

        return [join] + [multiply(c) for c in range(cuts)]

    def finish_stages(s):
        gain = gain_ref[...]
        stages = []
        cuts = 2
        chunk = rows // cuts
        held = {}

        def norm(c):
            def run():
                held[c] = layer_norm(again_ref[0, c * chunk : (c + 1) * chunk].astype(F32), gain)

            return run

        def multiply(c):
            def run():
                held["gh", c] = mm(d_all[s, c * chunk : (c + 1) * chunk], wall_scr[...], NT)

            return run

        def finish(c):
            def run():
                normed, inv_std, _ = held[c]
                gx = held["gh", c] * gain
                grad_ln = inv_std * (
                    gx
                    - jnp.mean(gx, axis=-1, keepdims=True)
                    - normed * jnp.mean(gx * normed, axis=-1, keepdims=True)
                )
                span = slice(c * chunk, (c + 1) * chunk)
                gatoms_ref[0, span] = (gupd_all[s, span].astype(F32) + grad_ln).astype(BF16)

            return run

        for c in range(cuts):
            stages += [norm(c), multiply(c)]
        for c in range(cuts):
            stages.append(finish(c))
        return stages

    @pl.when(step == 0)
    def _():
        barrier = pltpu.get_barrier_semaphore()
        for axis, count in axes:
            for d in range(1, count):
                pl.semaphore_signal(
                    barrier,
                    inc=1,
                    device_id={axis: shifted_index(axis, count, d)},
                    device_id_type=MESH,
                )

        pair_copy = pltpu.make_async_copy(pair_hbm, pair_ref, pair_sem.at[0])
        pair_copy.start()

        @pl.when(pos == 0)
        def _():
            low_in[...] = jnp.zeros_like(low_in)
            edge_in[0] = jnp.zeros_like(edge_in[0])

        @pl.when(pos == size - 1)
        def _():
            high_in[...] = jnp.zeros_like(high_in)
            edge_in[1] = jnp.zeros_like(edge_in[1])

        token = lax.broadcasted_iota(jnp.int32, (tokens, rows), 0)
        place = lax.broadcasted_iota(jnp.int32, (tokens, rows), 1)
        hit = (ids_ref[...] - pos * tokens == token) & (place < counts_ref[pos])
        member_t = jnp.where(hit, 1.0, 0.0).astype(F32)
        inv_scr[...] = 1.0 / jnp.sum(member_t, axis=1, keepdims=True)
        member_t_scr[...] = member_t.astype(BF16)
        member_scr[...] = member_t.T.astype(BF16)
        half_scr[...] = (0.5 * wt_ref[...].astype(F32)).astype(BF16)
        wqg_scr[:, :width] = wq_ref[...]
        wqg_scr[:, width:] = wg_ref[...]
        wkv_scr[:, :width] = wk_ref[...]
        wkv_scr[:, width:] = wv_ref[...]
        for n, ref in enumerate((wq_ref, wk_ref, wv_ref, wg_ref)):
            wall_scr[:, n * width : (n + 1) * width] = ref[...]
        for ref in (score_scr, gout_scr, gtok_scr, gw_scr):
            ref[...] = jnp.zeros_like(ref)
        pair_copy.wait()
        build_bias(
            counts_ref, pair_ref, pair_weights(wpair_ref, per), bias_scr, blocks, rows
        )
        pl.semaphore_wait(barrier, sum(count - 1 for _, count in axes))
        for part in range(len(halo_cuts)):
            launch(halo(part))
        outer, own, rest = forward_stages(0)
        weave(own)
        collect(halo(0))
        weave(outer + rest)

    for part in range(1, len(halo_cuts)):
        pl.when(step == halo_cuts[part][0])(lambda part=part: collect(halo(part)))

    @pl.when((step > 0) & (step < samples))
    def _():
        outer, own, rest = forward_stages(step)
        weave(token_stages(step - 1), outer + own + rest)

    @pl.when(step == samples)
    def _():
        weave(token_stages(samples - 1), backward_stages(0))

    @pl.when((step > samples) & (step < samples + LAG))
    def _():
        weave(backward_stages(step - samples))

    @pl.when((step >= samples + LAG) & (step < 2 * samples))
    def _():
        collect(edges(step - samples - LAG))
        weave(weight_stages(step - samples - LAG), backward_stages(step - samples))

    @pl.when((step >= samples) & (step < 2 * samples))
    def _():
        launch(edges(step - samples))

    @pl.when(step >= 2 * samples)
    def _():
        weave(finish_stages(step - 2 * samples))

    @pl.when(step == min(2 * samples + 3, last))
    def _():
        lines = pair_gradient(pair_ref, score_scr, per, pair_chunk, blocks)
        for n, line in enumerate(lines):
            small_src[0, n : n + 1, :] = line
        small_src[0, HEADS:, :] = jnp.zeros((8 - HEADS, width), F32)

    def fill_early():
        for n in range(gtok_scr.shape[1] // width):
            early_buf[n * width : (n + 1) * width, :] = gtok_scr[:, n * width : (n + 1) * width]
        at = gtok_scr.shape[1]
        early_buf[at : at + width, :] = gout_scr[...]
        early_buf[at + width :, :] = jnp.zeros((early_buf.shape[0] - at - width, width), F32)

    for n, action in enumerate(early.actions()):

        def run(n=n, action=action):
            if n == 0:
                fill_early()
            action()

        pl.when(step == min(samples + EARLY_AT[n], last))(run)

    def small_copies(k):
        axis, count = axes[k]
        base = 0 if k == 0 else axes[0][1] - 1
        return [
            pltpu.make_async_remote_copy(
                src_ref=small_src.at[k],
                dst_ref=(small_a, small_b)[k].at[d - 1],
                send_sem=small_send.at[base + d - 1],
                recv_sem=small_recv.at[base + d - 1],
                device_id={axis: shifted_index(axis, count, d)},
                device_id_type=MESH,
            )
            for d in range(1, count)
        ]

    def small_total(k):
        value = small_src[k]
        for n, copy in enumerate(small_copies(k)):
            copy.wait()
            value = value + (small_a, small_b)[k][n]
        return value

    def late_start():
        for s in range(samples - LAG, samples):
            collect(edges(s))
            weave(weight_stages(s))
        for n in range(4):
            late_buf[n * width : (n + 1) * width, :] = gw_scr[:, n * width : (n + 1) * width]
        if late_buf.shape[0] > 4 * width:
            late_buf[4 * width :, :] = jnp.zeros((late_buf.shape[0] - 4 * width, width), F32)
        late.scatter(0)

    def late_second():
        for copy in small_copies(0):
            copy.start()
        late.scatter(1)

    def late_third():
        late.gather(1)
        small_src[1] = small_total(0)
        for copy in small_copies(1):
            copy.start()

    def late_fourth():
        late.gather(0)
        small_ref[...] = small_total(1)

    def late_end():
        late.finish()
        early_ref[...] = early_sum[...]
        late_ref[...] = late_sum[...]

    late_actions = [late_start, late_second, late_third, late_fourth, late_end]
    for n, action in enumerate(late_actions):
        pl.when(step == min(2 * samples + LATE_AT[n], last))(action)


def unpack_kernel(channels, inputs, outputs, *refs):
    ins, refs = refs[:inputs], refs[inputs:]
    big_ins, refs = refs[:2], refs[2:]
    outs, refs = refs[:outputs], refs[outputs:]
    big_outs, refs = refs[:2], refs[2:]
    held_ins, refs = refs[:inputs], refs[inputs:]
    held_outs, refs = refs[:outputs], refs[outputs:]
    big_held, (in_sems, out_sems, sems) = refs[:2], refs[2:]
    loads = [
        pltpu.make_async_copy(src, dst, in_sems.at[n])
        for n, (src, dst) in enumerate(zip(ins, held_ins))
    ]
    stores = [
        pltpu.make_async_copy(src, dst, out_sems.at[n])
        for n, (src, dst) in enumerate(zip(held_outs, outs))
    ]
    moves = []
    count = sems.shape[0] // 4
    for n, (src, mid, dst) in enumerate(zip(big_ins, big_held, big_outs)):
        size = src.shape[0] // count
        for c in range(count):
            span = pl.ds(c * size, size)
            at = 2 * (n * count + c)
            moves.append(
                (
                    pltpu.make_async_copy(src.at[span], mid.at[span], sems.at[at]),
                    pltpu.make_async_copy(mid.at[span], dst.at[span], sems.at[at + 1]),
                )
            )
    for load in loads:
        load.start()
    for fetch, _ in moves:
        fetch.start()
    for load in loads:
        load.wait()
    early_ref, late_ref, small_ref, gain_ref = held_ins[:4]
    weights = held_ins[4:]
    ggain_out, gq_out, gk_out, gv_out, gg_out, gout_out, gtok_out, gpair_out = held_outs
    width = gout_out.shape[0]
    blocks = gtok_out.shape[1] // width

    def block(ref, n):
        return ref[n * width : (n + 1) * width, :].astype(F32)

    for n in range(blocks):
        gtok_out[:, n * width : (n + 1) * width] = block(early_ref, n)
    gout_out[...] = block(early_ref, blocks)
    by_gain = None
    for n, (ref, weight) in enumerate(zip((gq_out, gk_out, gv_out, gg_out), weights)):
        grad = block(late_ref, n)
        ref[...] = grad
        part = grad * weight[...].astype(F32)
        by_gain = part if by_gain is None else by_gain + part
    ggain_out[...] = jnp.sum(by_gain.T, axis=0, keepdims=True) / gain_ref[...]
    lines = small_ref[...]
    shift = width // 2
    while shift >= channels:
        lines = lines + pltpu.roll(lines, shift, 1)
        shift //= 2
    gpair_out[...] = lines[:HEADS, :channels]
    for store in stores:
        store.start()
    for fetch, put in moves:
        fetch.wait()
        put.start()
    for store in stores:
        store.wait()
    for _, put in moves:
        put.wait()


def whole(*shape):
    return pl.BlockSpec(shape, lambda s: (0,) * len(shape))


def sum_scratch(total, streams, orders, width):
    unit = total // streams
    slots = []
    for stream in range(streams):
        length = unit
        for _, size in orders[stream]:
            length //= size
            slots.append(pltpu.VMEM((size - 1, length, width), BF16))
    return slots * 2


def on_device(
    atoms,
    gain,
    w_query,
    w_key,
    w_value,
    w_gate,
    w_out,
    w_token,
    w_pair,
    pair_cond,
    counts,
    membership,
    pooled_cot,
):
    samples, rows, width = atoms.shape
    blocks = rows // QBLK
    rim = (KWIN - QBLK) // 2
    tokens, token_width = pooled_cot.shape[1:]
    channels = w_pair.shape[0]
    pair2 = pair_cond.reshape(blocks * QBLK, pair_cond.shape[-1])
    gain2 = gain.reshape(1, width)
    ids2 = membership.reshape(1, rows)
    square = whole(width, width)
    shape = jax.ShapeDtypeStruct
    vmem = pltpu.VMEM
    dma = pltpu.SemaphoreType.DMA

    axes = axis_sizes()
    devices = axes[0][1] * axes[1][1]
    peers = sum(size - 1 for _, size in axes)
    unit = 16 * devices
    early_total = -(-(token_width + width) // unit) * unit
    late_total = -(-(4 * width) // unit) * unit
    early_streams = early_total // unit
    late_streams = late_total // unit
    early_orders = [axes] * early_streams

    def clip(x):
        return jnp.clip(x, 0, samples - 1)

    def again(i):
        return jnp.where(i <= samples, clip(i - 1), clip(i - 2 * samples))

    pooled, gatoms, early, late, small = pl.pallas_call(
        functools.partial(step_kernel, samples, early_streams, late_streams),
        grid=(3 * samples,),
        in_specs=[
            pl.BlockSpec(memory_space=pltpu.SMEM),
            pl.BlockSpec(memory_space=pl.ANY),
            pl.BlockSpec((1, rows, width), lambda i: (clip(i), 0, 0)),
            pl.BlockSpec((1, rows, width), lambda i: (again(i), 0, 0)),
            whole(1, width),
            square,
            square,
            square,
            square,
            square,
            whole(width, token_width),
            whole(*w_pair.T.shape),
            pl.BlockSpec(memory_space=pl.ANY),
            whole(1, rows),
            pl.BlockSpec((1, tokens, token_width), lambda i: (clip(i - 1), 0, 0)),
        ],
        out_specs=[
            pl.BlockSpec((1, tokens, token_width), lambda i: (clip(i - 1), 0, 0)),
            pl.BlockSpec((1, rows, width), lambda i: (clip(i - 2 * samples), 0, 0)),
            whole(early_total, width),
            whole(late_total, width),
            whole(8, width),
        ],
        out_shape=[
            shape((samples, tokens, token_width), BF16),
            shape((samples, rows, width), BF16),
            shape((early_total, width), BF16),
            shape((late_total, width), BF16),
            shape((8, width), F32),
        ],
        scratch_shapes=[
            vmem((samples, rim, width), BF16),
            vmem((samples, rim, width), BF16),
            vmem((2, samples, rim, 2 * width), BF16),
            vmem((2, samples, rim, 2 * width), BF16),
            vmem(pair2.shape, BF16),
            vmem((blocks, KWIN, LANES), F32),
            vmem((blocks, KWIN, LANES), F32),
            vmem((rows, tokens), BF16),
            vmem((tokens, rows), BF16),
            vmem((tokens, 1), F32),
            vmem((width, 2 * width), BF16),
            vmem((width, 2 * width), BF16),
            vmem((width, 4 * width), BF16),
            vmem((width, token_width), BF16),
            vmem((samples, rows + 2 * rim, width), BF16),
            vmem((rows, width), F32),
            vmem((2, rows, width), BF16),
            vmem((2, 2, rows, width), F32),
            vmem((samples, rows, width), BF16),
            vmem((samples, rows + 2 * rim, 2 * width), BF16),
            vmem((samples, blocks, KWIN, LANES), BF16),
            vmem((samples, rows, width), BF16),
            vmem((samples, rows, width), BF16),
            vmem((samples, rows, 4 * width), BF16),
            vmem((width, width), F32),
            vmem((width, token_width), F32),
            vmem((width, 4 * width), F32),
            vmem((early_total, width), F32),
            vmem((late_total, width), F32),
            vmem((early_total, width), BF16),
            vmem((late_total, width), BF16),
            vmem((axes[0][1] - 1, 8, width), F32),
            vmem((axes[1][1] - 1, 8, width), F32),
            vmem((2, 8, width), F32),
            dma((2, 3)),
            dma((2, 3)),
            dma((2, samples)),
            dma((2, samples)),
            dma((2 * early_streams * peers,)),
            dma((2 * early_streams * peers,)),
            dma((2 * late_streams * peers,)),
            dma((2 * late_streams * peers,)),
            dma((peers,)),
            dma((peers,)),
            dma((1,)),
        ]
        + sum_scratch(early_total, early_streams, early_orders, width)
        + sum_scratch(late_total, late_streams, [axes] * late_streams, width),
        compiler_params=pltpu.CompilerParams(
            dimension_semantics=("arbitrary",),
            vmem_limit_bytes=56 * 1024 * 1024,
            collective_id=0,
            has_side_effects=True,
        ),
    )(
        counts,
        atoms,
        atoms,
        atoms,
        gain2,
        w_query,
        w_key,
        w_value,
        w_gate,
        w_out,
        w_token,
        w_pair.T,
        pair2,
        ids2,
        pooled_cot,
    )
    anywhere = pl.BlockSpec(memory_space=pl.ANY)
    pieces = next(n for n in (4, 3, 2, 1) if samples % n == 0)
    operands = (early, late, small, gain2, w_query, w_key, w_value, w_gate)
    results = (
        [shape((1, width), F32)]
        + [shape((width, width), F32)] * 5
        + [shape((width, token_width), F32), shape((HEADS, channels), F32)]
    )
    large = [shape(pooled.shape, BF16), shape(gatoms.shape, BF16)]
    ggain, gq, gk, gv, gg, gout, gtok, gpair, pooled, gatoms = pl.pallas_call(
        functools.partial(unpack_kernel, channels, len(operands), len(results)),
        in_specs=[anywhere] * (len(operands) + 2),
        out_specs=[anywhere] * (len(results) + 2),
        out_shape=results + large,
        scratch_shapes=[vmem(x.shape, x.dtype) for x in (*operands, *results, *large)]
        + [dma((len(operands),)), dma((len(results),)), dma((4 * pieces,))],
    )(*operands, pooled, gatoms)
    return (pooled, gatoms, ggain.reshape(width), gq, gk, gv, gg, gout, gtok, gpair.T)


def solution(mesh):
    placed = (
        P("samp", "seq", None),
        P(),
        P(),
        P(),
        P(),
        P(),
        P(),
        P(),
        P(),
        P("seq", None, None),
        P(),
        P("seq"),
        P("samp", "seq", None),
    )
    return jax.shard_map(
        on_device,
        mesh=mesh,
        in_specs=placed,
        out_specs=(
            P("samp", "seq", None),
            P("samp", "seq", None),
            P(),
            P(),
            P(),
            P(),
            P(),
            P(),
            P(),
            P(),
        ),
        check_vma=False,
    )
```
